512 devices in a mesh: region: 64 (over x, z), rays: 8 (over y, core).
Axes of the slice: x: 4, y: 4, z: 16, core: 2. Of those that a mesh axis runs over, the one named last changes fastest.
Arguments:
- ray_codes: bfloat16 [2, 4096, 128], P(None, 'rays'), may hold values from -6 to 6
- target: bfloat16 [4096, 384], P('rays'), may hold values from -0.19921875 to 1
- direction: int32 [4096], P('rays'), may hold values from 0 to 1
- entries: int32 [64, 4096], P('region', 'rays'), may hold values from 0 to 4
- exits: int32 [64, 4096], P('region', 'rays'), may hold values from 4 to 8
- depth_bins: int32 [64, 8, 4096], P('region', None, 'rays'), may hold values from 0 to 63, as said below
- in_layer: float32 [3, 64, 128, 256], P(None, 'region', 'rays'), as said below
- mid_layer: float32 [3, 64, 256, 256], P(None, 'region', 'rays'), as said below
- feat_layer: float32 [3, 64, 256, 384], P(None, 'region', 'rays'), as said below
- vectors: float32 [3, 64, 1152], P(None, 'region', 'rays'), as said below
Outputs:
- new_in_layer: float32 [3, 64, 128, 256], P(None, 'region', 'rays')
- new_mid_layer: float32 [3, 64, 256, 256], P(None, 'region', 'rays')
- new_feat_layer: float32 [3, 64, 256, 384], P(None, 'region', 'rays')
- new_vectors: float32 [3, 64, 1152], P(None, 'region', 'rays')
- depth_grad: float32 [64, 4096], P('region', 'rays')
The draws below stay inside these ranges and needn't reach their ends.
Inputs may be any that keep to these rules, and one draw needn't show every extreme that they name: `direction`: 0: the ray meets the regions in increasing index order; 1: in decreasing order. A ray's samples inside a region are the slots j with entries <= j < exits. `depth_bins`: slot j lies in bins j * (8) to (j + 1) * 8 - 1. `in_layer`: the second moments (index 2 of the first dimension) are positive. `mid_layer`: the second moments (index 2 of the first dimension) are positive. `feat_layer`: the second moments (index 2 of the first dimension) are positive. `vectors`: the second moments (index 2 of the first dimension) are positive.
All inputs are finite; a program needn't handle non-finite values.
Results may differ from the reference program's by a relative error of at most 0.0025.
The reference program's roundings to bfloat16 on the way (of `encoded`, `hidden_one`, `hidden_two`, `feature_grad`, `density_grad`, `colour_grad`, `second_grad` and `first_grad`) count: a program that leaves them out, or rounds other values in their place, can miss the bound.
Values may be sent and summed in bfloat16 or wider, within the bound.
A program may use at most 64 MiB of HBM per device.

```python
import math
import jax
import jax.numpy as jnp
from jax import lax

IN = 128
HID = 256
FEAT = 384
SAMPLES = 8
BINS = 64
RAYS = 4096
REGIONS = 64
VEC = 1152


def moments(key, full_shape, spread, state_scale):
    master_key = jax.random.fold_in(key, 101)
    first_key = jax.random.fold_in(key, 202)
    second_key = jax.random.fold_in(key, 303)
    master = jax.random.normal(master_key, full_shape, jnp.float32) * spread
    first_moment = jax.random.normal(first_key, full_shape, jnp.float32) * (0.3 * state_scale)
    second = jnp.exp(jax.random.uniform(second_key, full_shape, jnp.float32, math.log(0.3), 0.0)) * (state_scale * state_scale)
    return jnp.stack([master, first_moment, second])


def draw_in_layer(key, part):
    return moments(key, (REGIONS, IN, HID), IN ** (-0.5), 0.2)


def draw_mid_layer(key, part):
    return moments(key, (REGIONS, HID, HID), HID ** (-0.5), 0.15)


def draw_feat_layer(key, part):
    return moments(key, (REGIONS, HID, FEAT), 4.0 * HID ** (-0.5), 0.15)


def draw_vectors(key, part):
    spread = jnp.concatenate([jnp.full((2 * HID,), 0.5, jnp.float32), jnp.full((HID,), HID ** (-0.5), jnp.float32), jnp.full((FEAT,), 1.0, jnp.float32)])
    state_scale = jnp.concatenate([jnp.full((HID,), 0.15, jnp.float32), jnp.full((HID,), 0.2, jnp.float32), jnp.full((HID,), 1.0, jnp.float32), jnp.full((FEAT,), 0.15, jnp.float32)])
    return moments(key, (REGIONS, VEC), spread[None, :], state_scale[None, :])


def draw_depth_bins(key, part):
    stride = BINS // SAMPLES
    jitter = jax.random.randint(key, (REGIONS, SAMPLES, RAYS), 0, stride, jnp.int32)
    base = lax.broadcasted_iota(jnp.int32, (REGIONS, SAMPLES, RAYS), 1) * stride
    return (base + jitter).astype(jnp.int32)


def set_ends(values, key, smallest, high):
    extent = values.shape
    spot = [jax.random.randint(jax.random.fold_in(key, axis), (), 0, extent[axis]) for axis in range(len(extent))]
    values = values.at[tuple(spot)].set(smallest)
    longest = extent.index(max(extent))
    spot[longest] = (spot[longest] + 1) % extent[longest]
    return values.at[tuple(spot)].set(high)


def block_scale(key, dims, cuts, smallest, high):
    factor_of, own = 1.0, jax.random.fold_in(key, 6)
    for dim, parts in cuts:
        steps = jnp.exp(jax.random.uniform(jax.random.fold_in(own, dim), (parts,), jnp.float32, smallest / len(cuts), high / len(cuts)))
        factor_of = factor_of * jnp.repeat(steps, dims[dim] // parts).reshape([-1 if axis == dim else 1 for axis in range(len(dims))])
    return factor_of


def gaussian(stream_key, dims, width, limit, cuts=(), held_as=jnp.bfloat16):
    values = width * jax.random.normal(stream_key, dims, jnp.float32)
    if cuts:
        values = values * block_scale(stream_key, dims, cuts, -0.22, 0.18)
    return jnp.clip(values, -limit, limit).astype(held_as)


def setup_inputs(seed: int = 0) -> dict:
    keys = jax.random.split(jax.random.key(seed), 11)
    return {
        "ray_codes": gaussian(keys[0], (2, RAYS, IN), 1.0, 6.0, ((1, 8),)),
        "target": jnp.clip(-0.19921875 + 1.1992188 * jax.random.uniform(keys[1], (RAYS, FEAT), jnp.float32) ** block_scale(keys[1], (RAYS, FEAT), ((0, 8),), -0.2, 0.2), -0.19921875, 1.0).astype(jnp.bfloat16),
        "direction": set_ends(jax.random.randint(keys[2], (RAYS,), 0, 2), jax.random.fold_in(keys[2], 1), 0, 1).astype(jnp.int32),
        "entries": set_ends(jax.random.randint(keys[3], (REGIONS, RAYS), 0, SAMPLES // 2 + 1), jax.random.fold_in(keys[3], 1), 0, (SAMPLES // 2 + 1) - 1).astype(jnp.int32),
        "exits": set_ends(jax.random.randint(keys[4], (REGIONS, RAYS), SAMPLES // 2, SAMPLES + 1), jax.random.fold_in(keys[4], 1), SAMPLES // 2, SAMPLES).astype(jnp.int32),
        "depth_bins": draw_depth_bins(jax.random.fold_in(keys[10], 71), 0),
        "in_layer": draw_in_layer(jax.random.fold_in(keys[10], 71), 0),
        "mid_layer": draw_mid_layer(jax.random.fold_in(keys[10], 71), 0),
        "feat_layer": draw_feat_layer(jax.random.fold_in(keys[10], 71), 0),
        "vectors": draw_vectors(jax.random.fold_in(keys[10], 71), 0),
    }


depth_scale = 4.0
beta_one = 0.9
beta_two = 0.999
learn_rate = 0.001
epsilon = 1e-08
first_fix = 1.0 - 0.9 ** 10
second_fix = 1.0 - 0.999 ** 10

def forward(ray_codes, depth_bins, entry_row, exit_row, weights, unit_length):
    in_weight, mid_weight, feat_weight, vec_weight = weights
    hidden_width = in_weight.shape[1]
    bias_one = vec_weight[:hidden_width].astype(jnp.float32)
    bias_two = vec_weight[hidden_width:2 * hidden_width].astype(jnp.float32)
    density_weight = vec_weight[2 * hidden_width:3 * hidden_width]
    bias_feat = vec_weight[3 * hidden_width:].astype(jnp.float32)
    samples, ray_count = depth_bins.shape
    bin_float = depth_bins.astype(jnp.float32)
    following = jnp.concatenate([bin_float[1:], jnp.full((1, ray_count), float(BINS), jnp.float32)], 0)
    spacing = (following - bin_float) * unit_length
    position = (bin_float + 0.5) / BINS
    sample_slot = lax.broadcasted_iota(jnp.int32, (samples, ray_count), 0)
    inside = ((sample_slot >= entry_row[None, :]) & (sample_slot < exit_row[None, :])).astype(jnp.float32)
    codes_float = ray_codes.astype(jnp.float32)
    encoded = (codes_float[0][None] + position[:, :, None] * codes_float[1][None]).astype(jnp.bfloat16)
    encoded = encoded.reshape(samples * ray_count, codes_float.shape[2])
    hidden_one = jnp.maximum(jnp.dot(encoded, in_weight, preferred_element_type=jnp.float32) + bias_one, 0.0).astype(jnp.bfloat16)
    hidden_two = jnp.maximum(jnp.dot(hidden_one, mid_weight, preferred_element_type=jnp.float32) + bias_two, 0.0).astype(jnp.bfloat16)
    density_raw = jnp.dot(hidden_two, density_weight, preferred_element_type=jnp.float32).reshape(samples, ray_count)
    colour = jax.nn.sigmoid(jnp.dot(hidden_two, feat_weight, preferred_element_type=jnp.float32) + bias_feat)
    colour = colour.reshape(samples, ray_count, feat_weight.shape[1])
    optical = jax.nn.softplus(density_raw) * spacing * inside
    optical_before = jnp.cumsum(optical, 0) - optical
    local_weight = jnp.exp(-optical_before) * -jnp.expm1(-optical)
    return (encoded, hidden_one, hidden_two, density_raw, colour, optical, optical_before, local_weight, spacing, inside)

def backward(found, weights, entry_trans, after_sum, feature_grad):
    encoded, hidden_one, hidden_two, density_raw, colour, optical, optical_before, local_weight, spacing, inside = found
    in_weight, mid_weight, feat_weight, vec_weight = weights
    hidden_width = in_weight.shape[1]
    density_weight = vec_weight[2 * hidden_width:3 * hidden_width]
    grad_float = feature_grad.astype(jnp.float32)
    sample_grad = lax.optimization_barrier(jnp.sum(colour * grad_float[None], -1))
    weighted = local_weight * sample_grad
    later_local = jnp.cumsum(weighted[::-1], 0)[::-1] - weighted
    optical_grad = entry_trans[None] * (jnp.exp(-(optical_before + optical)) * sample_grad - later_local) - after_sum[None]
    density_grad = (optical_grad * spacing * inside * jax.nn.sigmoid(density_raw)).astype(jnp.bfloat16).reshape(-1)
    colour_grad = ((entry_trans[None] * local_weight)[:, :, None] * grad_float[None] * colour * (1.0 - colour)).astype(jnp.bfloat16)
    colour_grad = colour_grad.reshape(-1, colour.shape[2])
    hidden_grad = jnp.dot(colour_grad, feat_weight.T, preferred_element_type=jnp.float32)
    hidden_grad = hidden_grad + density_grad.astype(jnp.float32)[:, None] * density_weight.astype(jnp.float32)[None, :]
    second_grad = (hidden_grad * (hidden_two > 0)).astype(jnp.bfloat16)
    first_grad = (jnp.dot(second_grad, mid_weight.T, preferred_element_type=jnp.float32) * (hidden_one > 0)).astype(jnp.bfloat16)
    in_grad = jnp.dot(encoded.T, first_grad, preferred_element_type=jnp.float32)
    mid_grad = jnp.dot(hidden_one.T, second_grad, preferred_element_type=jnp.float32)
    feat_grad = jnp.dot(hidden_two.T, colour_grad, preferred_element_type=jnp.float32)
    density_sum = jnp.dot(density_grad, hidden_two, preferred_element_type=jnp.float32)
    vec_grad = jnp.concatenate([lax.optimization_barrier(jnp.sum(first_grad, 0, dtype=jnp.float32)), lax.optimization_barrier(jnp.sum(second_grad, 0, dtype=jnp.float32)), density_sum, lax.optimization_barrier(jnp.sum(colour_grad, 0, dtype=jnp.float32))])
    return (in_grad, mid_grad, feat_grad, vec_grad)

def adam_update(stacked, gradient):
    first_moment = beta_one * stacked[1] + (1.0 - beta_one) * gradient
    second = beta_two * stacked[2] + (1.0 - beta_two) * gradient * gradient
    update_step = first_moment / first_fix / (jnp.sqrt(second / second_fix) + epsilon)
    return jnp.stack([stacked[0] - learn_rate * update_step, first_moment, second])

def exclusive_lower(values):
    running = jnp.cumsum(values, 0)
    return jnp.concatenate([jnp.zeros_like(values[:1]), running[:-1]], 0)

def exclusive_upper(values):
    running = jnp.cumsum(values[::-1], 0)[::-1]
    return jnp.concatenate([running[1:], jnp.zeros_like(values[:1])], 0)

def reference(ray_codes, target, direction, entries, exits, depth_bins, in_layer, mid_layer, feat_layer, vectors):
    unit_length = depth_scale / (REGIONS * BINS)
    weight_sets = (in_layer[0].astype(jnp.bfloat16), mid_layer[0].astype(jnp.bfloat16), feat_layer[0].astype(jnp.bfloat16), vectors[0].astype(jnp.bfloat16))

    def first_pass(region_inputs):
        found = forward(ray_codes, region_inputs[0], region_inputs[1], region_inputs[2], region_inputs[3:], unit_length)
        colour, optical, local_weight = (found[4], found[5], found[7])
        return (lax.optimization_barrier(jnp.sum(optical, 0)), lax.optimization_barrier(jnp.sum(local_weight[:, :, None] * colour, 0)))
    depth, local_partial = lax.map(first_pass, (depth_bins, entries, exits) + weight_sets)
    onward = (direction == 0)[None, :]
    entry_trans = jnp.exp(-jnp.where(onward, exclusive_lower(depth), exclusive_upper(depth)))
    rendered = lax.optimization_barrier(jnp.sum(entry_trans[:, :, None] * local_partial, 0))
    feature_grad = (rendered - target.astype(jnp.float32)).astype(jnp.bfloat16)
    region_grad = entry_trans * lax.optimization_barrier(jnp.sum(feature_grad.astype(jnp.float32)[None] * local_partial, -1))
    after_sum = jnp.where(onward, exclusive_upper(region_grad), exclusive_lower(region_grad))

    def second_pass(region_inputs):
        weights = region_inputs[3:7]
        found = forward(ray_codes, region_inputs[0], region_inputs[1], region_inputs[2], weights, unit_length)
        return backward(found, weights, region_inputs[7], region_inputs[8], feature_grad)
    in_grad, mid_grad, feat_grad, vec_grad = lax.map(second_pass, (depth_bins, entries, exits) + weight_sets + (entry_trans, after_sum))
    return (adam_update(in_layer, in_grad), adam_update(mid_layer, mid_grad), adam_update(feat_layer, feat_grad), adam_update(vectors, vec_grad), -after_sum)
```

```python
import jax
import jax.numpy as jnp
from jax import lax
from jax.experimental import pallas as pl
from jax.experimental.pallas import tpu as pltpu
from jax.sharding import PartitionSpec as P

BINS = 64


depth_scale = 4.0
beta_one = 0.9
beta_two = 0.999
learn_rate = 0.001
epsilon = 1e-08
first_fix = 1.0 - 0.9**10
second_fix = 1.0 - 0.999**10


def forward(ray_codes, depth_bins, entry_row, exit_row, weights, unit_length):
    in_weight, mid_weight, feat_weight, vec_weight = weights
    hidden_width = in_weight.shape[1]
    bias_one = vec_weight[:hidden_width].astype(jnp.float32)
    bias_two = vec_weight[hidden_width : 2 * hidden_width].astype(jnp.float32)
    density_weight = vec_weight[2 * hidden_width : 3 * hidden_width]
    bias_feat = vec_weight[3 * hidden_width :].astype(jnp.float32)
    samples, ray_count = depth_bins.shape
    bin_float = depth_bins.astype(jnp.float32)
    following = jnp.concatenate(
        [bin_float[1:], jnp.full((1, ray_count), float(BINS), jnp.float32)], 0
    )
    spacing = (following - bin_float) * unit_length
    position = (bin_float + 0.5) / BINS
    sample_slot = lax.broadcasted_iota(jnp.int32, (samples, ray_count), 0)
    inside = ((sample_slot >= entry_row[None, :]) & (sample_slot < exit_row[None, :])).astype(
        jnp.float32
    )
    codes_float = ray_codes.astype(jnp.float32)
    encoded = (codes_float[0][None] + position[:, :, None] * codes_float[1][None]).astype(
        jnp.bfloat16
    )
    encoded = encoded.reshape(samples * ray_count, codes_float.shape[2])
    hidden_one = jnp.maximum(
        jnp.dot(encoded, in_weight, preferred_element_type=jnp.float32) + bias_one, 0.0
    ).astype(jnp.bfloat16)
    hidden_two = jnp.maximum(
        jnp.dot(hidden_one, mid_weight, preferred_element_type=jnp.float32) + bias_two, 0.0
    ).astype(jnp.bfloat16)
    density_raw = jnp.dot(hidden_two, density_weight, preferred_element_type=jnp.float32).reshape(
        samples, ray_count
    )
    colour = jax.nn.sigmoid(
        jnp.dot(hidden_two, feat_weight, preferred_element_type=jnp.float32) + bias_feat
    )
    colour = colour.reshape(samples, ray_count, feat_weight.shape[1])
    optical = jax.nn.softplus(density_raw) * spacing * inside
    optical_before = jnp.cumsum(optical, 0) - optical
    local_weight = jnp.exp(-optical_before) * -jnp.expm1(-optical)
    return (
        encoded,
        hidden_one,
        hidden_two,
        density_raw,
        colour,
        optical,
        optical_before,
        local_weight,
        spacing,
        inside,
    )


def backward(found, weights, entry_trans, after_sum, feature_grad):
    (
        encoded,
        hidden_one,
        hidden_two,
        density_raw,
        colour,
        optical,
        optical_before,
        local_weight,
        spacing,
        inside,
    ) = found
    in_weight, mid_weight, feat_weight, vec_weight = weights
    hidden_width = in_weight.shape[1]
    density_weight = vec_weight[2 * hidden_width : 3 * hidden_width]
    grad_float = feature_grad.astype(jnp.float32)
    sample_grad = jnp.sum(colour * grad_float[None], -1)
    weighted = local_weight * sample_grad
    later_local = jnp.cumsum(weighted[::-1], 0)[::-1] - weighted
    optical_grad = (
        entry_trans[None] * (jnp.exp(-(optical_before + optical)) * sample_grad - later_local)
        - after_sum[None]
    )
    density_grad = (
        (optical_grad * spacing * inside * jax.nn.sigmoid(density_raw))
        .astype(jnp.bfloat16)
        .reshape(-1)
    )
    colour_grad = (
        (entry_trans[None] * local_weight)[:, :, None] * grad_float[None] * colour * (1.0 - colour)
    ).astype(jnp.bfloat16)
    colour_grad = colour_grad.reshape(-1, colour.shape[2])
    hidden_grad = jnp.dot(colour_grad, feat_weight.T, preferred_element_type=jnp.float32)
    hidden_grad = (
        hidden_grad
        + density_grad.astype(jnp.float32)[:, None] * density_weight.astype(jnp.float32)[None, :]
    )
    second_grad = (hidden_grad * (hidden_two > 0)).astype(jnp.bfloat16)
    first_grad = (
        jnp.dot(second_grad, mid_weight.T, preferred_element_type=jnp.float32) * (hidden_one > 0)
    ).astype(jnp.bfloat16)
    in_grad = jnp.dot(encoded.T, first_grad, preferred_element_type=jnp.float32)
    mid_grad = jnp.dot(hidden_one.T, second_grad, preferred_element_type=jnp.float32)
    feat_grad = jnp.dot(hidden_two.T, colour_grad, preferred_element_type=jnp.float32)
    density_sum = jnp.dot(density_grad, hidden_two, preferred_element_type=jnp.float32)
    vec_grad = jnp.concatenate(
        [
            jnp.sum(first_grad, 0, dtype=jnp.float32),
            jnp.sum(second_grad, 0, dtype=jnp.float32),
            density_sum,
            jnp.sum(colour_grad, 0, dtype=jnp.float32),
        ]
    )
    return (in_grad, mid_grad, feat_grad, vec_grad)


def adam_update(stacked, gradient):
    first_moment = beta_one * stacked[1] + (1.0 - beta_one) * gradient
    second = beta_two * stacked[2] + (1.0 - beta_two) * gradient * gradient
    update_step = first_moment / first_fix / (jnp.sqrt(second / second_fix) + epsilon)
    return jnp.stack([stacked[0] - learn_rate * update_step, first_moment, second])


MESH = pl.DeviceIdType.MESH
NX = 4
NZ = 16
NR = 8
RX = 128
RZ = 8
FEAT = 384


def vmem(count):
    return [pl.BlockSpec(memory_space=pltpu.VMEM)] * count


def remote(source, target, send_sem, recv_sem, peer):
    return pltpu.make_async_remote_copy(
        src_ref=source,
        dst_ref=target,
        send_sem=send_sem,
        recv_sem=recv_sem,
        device_id=peer,
        device_id_type=MESH,
    )


def gather_kernel(
    in_ref, mid_ref, feat_ref, vec_ref, in_out, mid_out, feat_out, vec_out, send_sem, recv_sem
):
    me = lax.axis_index("rays")
    in_out[me] = in_ref[...].astype(jnp.bfloat16)
    mid_out[me] = mid_ref[...].astype(jnp.bfloat16)
    feat_out[me] = feat_ref[...].astype(jnp.bfloat16)
    vec_out[me] = vec_ref[...].astype(jnp.bfloat16).astype(jnp.float32)
    barrier = pltpu.get_barrier_semaphore()
    for step in range(1, NR):
        pl.semaphore_signal(
            barrier, inc=1, device_id={"rays": lax.rem(me + step, NR)}, device_id_type=MESH
        )
    pl.semaphore_wait(barrier, NR - 1)
    outs = (in_out, mid_out, feat_out, vec_out)
    for kind, out in enumerate(outs):
        for step in range(1, NR):
            peer = lax.rem(me + step, NR)
            remote(
                out.at[me],
                out.at[me],
                send_sem.at[kind, step],
                recv_sem.at[kind, step],
                {"rays": peer},
            ).start()
    for kind, out in enumerate(outs):
        for step in range(1, NR):
            origin = lax.rem(me + NR - step, NR)
            remote(
                out.at[origin],
                out.at[origin],
                send_sem.at[kind, step],
                recv_sem.at[kind, step],
                {"rays": origin},
            ).wait()


def gather_weights(in_part, mid_part, feat_part, vec_part):
    shapes = (
        jax.ShapeDtypeStruct((NR, 16, 256), jnp.bfloat16),
        jax.ShapeDtypeStruct((NR, 32, 256), jnp.bfloat16),
        jax.ShapeDtypeStruct((NR, 32, 384), jnp.bfloat16),
        jax.ShapeDtypeStruct((NR, 1, 144), jnp.float32),
    )
    return pl.pallas_call(
        gather_kernel,
        out_shape=shapes,
        in_specs=vmem(4),
        out_specs=tuple(vmem(4)),
        scratch_shapes=[pltpu.SemaphoreType.DMA((4, NR)), pltpu.SemaphoreType.DMA((4, NR))],
        compiler_params=pltpu.CompilerParams(collective_id=0, has_side_effects=True),
        name="gather_weights",
    )(in_part, mid_part, feat_part, vec_part)


def far_first(count):
    half = count // 2
    order = [half]
    for gap in range(1, half):
        order += [half - gap, half + gap]
    return order


def ordered_sums(table, own_z):
    column = jnp.zeros((NX, 1, RX), jnp.float32)
    lower = jnp.zeros((NX, 1, RX), jnp.float32)
    upper = jnp.zeros((NX, 1, RX), jnp.float32)
    for z in range(NZ):
        rows = table[z]
        column = column + rows
        lower = lower + rows * (z < own_z).astype(jnp.float32)
        upper = upper + rows * (z > own_z).astype(jnp.float32)
    below, above = [], []
    for x in range(NX):
        under, over = lower[x], upper[x]
        for other in range(NX):
            if other < x:
                under = under + column[other]
            if other > x:
                over = over + column[other]
        below.append(under)
        above.append(over)
    return below, above


def region_kernel(
    partial_ref,
    depth_ref,
    onward_ref,
    target_ref,
    trans_out,
    after_out,
    grad_out,
    partial_x,
    depth_z,
    pieces,
    pieces_z,
    grad_z,
    region_z,
    trans_send,
    after_send,
    sem_partial,
    sem_depth,
    sem_depth_z,
    sem_piece,
    sem_grad_z,
    sem_region,
    sem_trans,
    sem_grad,
    sem_after,
):
    place = lax.axis_index("region")
    own_x, own_z = place // NZ, lax.rem(place, NZ)

    def along_x(step):
        return lax.rem(own_x + step, NX)

    def along_z(step):
        return lax.rem(own_z + step, NZ)

    def at(x, z):
        return {"region": x * NZ + z}

    barrier = pltpu.get_barrier_semaphore()
    for step in range(1, NZ):
        pl.semaphore_signal(
            barrier, inc=1, device_id=at(own_x, along_z(step)), device_id_type=MESH
        )
    for step in range(1, NX):
        pl.semaphore_signal(
            barrier, inc=1, device_id=at(along_x(step), own_z), device_id_type=MESH
        )
    pl.semaphore_wait(barrier, NX + NZ - 2)

    def spread_x(source, target, sems):
        for step in (2, 1, 3):
            x = along_x(step)
            remote(
                source(x), target.at[own_x], sems.at[0, step], sems.at[1, step], at(x, own_z)
            ).start()

    def wait_x(source, target, sems):
        for step in (1, 3, 2):
            x = along_x(NX - step)
            remote(source(x), target.at[x], sems.at[0, step], sems.at[1, step], at(x, own_z)).wait()

    def spread_z(source, target, sems):
        for step in far_first(NZ):
            z = along_z(step)
            remote(
                source(z), target.at[own_z], sems.at[0, step], sems.at[1, step], at(own_x, z)
            ).start()

    def wait_z(source, target, sems):
        for step in far_first(NZ)[::-1]:
            z = along_z(NZ - step)
            remote(source(z), target.at[z], sems.at[0, step], sems.at[1, step], at(own_x, z)).wait()

    depth_own = depth_z.at[own_z]
    depth_own[own_x] = depth_ref[own_x]
    spread_x(lambda x: depth_ref.at[x], depth_own, sem_depth)
    spread_x(lambda x: partial_ref.at[x], partial_x, sem_partial)
    partial_x[own_x] = partial_ref[own_x]
    wait_x(lambda x: depth_ref.at[x], depth_own, sem_depth)
    spread_z(lambda z: depth_own, depth_z, sem_depth_z)
    wait_z(lambda z: depth_own, depth_z, sem_depth_z)
    below, above = ordered_sums(depth_z, own_z)
    onward = onward_ref[own_x] == 0
    filler = jnp.zeros((RX - NX, RX), jnp.float32)
    trans = [jnp.exp(-jnp.where(onward, below[x], above[x])) for x in range(NX)]
    for x in range(NX):
        trans_send[x] = trans[x]
    trans_out[own_x] = trans_send[own_x]
    spread_x(lambda x: trans_send.at[x], trans_out, sem_trans)
    columns = jnp.transpose(jnp.concatenate(trans + [filler], 0))
    wait_x(lambda x: partial_ref.at[x], partial_x, sem_partial)
    total = jnp.zeros((RX, FEAT), jnp.float32)
    for x in range(NX):
        total = total + columns[:, x : x + 1] * partial_x[x].astype(jnp.float32)
    pieces[...] = total.reshape(NZ, RZ, FEAT).astype(jnp.bfloat16)
    spread_z(lambda z: pieces.at[z], pieces_z, sem_piece)
    pieces_z[own_z] = pieces[own_z]
    first = pl.multiple_of(own_x * RX + (own_z // 2) * (2 * RZ), 2 * RZ)
    wanted = target_ref[pl.ds(first, 2 * RZ), :].astype(jnp.float32)
    odd = (lax.rem(own_z, 2)).astype(jnp.float32)
    wanted = wanted[:RZ] * (1.0 - odd) + wanted[RZ:] * odd
    wait_z(lambda z: pieces.at[z], pieces_z, sem_piece)
    rendered = jnp.sum(pieces_z[...].astype(jnp.float32), 0)
    grad_z[own_z] = (rendered - wanted).astype(jnp.bfloat16)
    spread_z(lambda z: grad_z.at[own_z], grad_z, sem_grad_z)
    wait_z(lambda z: grad_z.at[own_z], grad_z, sem_grad_z)
    grad_float = grad_z[...].astype(jnp.float32).reshape(RX, FEAT)
    grad_out[own_x] = grad_float.astype(jnp.bfloat16)
    dots = [
        jnp.sum(grad_float * partial_x[x].astype(jnp.float32), -1, keepdims=True)
        for x in range(NX)
    ]
    lane = lax.broadcasted_iota(jnp.int32, (RX, RX), 1)
    grid = jnp.zeros((RX, RX), jnp.float32)
    for x in range(NX):
        grid = jnp.where(lane == x, dots[x], grid)
    grid = jnp.transpose(grid)
    region_own = region_z.at[own_z]
    for x in range(NX):
        region_own[x] = grid[x : x + 1] * trans_send[x]
    spread_z(lambda z: region_own, region_z, sem_region)
    spread_x(lambda x: grad_out.at[own_x], grad_out, sem_grad)
    wait_z(lambda z: region_own, region_z, sem_region)
    below, above = ordered_sums(region_z, own_z)
    for x in range(NX):
        after_send[x] = jnp.where(onward, above[x], below[x])
    after_out[own_x] = after_send[own_x]
    spread_x(lambda x: after_send.at[x], after_out, sem_after)
    wait_x(lambda x: trans_send.at[x], trans_out, sem_trans)
    wait_x(lambda x: grad_out.at[own_x], grad_out, sem_grad)
    wait_x(lambda x: after_send.at[x], after_out, sem_after)


def exchange_regions(partial, depth, direction, target):
    row = jax.ShapeDtypeStruct((NX, 1, RX), jnp.float32)
    return pl.pallas_call(
        region_kernel,
        out_shape=(row, row, jax.ShapeDtypeStruct((NX, RX, FEAT), jnp.bfloat16)),
        in_specs=vmem(4),
        out_specs=tuple(vmem(3)),
        scratch_shapes=[
            pltpu.VMEM((NX, RX, FEAT), jnp.bfloat16),
            pltpu.VMEM((NZ, NX, 1, RX), jnp.float32),
            pltpu.VMEM((NZ, RZ, FEAT), jnp.bfloat16),
            pltpu.VMEM((NZ, RZ, FEAT), jnp.bfloat16),
            pltpu.VMEM((NZ, RZ, FEAT), jnp.bfloat16),
            pltpu.VMEM((NZ, NX, 1, RX), jnp.float32),
            pltpu.VMEM((NX, 1, RX), jnp.float32),
            pltpu.VMEM((NX, 1, RX), jnp.float32),
            pltpu.SemaphoreType.DMA((2, NX)),
            pltpu.SemaphoreType.DMA((2, NX)),
            pltpu.SemaphoreType.DMA((2, NZ)),
            pltpu.SemaphoreType.DMA((2, NZ)),
            pltpu.SemaphoreType.DMA((2, NZ)),
            pltpu.SemaphoreType.DMA((2, NZ)),
            pltpu.SemaphoreType.DMA((2, NX)),
            pltpu.SemaphoreType.DMA((2, NX)),
            pltpu.SemaphoreType.DMA((2, NX)),
        ],
        compiler_params=pltpu.CompilerParams(collective_id=1, has_side_effects=True),
        name="exchange_regions",
    )(partial, depth, direction, target)


def reduce_kernel(
    in_ref,
    mid_ref,
    feat_ref,
    vec_ref,
    in_out,
    mid_out,
    feat_out,
    vec_out,
    in_send,
    mid_send,
    feat_send,
    in_got,
    mid_got,
    feat_got,
    vec_got,
    send_sem,
    recv_sem,
):
    me = lax.axis_index("rays")
    feat_send[...] = feat_ref[...].astype(jnp.bfloat16)
    mid_send[...] = mid_ref[...].astype(jnp.bfloat16)
    in_send[...] = in_ref[...].astype(jnp.bfloat16)
    barrier = pltpu.get_barrier_semaphore()
    for step in range(1, NR):
        pl.semaphore_signal(
            barrier, inc=1, device_id={"rays": lax.rem(me + step, NR)}, device_id_type=MESH
        )
    pl.semaphore_wait(barrier, NR - 1)
    moves = (
        (feat_send, feat_got, feat_ref, feat_out),
        (mid_send, mid_got, mid_ref, mid_out),
        (in_send, in_got, in_ref, in_out),
        (vec_ref, vec_got, vec_ref, vec_out),
    )
    for kind, (source, got, _, _) in enumerate(moves):
        for step in range(1, NR):
            peer = lax.rem(me + step, NR)
            remote(
                source.at[peer],
                got.at[step],
                send_sem.at[kind, step],
                recv_sem.at[kind, step],
                {"rays": peer},
            ).start()
    for kind, (source, got, own, out) in enumerate(moves):
        total = own[me]
        for step in range(1, NR):
            origin = lax.rem(me + NR - step, NR)
            remote(
                source.at[origin],
                got.at[step],
                send_sem.at[kind, step],
                recv_sem.at[kind, step],
                {"rays": origin},
            ).wait()
            total = total + got[step].astype(jnp.float32)
        out[...] = total


def reduce_grads(in_grad, mid_grad, feat_grad, vec_grad):
    shapes = ((16, 256), (32, 256), (32, 384), (1, 144))
    return pl.pallas_call(
        reduce_kernel,
        out_shape=tuple(jax.ShapeDtypeStruct(shape, jnp.float32) for shape in shapes),
        in_specs=vmem(4),
        out_specs=tuple(vmem(4)),
        scratch_shapes=[pltpu.VMEM((NR,) + shape, jnp.bfloat16) for shape in shapes[:3]]
        + [pltpu.VMEM((NR,) + shape, jnp.bfloat16) for shape in shapes[:3]]
        + [
            pltpu.VMEM((NR, 1, 144), jnp.float32),
            pltpu.SemaphoreType.DMA((4, NR)),
            pltpu.SemaphoreType.DMA((4, NR)),
        ],
        compiler_params=pltpu.CompilerParams(collective_id=2, has_side_effects=True),
        name="reduce_grads",
    )(in_grad, mid_grad, feat_grad, vec_grad)


def per_device(
    ray_codes,
    target,
    direction,
    entries,
    exits,
    depth_bins,
    in_layer,
    mid_layer,
    feat_layer,
    vectors,
):
    in_all, mid_all, feat_all, vec_all = gather_weights(
        in_layer[0, 0], mid_layer[0, 0], feat_layer[0, 0], vectors[0]
    )
    weights = (
        in_all.reshape(128, 256),
        mid_all.reshape(256, 256),
        feat_all.reshape(256, 384),
        vec_all.reshape(1152).astype(jnp.bfloat16),
    )
    regions = lax.axis_size("region")
    found = forward(
        ray_codes, depth_bins[0], entries[0], exits[0], weights, depth_scale / (regions * BINS)
    )
    colour, optical, local_weight = (found[4], found[5], found[7])
    depth = jnp.sum(optical, 0)
    local_partial = jnp.sum(local_weight[:, :, None] * colour, 0)
    entry_trans, after_sum, feature_grad = exchange_regions(
        local_partial.astype(jnp.bfloat16).reshape(NX, RX, FEAT),
        depth.reshape(NX, 1, RX),
        direction.reshape(NX, 1, RX),
        target,
    )
    entry_trans, after_sum = entry_trans.reshape(-1), after_sum.reshape(-1)
    feature_grad = feature_grad.reshape(NX * RX, FEAT)
    in_grad, mid_grad, feat_grad, vec_grad = backward(
        found, weights, entry_trans, after_sum, feature_grad
    )
    in_share, mid_share, feat_share, vec_share = reduce_grads(
        in_grad.reshape(NR, 16, 256),
        mid_grad.reshape(NR, 32, 256),
        feat_grad.reshape(NR, 32, 384),
        vec_grad.reshape(NR, 1, 144),
    )
    return (
        adam_update(in_layer[:, 0], in_share)[:, None],
        adam_update(mid_layer[:, 0], mid_share)[:, None],
        adam_update(feat_layer[:, 0], feat_share)[:, None],
        adam_update(vectors[:, 0], vec_share[0])[:, None],
        (-after_sum)[None],
    )


def solution(mesh):
    placed = (
        P(None, "rays", None),
        P("rays", None),
        P("rays"),
        P("region", "rays"),
        P("region", "rays"),
        P("region", None, "rays"),
        P(None, "region", "rays", None),
        P(None, "region", "rays", None),
        P(None, "region", "rays", None),
        P(None, "region", "rays"),
    )
    return jax.shard_map(
        per_device,
        mesh=mesh,
        in_specs=placed,
        out_specs=(
            P(None, "region", "rays", None),
            P(None, "region", "rays", None),
            P(None, "region", "rays", None),
            P(None, "region", "rays"),
            P("region", "rays"),
        ),
        check_vma=False,
    )
```

```python
import jax
import jax.numpy as jnp
from jax import lax
from jax.experimental import pallas as pl
from jax.experimental.pallas import tpu as pltpu
from jax.sharding import PartitionSpec as P

BINS = 64


depth_scale = 4.0
beta_one = 0.9
beta_two = 0.999
learn_rate = 0.001
epsilon = 1e-08
first_fix = 1.0 - 0.9**10
second_fix = 1.0 - 0.999**10

MESH = pl.DeviceIdType.MESH
NX = 4
NZ = 16
NR = 8
RX = 128
RZ = 8
IN = 128
HID = 256
FEAT = 384
SLOTS = 8
ROWS = SLOTS * RX
PART = 144
WIDE = 256
F32 = jnp.float32
BF16 = jnp.bfloat16


def vmem(count):
    return [pl.BlockSpec(memory_space=pltpu.VMEM)] * count


def remote(source, target, send_sem, recv_sem, peer):
    return pltpu.make_async_remote_copy(
        src_ref=source,
        dst_ref=target,
        send_sem=send_sem,
        recv_sem=recv_sem,
        device_id=peer,
        device_id_type=MESH,
    )


def gather_kernel(
    in_ref,
    mid_ref,
    feat_ref,
    vec_ref,
    in_out,
    mid_out,
    feat_out,
    vec_out,
    in_own,
    mid_own,
    feat_own,
    vec_own,
    load_sem,
    send_sem,
    recv_sem,
):
    me = lax.axis_index("rays")
    barrier = pltpu.get_barrier_semaphore()
    for step in range(1, NR):
        pl.semaphore_signal(
            barrier, inc=1, device_id={"rays": lax.rem(me + step, NR)}, device_id_type=MESH
        )
    loads = (
        pltpu.make_async_copy(in_ref.at[0, 0], in_own, load_sem.at[0]),
        pltpu.make_async_copy(mid_ref.at[0, 0], mid_own, load_sem.at[1]),
        pltpu.make_async_copy(feat_ref.at[0, 0], feat_own, load_sem.at[2]),
        pltpu.make_async_copy(vec_ref.at[0], vec_own, load_sem.at[3]),
    )
    for load in loads:
        load.start()
    for load in loads:
        load.wait()
    in_out[me] = in_own[...].astype(BF16)
    mid_out[me] = mid_own[...].astype(BF16)
    feat_out[me] = feat_own[...].astype(BF16)
    vec_out[me] = jnp.zeros((1, WIDE), F32)
    vec_out[me, :, pl.ds(0, PART)] = vec_own[...].astype(BF16).astype(F32)
    pl.semaphore_wait(barrier, NR - 1)
    outs = (in_out, mid_out, vec_out, feat_out)
    for kind, out in enumerate(outs):
        for step in range(1, NR):
            peer = lax.rem(me + step, NR)
            remote(
                out.at[me],
                out.at[me],
                send_sem.at[kind, step],
                recv_sem.at[kind, step],
                {"rays": peer},
            ).start()
    for kind, out in enumerate(outs):
        for step in range(1, NR):
            origin = lax.rem(me + NR - step, NR)
            remote(
                out.at[origin],
                out.at[origin],
                send_sem.at[kind, step],
                recv_sem.at[kind, step],
                {"rays": origin},
            ).wait()


def gather_weights(in_layer, mid_layer, feat_layer, vectors):
    shapes = (
        jax.ShapeDtypeStruct((NR, 16, 256), BF16),
        jax.ShapeDtypeStruct((NR, 32, 256), BF16),
        jax.ShapeDtypeStruct((NR, 32, 384), BF16),
        jax.ShapeDtypeStruct((NR, 1, WIDE), F32),
    )
    return pl.pallas_call(
        gather_kernel,
        out_shape=shapes,
        in_specs=[pl.BlockSpec(memory_space=pl.ANY)] * 4,
        out_specs=tuple(vmem(4)),
        scratch_shapes=[
            pltpu.VMEM((16, 256), F32),
            pltpu.VMEM((32, 256), F32),
            pltpu.VMEM((32, 384), F32),
            pltpu.VMEM((1, PART), F32),
            pltpu.SemaphoreType.DMA((4,)),
            pltpu.SemaphoreType.DMA((4, NR)),
            pltpu.SemaphoreType.DMA((4, NR)),
        ],
        compiler_params=pltpu.CompilerParams(collective_id=0, has_side_effects=True),
        name="gather_weights",
    )(in_layer, mid_layer, feat_layer, vectors)


def far_first(count):
    half = count // 2
    order = [half]
    for gap in range(1, half):
        order += [half - gap, half + gap]
    return order


def z_sums(table, own_z):
    column = jnp.zeros((NX, 1, RX), F32)
    lower = jnp.zeros((NX, 1, RX), F32)
    upper = jnp.zeros((NX, 1, RX), F32)
    for z in range(NZ):
        rows = table[z]
        column = column + rows
        lower = lower + rows * (z < own_z).astype(F32)
        upper = upper + rows * (z > own_z).astype(F32)
    return column, lower, upper


def x_sums(column, lower, upper):
    below, above = [], []
    for x in range(NX):
        under, over = lower[x], upper[x]
        for other in range(NX):
            if other < x:
                under = under + column[other]
            if other > x:
                over = over + column[other]
        below.append(under)
        above.append(over)
    return below, above


def one_less_exp(value):
    series = value * (
        1.0 - value / 2.0 * (1.0 - value / 3.0 * (1.0 - value / 4.0 * (1.0 - value / 5.0)))
    )
    return jnp.where(value < 0.0625, series, 1.0 - jnp.exp(-value))


def sum_before(rows):
    running = jnp.zeros((1, RX), F32)
    found = []
    for slot in range(SLOTS):
        found.append(running)
        running = running + rows[slot : slot + 1]
    return jnp.concatenate(found, 0), running


def sum_after(rows):
    running = jnp.zeros((1, RX), F32)
    found = []
    for slot in range(SLOTS - 1, -1, -1):
        found.append(running)
        running = running + rows[slot : slot + 1]
    return jnp.concatenate(found[::-1], 0)


def to_row_groups(values):
    return jnp.sum(values.reshape(values.shape[0] // 8, 8, values.shape[1]), 0)


def dot_nt(left, right):
    return lax.dot_general(left, right, (((1,), (1,)), ((), ())), preferred_element_type=F32)


def step_kernel(
    codes_ref,
    bins_ref,
    entry_ref,
    exit_ref,
    onward_ref,
    target_ref,
    w_in,
    w_mid,
    w_feat,
    vec_ref,
    in_out,
    mid_out,
    feat_out,
    vec_out,
    after_out,
    enc,
    h1,
    h2,
    enc_t,
    h1_t,
    h2_t,
    colour,
    coef,
    cgrad,
    hgrad,
    second,
    first,
    raw_rows,
    optical_rows,
    before_rows,
    weight_rows,
    span_rows,
    sample_rows,
    dense_wide,
    vec_row,
    g_in,
    g_mid,
    g_feat,
    sum_one,
    sum_two,
    sum_dense,
    sum_feat,
    depth_z,
    stats_send,
    stats_x,
    partial_send,
    partial_x,
    trans_send,
    trans_all,
    pieces,
    pieces_z,
    grad_z,
    grad_all,
    region_z,
    after_send,
    in_send,
    mid_send,
    feat_send,
    vec_send,
    in_got,
    mid_got,
    feat_got,
    vec_got,
    sem_depth,
    sem_stats,
    sem_partial,
    sem_trans,
    sem_piece,
    sem_grad_z,
    sem_grad,
    sem_region,
    sem_after,
    sem_rays,
):
    place = lax.axis_index("region")
    me = lax.axis_index("rays")
    own_x, own_z = place // NZ, lax.rem(place, NZ)

    def along_x(step):
        return lax.rem(own_x + step, NX)

    def along_z(step):
        return lax.rem(own_z + step, NZ)

    def at(x, z):
        return {"region": x * NZ + z}

    barrier = pltpu.get_barrier_semaphore()
    for step in range(1, NZ):
        pl.semaphore_signal(
            barrier, inc=1, device_id=at(own_x, along_z(step)), device_id_type=MESH
        )
    for step in range(1, NX):
        pl.semaphore_signal(
            barrier, inc=1, device_id=at(along_x(step), own_z), device_id_type=MESH
        )
    for step in range(1, NR):
        pl.semaphore_signal(
            barrier, inc=1, device_id={"rays": lax.rem(me + step, NR)}, device_id_type=MESH
        )

    def move_x(step, source, target, sems):
        x = along_x(step)
        return remote(
            source(x), target.at[own_x], sems.at[0, step], sems.at[1, step], at(x, own_z)
        )

    def spread_x(source, target, sems):
        for step in (2, 1, 3):
            move_x(step, source, target, sems).start()

    def wait_x(source, target, sems, steps=(1, 3, 2)):
        for step in steps:
            x = along_x(NX - step)
            remote(source(x), target.at[x], sems.at[0, step], sems.at[1, step], at(x, own_z)).wait()

    def spread_z(source, target, sems):
        for step in far_first(NZ):
            z = along_z(step)
            remote(
                source(z), target.at[own_z], sems.at[0, step], sems.at[1, step], at(own_x, z)
            ).start()

    def wait_z(source, target, sems):
        for step in far_first(NZ)[::-1]:
            z = along_z(NZ - step)
            remote(source(z), target.at[z], sems.at[0, step], sems.at[1, step], at(own_x, z)).wait()

    def spread_rays(kind, source, target):
        for step in range(1, NR):
            peer = lax.rem(me + step, NR)
            remote(
                source.at[peer],
                target.at[step],
                sem_rays.at[0, kind, step],
                sem_rays.at[1, kind, step],
                {"rays": peer},
            ).start()

    def gather_rays(kind, source, target, total):
        for step in range(1, NR):
            origin = lax.rem(me + NR - step, NR)
            remote(
                source.at[origin],
                target.at[step],
                sem_rays.at[0, kind, step],
                sem_rays.at[1, kind, step],
                {"rays": origin},
            ).wait()
            total = total + target[step].astype(F32)
        return total

    unit = depth_scale / (NX * NZ * BINS)
    lane = lax.broadcasted_iota(jnp.int32, (RX, RX), 1)
    slot_row = lax.broadcasted_iota(jnp.int32, (SLOTS, RX), 0)

    row = jnp.zeros((1, 1280), F32)
    tail = jnp.zeros((1, 1280 - WIDE), F32)
    for index in range(NR):
        wide = jnp.concatenate([vec_ref[index], tail], 1)
        row = row + (pltpu.roll(wide, PART * index, 1) if index else wide)
    vec_row[...] = row
    dense_wide[...] = jnp.transpose(
        jnp.broadcast_to(row[:, 2 * HID : 3 * HID], (RX, HID))
    ).astype(BF16)
    for total in (g_in, g_mid, g_feat, sum_one, sum_two, sum_dense, sum_feat):
        total[...] = jnp.zeros(total.shape, F32)

    depth_own = depth_z.at[own_z]

    def hidden_part(index, carry):
        x = along_x(index + 1)
        lanes = pl.ds(pl.multiple_of(x * RX, RX), RX)
        bins = bins_ref[:, lanes].astype(F32)
        columns = jnp.transpose((bins + 0.5) / BINS)
        anchor = codes_ref[0, lanes, :].astype(F32)
        heading = codes_ref[1, lanes, :].astype(F32)
        for slot in range(SLOTS):
            enc[x, pl.ds(slot * RX, RX), :] = (
                anchor + columns[:, slot : slot + 1] * heading
            ).astype(BF16)
        h1[x] = jnp.maximum(
            jnp.dot(enc[x], w_in[...], preferred_element_type=F32) + vec_row[:, :HID], 0.0
        ).astype(BF16)
        h2[x] = jnp.maximum(
            jnp.dot(h1[x], w_mid[...], preferred_element_type=F32) + vec_row[:, HID : 2 * HID],
            0.0,
        ).astype(BF16)
        dense = jnp.dot(h2[x], dense_wide[...], preferred_element_type=F32)
        grid = jnp.zeros((RX, RX), F32)
        for slot in range(SLOTS):
            grid = jnp.where(lane == slot, dense[slot * RX : (slot + 1) * RX], grid)
        raw = jnp.transpose(grid)[:SLOTS]
        following = jnp.concatenate([bins[1:], jnp.full((1, RX), float(BINS), F32)], 0)
        inside = (slot_row >= entry_ref[:, lanes]) & (slot_row < exit_ref[:, lanes])
        span = jnp.where(inside, (following - bins) * unit, 0.0)
        soft = jnp.maximum(raw, 0.0) + jnp.log1p(jnp.exp(-jnp.abs(raw)))
        optical = soft * span
        before, total = sum_before(optical)
        raw_rows[x] = raw
        optical_rows[x] = optical
        before_rows[x] = before
        weight_rows[x] = jnp.exp(-before) * one_less_exp(optical)
        span_rows[x] = span
        depth_own[x] = total
        return carry

    lax.fori_loop(0, NX, hidden_part, 0)
    pl.semaphore_wait(barrier, NX + NZ + NR - 3)
    spread_z(lambda z: depth_own, depth_z, sem_depth)

    def colour_part(index, carry):
        x = along_x(index + 1)
        colour[x] = jax.nn.sigmoid(
            jnp.dot(h2[x], w_feat[...], preferred_element_type=F32)
            + vec_row[:, 3 * HID : 3 * HID + FEAT]
        )
        columns = jnp.transpose(weight_rows[x])
        local = jnp.zeros((RX, FEAT), F32)
        for slot in range(SLOTS):
            local = local + columns[:, slot : slot + 1] * colour[x, pl.ds(slot * RX, RX), :]
        partial_send[x] = local.astype(BF16)

        @pl.when(index < NX - 1)
        def _():
            move_x(index + 1, lambda x: partial_send.at[x], partial_x, sem_partial).start()

        return carry

    lax.fori_loop(0, NX, colour_part, 0)
    partial_x[own_x] = partial_send[own_x]
    wait_z(lambda z: depth_own, depth_z, sem_depth)
    column, lower, upper = z_sums(depth_z, own_z)
    for x in range(NX):
        stats_send[x, 0] = column[x]
        stats_send[x, 1] = lower[x]
        stats_send[x, 2] = upper[x]
    stats_x[own_x] = stats_send[own_x]
    spread_x(lambda x: stats_send.at[x], stats_x, sem_stats)
    wait_x(lambda x: stats_send.at[x], stats_x, sem_stats)
    below, above = x_sums(
        [stats_x[x, 0] for x in range(NX)],
        [stats_x[x, 1] for x in range(NX)],
        [stats_x[x, 2] for x in range(NX)],
    )
    onward = onward_ref[own_x] == 0
    trans = [jnp.exp(-jnp.where(onward, below[x], above[x])) for x in range(NX)]
    for x in range(NX):
        trans_send[x] = trans[x]
    trans_all[own_x] = trans_send[own_x]
    spread_x(lambda x: trans_send.at[x], trans_all, sem_trans)
    columns = jnp.transpose(jnp.concatenate(trans + trans, 0))
    wait_x(lambda x: partial_send.at[x], partial_x, sem_partial)
    total = jnp.zeros((RX, FEAT), F32)
    for x in range(NX):
        total = total + columns[:, x : x + 1] * partial_x[x].astype(F32)
    pieces[...] = total.reshape(NZ, RZ, FEAT).astype(BF16)
    spread_z(lambda z: pieces.at[z], pieces_z, sem_piece)
    pieces_z[own_z] = pieces[own_z]

    def turn_part(x, carry):
        h1_t[x] = jnp.transpose(h1[x])
        h2_t[x] = jnp.transpose(h2[x])
        return carry

    lax.fori_loop(0, NX, turn_part, 0)
    start = pl.multiple_of(own_x * RX + (own_z // 2) * (2 * RZ), 2 * RZ)
    wanted = target_ref[pl.ds(start, 2 * RZ), :].astype(F32)
    odd = lax.rem(own_z, 2).astype(F32)
    wanted = wanted[:RZ] * (1.0 - odd) + wanted[RZ:] * odd
    wait_z(lambda z: pieces.at[z], pieces_z, sem_piece)
    rendered = jnp.sum(pieces_z[...].astype(F32), 0)
    grad_z[own_z] = (rendered - wanted).astype(BF16)
    spread_z(lambda z: grad_z.at[own_z], grad_z, sem_grad_z)
    wait_x(lambda x: trans_send.at[x], trans_all, sem_trans)

    def coef_part(x, carry):
        enc_t[x] = jnp.transpose(enc[x])
        columns = jnp.transpose(trans_all[x] * weight_rows[x])
        for slot in range(SLOTS):
            rows = pl.ds(slot * RX, RX)
            shade = colour[x, rows, :]
            coef[x, rows, :] = columns[:, slot : slot + 1] * (shade * (1.0 - shade))
        return carry

    lax.fori_loop(0, NX, coef_part, 0)
    wait_z(lambda z: grad_z.at[own_z], grad_z, sem_grad_z)
    grad_float = grad_z[...].astype(F32).reshape(RX, FEAT)
    grad_all[own_x] = grad_float.astype(BF16)
    spread_x(lambda x: grad_all.at[own_x], grad_all, sem_grad)
    grid = jnp.zeros((RX, RX), F32)
    for x in range(NX):
        dots = jnp.sum(grad_float * partial_x[x].astype(F32), -1, keepdims=True)
        grid = jnp.where(lane == x, dots, grid)
    grid = jnp.transpose(grid)
    region_own = region_z.at[own_z]
    for x in range(NX):
        region_own[x] = grid[x : x + 1] * trans_send[x]
    spread_z(lambda z: region_own, region_z, sem_region)

    def feat_part(index, carry):
        x = along_x(index)

        @pl.when(index > 0)
        def _():
            wait_x(lambda x: grad_all.at[own_x], grad_all, sem_grad, (NX - index,))

        grads = grad_all[x].astype(F32)
        grid = jnp.zeros((RX, RX), F32)
        added = jnp.zeros((8, FEAT), F32)
        for slot in range(SLOTS):
            rows = pl.ds(slot * RX, RX)
            shade = colour[x, rows, :]
            grid = jnp.where(lane == slot, jnp.sum(shade * grads, -1, keepdims=True), grid)
            found = (coef[x, rows, :] * grads).astype(BF16)
            cgrad[rows, :] = found
            added = added + to_row_groups(found.astype(F32))
        sample_rows[x] = jnp.transpose(grid)[:SLOTS]
        sum_feat[...] += added
        g_feat[...] += jnp.dot(h2_t[x], cgrad[...], preferred_element_type=F32)
        hgrad[x] = dot_nt(cgrad[...], w_feat[...])
        return carry

    lax.fori_loop(0, NX, feat_part, 0)
    feat_send[...] = g_feat[...].astype(BF16).reshape(NR, 32, FEAT)
    spread_rays(0, feat_send, feat_got)
    wait_z(lambda z: region_own, region_z, sem_region)
    below, above = x_sums(*z_sums(region_z, own_z))
    for x in range(NX):
        after_send[x] = jnp.where(onward, above[x], below[x])
    after_out[own_x] = after_send[own_x]
    spread_x(lambda x: after_send.at[x], after_out, sem_after)
    wait_x(lambda x: after_send.at[x], after_out, sem_after)

    def mid_part(x, carry):
        samples = sample_rows[x]
        later = sum_after(weight_rows[x] * samples)
        optical_grad = (
            trans_all[x] * (jnp.exp(-(before_rows[x] + optical_rows[x])) * samples - later)
            - after_out[x]
        )
        dense_grad = (
            (optical_grad * span_rows[x] * jax.nn.sigmoid(raw_rows[x])).astype(BF16).astype(F32)
        )
        columns = jnp.transpose(dense_grad)
        dense_row = vec_row[:, 2 * HID : 3 * HID]
        added = jnp.zeros((8, HID), F32)
        dense_added = jnp.zeros((8, HID), F32)
        for slot in range(SLOTS):
            rows = pl.ds(slot * RX, RX)
            hidden = h2[x, rows, :].astype(F32)
            scale = columns[:, slot : slot + 1]
            found = jnp.where(hidden > 0.0, hgrad[x, rows, :] + scale * dense_row, 0.0)
            found = found.astype(BF16)
            second[x, rows, :] = found
            added = added + to_row_groups(found.astype(F32))
            dense_added = dense_added + to_row_groups(scale * hidden)
        sum_two[...] += added
        sum_dense[...] += dense_added
        g_mid[...] += jnp.dot(h1_t[x], second[x], preferred_element_type=F32)
        return carry

    lax.fori_loop(0, NX, mid_part, 0)
    mid_send[...] = g_mid[...].astype(BF16).reshape(NR, 32, HID)
    spread_rays(1, mid_send, mid_got)

    def in_part(x, carry):
        found = jnp.where(
            h1[x].astype(F32) > 0.0, dot_nt(second[x], w_mid[...]), 0.0
        ).astype(BF16)
        first[...] = found
        sum_one[...] += to_row_groups(found.astype(F32))
        g_in[...] += jnp.dot(enc_t[x], first[...], preferred_element_type=F32)
        return carry

    lax.fori_loop(0, NX, in_part, 0)
    in_send[...] = g_in[...].astype(BF16).reshape(NR, 16, HID)
    spread_rays(2, in_send, in_got)
    sums = [
        jnp.sum(part[...], 0, keepdims=True) for part in (sum_one, sum_two, sum_dense, sum_feat)
    ]
    row = jnp.concatenate(sums + [jnp.zeros((1, 128), F32)], 1)
    for index in range(NR):
        turned = pltpu.roll(row, 1280 - PART * index, 1) if index else row
        vec_send[index] = turned[:, :WIDE]
    spread_rays(3, vec_send, vec_got)

    def own_rows(total, count):
        return total[pl.ds(pl.multiple_of(me * count, count), count), :]

    feat_out[...] = gather_rays(0, feat_send, feat_got, own_rows(g_feat, 32))
    mid_out[...] = gather_rays(1, mid_send, mid_got, own_rows(g_mid, 32))
    in_out[...] = gather_rays(2, in_send, in_got, own_rows(g_in, 16))
    vec_out[...] = gather_rays(3, vec_send, vec_got, vec_send[me])


def run_step(*operands):
    def pair(count):
        return pltpu.SemaphoreType.DMA((2, count))

    outs = (((16, 256), F32), ((32, 256), F32), ((32, 384), F32), ((1, WIDE), F32))
    outs += (((NX, 1, RX), F32),)
    scratch = (
        ((NX, ROWS, IN), BF16),
        ((NX, ROWS, HID), BF16),
        ((NX, ROWS, HID), BF16),
        ((NX, IN, ROWS), BF16),
        ((NX, HID, ROWS), BF16),
        ((NX, HID, ROWS), BF16),
        ((NX, ROWS, FEAT), F32),
        ((NX, ROWS, FEAT), F32),
        ((ROWS, FEAT), BF16),
        ((NX, ROWS, HID), F32),
        ((NX, ROWS, HID), BF16),
        ((ROWS, HID), BF16),
        ((NX, SLOTS, RX), F32),
        ((NX, SLOTS, RX), F32),
        ((NX, SLOTS, RX), F32),
        ((NX, SLOTS, RX), F32),
        ((NX, SLOTS, RX), F32),
        ((NX, SLOTS, RX), F32),
        ((HID, RX), BF16),
        ((1, 1280), F32),
        ((IN, HID), F32),
        ((HID, HID), F32),
        ((HID, FEAT), F32),
        ((8, HID), F32),
        ((8, HID), F32),
        ((8, HID), F32),
        ((8, FEAT), F32),
        ((NZ, NX, 1, RX), F32),
        ((NX, 3, 1, RX), F32),
        ((NX, 3, 1, RX), F32),
        ((NX, RX, FEAT), BF16),
        ((NX, RX, FEAT), BF16),
        ((NX, 1, RX), F32),
        ((NX, 1, RX), F32),
        ((NZ, RZ, FEAT), BF16),
        ((NZ, RZ, FEAT), BF16),
        ((NZ, RZ, FEAT), BF16),
        ((NX, RX, FEAT), BF16),
        ((NZ, NX, 1, RX), F32),
        ((NX, 1, RX), F32),
        ((NR, 16, 256), BF16),
        ((NR, 32, 256), BF16),
        ((NR, 32, 384), BF16),
        ((NR, 1, WIDE), F32),
        ((NR, 16, 256), BF16),
        ((NR, 32, 256), BF16),
        ((NR, 32, 384), BF16),
        ((NR, 1, WIDE), F32),
    )
    return pl.pallas_call(
        step_kernel,
        out_shape=tuple(jax.ShapeDtypeStruct(*out) for out in outs),
        in_specs=vmem(len(operands)),
        out_specs=tuple(vmem(len(outs))),
        scratch_shapes=[pltpu.VMEM(*part) for part in scratch]
        + [pair(NZ), pair(NX), pair(NX), pair(NX), pair(NZ), pair(NZ), pair(NX), pair(NZ), pair(NX)]
        + [pltpu.SemaphoreType.DMA((2, 4, NR))],
        compiler_params=pltpu.CompilerParams(
            collective_id=1, has_side_effects=True, vmem_limit_bytes=56 * 2**20
        ),
        name="run_step",
    )(*operands)


def adam_kernel(*refs):
    states, grads, after_ref, outs, depth_out = refs[:4], refs[4:8], refs[8], refs[9:13], refs[13]
    for state, grad, out in zip(states, grads, outs):
        gradient = grad[...].reshape((1,) + grad.shape) if len(state.shape) == 4 else grad[...]
        gradient = gradient[..., : state.shape[-1]]
        first_moment = beta_one * state[1] + (1.0 - beta_one) * gradient
        second = beta_two * state[2] + (1.0 - beta_two) * gradient * gradient
        update_step = first_moment / first_fix / (jnp.sqrt(second / second_fix) + epsilon)
        out[0] = state[0] - learn_rate * update_step
        out[1] = first_moment
        out[2] = second
    depth_out[...] = -after_ref[...]


def adam_all(states, grads, after):
    shapes = [jax.ShapeDtypeStruct(state.shape, F32) for state in states]
    shapes.append(jax.ShapeDtypeStruct(after.shape, F32))
    return pl.pallas_call(
        adam_kernel,
        out_shape=tuple(shapes),
        in_specs=vmem(9),
        out_specs=tuple(vmem(5)),
        name="adam_all",
    )(*states, *grads, after)


def per_device(
    ray_codes,
    target,
    direction,
    entries,
    exits,
    depth_bins,
    in_layer,
    mid_layer,
    feat_layer,
    vectors,
):
    in_all, mid_all, feat_all, vec_all = gather_weights(in_layer, mid_layer, feat_layer, vectors)
    *grads, after = run_step(
        ray_codes,
        depth_bins[0],
        entries,
        exits,
        direction.reshape(NX, 1, RX),
        target,
        in_all.reshape(IN, HID),
        mid_all.reshape(HID, HID),
        feat_all.reshape(HID, FEAT),
        vec_all,
    )
    *states, depth_grad = adam_all((in_layer, mid_layer, feat_layer, vectors), grads, after)
    return (*states, depth_grad.reshape(1, NX * RX))


def solution(mesh):
    placed = (
        P(None, "rays", None),
        P("rays", None),
        P("rays"),
        P("region", "rays"),
        P("region", "rays"),
        P("region", None, "rays"),
        P(None, "region", "rays", None),
        P(None, "region", "rays", None),
        P(None, "region", "rays", None),
        P(None, "region", "rays"),
    )
    return jax.shard_map(
        per_device,
        mesh=mesh,
        in_specs=placed,
        out_specs=(
            P(None, "region", "rays", None),
            P(None, "region", "rays", None),
            P(None, "region", "rays", None),
            P(None, "region", "rays"),
            P("region", "rays"),
        ),
        check_vma=False,
    )
```

```python
import jax
import jax.numpy as jnp
from jax import lax
from jax.experimental import pallas as pl
from jax.experimental.pallas import tpu as pltpu
from jax.sharding import PartitionSpec as P

BINS = 64


depth_scale = 4.0
beta_one = 0.9
beta_two = 0.999
learn_rate = 0.001
epsilon = 1e-08
first_fix = 1.0 - 0.9**10
second_fix = 1.0 - 0.999**10

MESH = pl.DeviceIdType.MESH
NX = 4
NZ = 16
NR = 8
RX = 128
RZ = 8
IN = 128
HID = 256
FEAT = 384
SLOTS = 8
ROWS = SLOTS * RX
PART = 144
WIDE = 256
F32 = jnp.float32
BF16 = jnp.bfloat16


def vmem(count):
    return [pl.BlockSpec(memory_space=pltpu.VMEM)] * count


def remote(source, target, send_sem, recv_sem, peer):
    return pltpu.make_async_remote_copy(
        src_ref=source,
        dst_ref=target,
        send_sem=send_sem,
        recv_sem=recv_sem,
        device_id=peer,
        device_id_type=MESH,
    )


def far_first(count):
    half = count // 2
    order = [half]
    for gap in range(1, half):
        order += [half - gap, half + gap]
    return order


def z_sums(table, own_z):
    column = jnp.zeros((NX, 1, RX), F32)
    lower = jnp.zeros((NX, 1, RX), F32)
    upper = jnp.zeros((NX, 1, RX), F32)
    for z in range(NZ):
        rows = table[z]
        column = column + rows
        lower = lower + rows * (z < own_z).astype(F32)
        upper = upper + rows * (z > own_z).astype(F32)
    return column, lower, upper


def x_sums(column, lower, upper):
    below, above = [], []
    for x in range(NX):
        under, over = lower[x], upper[x]
        for other in range(NX):
            if other < x:
                under = under + column[other]
            if other > x:
                over = over + column[other]
        below.append(under)
        above.append(over)
    return below, above


def one_less_exp(value):
    series = value * (
        1.0 - value / 2.0 * (1.0 - value / 3.0 * (1.0 - value / 4.0 * (1.0 - value / 5.0)))
    )
    return jnp.where(value < 0.0625, series, 1.0 - jnp.exp(-value))


def sum_before(rows):
    running = jnp.zeros((1, RX), F32)
    found = []
    for slot in range(SLOTS):
        found.append(running)
        running = running + rows[slot : slot + 1]
    return jnp.concatenate(found, 0), running


def sum_after(rows):
    running = jnp.zeros((1, RX), F32)
    found = []
    for slot in range(SLOTS - 1, -1, -1):
        found.append(running)
        running = running + rows[slot : slot + 1]
    return jnp.concatenate(found[::-1], 0)


def to_row_groups(values):
    return jnp.sum(values.reshape(values.shape[0] // 8, 8, values.shape[1]), 0)


def dot_nt(left, right):
    return lax.dot_general(left, right, (((1,), (1,)), ((), ())), preferred_element_type=F32)


def step_kernel(
    codes_hbm,
    bins_hbm,
    entry_hbm,
    exit_hbm,
    onward_hbm,
    target_hbm,
    in_layer,
    mid_layer,
    feat_layer,
    vectors,
    in_out,
    mid_out,
    feat_out,
    vec_out,
    after_out,
    codes_ref,
    bins_ref,
    entry_ref,
    exit_ref,
    onward_ref,
    target_ref,
    in_own,
    mid_own,
    feat_own,
    vec_own,
    w_in,
    w_mid,
    w_feat,
    vec_ref,
    enc,
    h1,
    h2,
    enc_t,
    h1_t,
    h2_t,
    colour,
    coef,
    cgrad,
    hgrad,
    second,
    first,
    raw_rows,
    optical_rows,
    before_rows,
    weight_rows,
    span_rows,
    sample_rows,
    dense_wide,
    vec_row,
    g_in,
    g_mid,
    g_feat,
    sum_one,
    sum_two,
    sum_dense,
    sum_feat,
    depth_z,
    stats_send,
    stats_x,
    partial_send,
    partial_x,
    trans_send,
    trans_all,
    pieces,
    pieces_z,
    grad_z,
    grad_all,
    region_z,
    after_send,
    in_send,
    mid_send,
    feat_send,
    vec_send,
    in_got,
    mid_got,
    feat_got,
    vec_got,
    sem_depth,
    sem_stats,
    sem_partial,
    sem_trans,
    sem_piece,
    sem_grad_z,
    sem_grad,
    sem_region,
    sem_after,
    sem_rays,
    sem_load,
    sem_weight,
):
    place = lax.axis_index("region")
    me = lax.axis_index("rays")
    own_x, own_z = place // NZ, lax.rem(place, NZ)

    def along_x(step):
        return lax.rem(own_x + step, NX)

    def along_z(step):
        return lax.rem(own_z + step, NZ)

    def at(x, z):
        return {"region": x * NZ + z}

    barrier = pltpu.get_barrier_semaphore()
    for step in range(1, NZ):
        pl.semaphore_signal(
            barrier, inc=1, device_id=at(own_x, along_z(step)), device_id_type=MESH
        )
    for step in range(1, NX):
        pl.semaphore_signal(
            barrier, inc=1, device_id=at(along_x(step), own_z), device_id_type=MESH
        )
    for step in range(1, NR):
        pl.semaphore_signal(
            barrier, inc=1, device_id={"rays": lax.rem(me + step, NR)}, device_id_type=MESH
        )

    def move_x(step, source, target, sems):
        x = along_x(step)
        return remote(
            source(x), target.at[own_x], sems.at[0, step], sems.at[1, step], at(x, own_z)
        )

    def spread_x(source, target, sems):
        for step in (2, 1, 3):
            move_x(step, source, target, sems).start()

    def wait_x(source, target, sems, steps=(1, 3, 2)):
        for step in steps:
            x = along_x(NX - step)
            remote(source(x), target.at[x], sems.at[0, step], sems.at[1, step], at(x, own_z)).wait()

    def spread_z(source, target, sems):
        for step in far_first(NZ):
            z = along_z(step)
            remote(
                source(z), target.at[own_z], sems.at[0, step], sems.at[1, step], at(own_x, z)
            ).start()

    def wait_z(source, target, sems):
        for step in far_first(NZ)[::-1]:
            z = along_z(NZ - step)
            remote(source(z), target.at[z], sems.at[0, step], sems.at[1, step], at(own_x, z)).wait()

    def spread_rays(kind, source, target):
        for step in range(1, NR):
            peer = lax.rem(me + step, NR)
            remote(
                source.at[peer],
                target.at[step],
                sem_rays.at[0, kind, step],
                sem_rays.at[1, kind, step],
                {"rays": peer},
            ).start()

    def gather_rays(kind, source, target, total):
        for step in range(1, NR):
            origin = lax.rem(me + NR - step, NR)
            remote(
                source.at[origin],
                target.at[step],
                sem_rays.at[0, kind, step],
                sem_rays.at[1, kind, step],
                {"rays": origin},
            ).wait()
            total = total + target[step].astype(F32)
        return total

    loads = [
        pltpu.make_async_copy(source, target, sem_load.at[index])
        for index, (source, target) in enumerate(
            (
                (in_layer.at[0, 0], in_own),
                (mid_layer.at[0, 0], mid_own),
                (feat_layer.at[0, 0], feat_own),
                (vectors.at[0], vec_own),
                (codes_hbm, codes_ref),
                (bins_hbm.at[0], bins_ref),
                (entry_hbm, entry_ref),
                (exit_hbm, exit_ref),
                (onward_hbm, onward_ref),
                (target_hbm, target_ref),
            )
        )
    ]
    for load in loads:
        load.start()

    def mine(array, count, index):
        return array.at[pl.ds(pl.multiple_of(index * count, count), count)]

    weights = (
        lambda index: mine(w_in, 16, index),
        lambda index: mine(w_mid, 32, index),
        lambda index: vec_ref.at[index],
        lambda index: mine(w_feat, 32, index),
    )

    def spread_weights(kind):
        for step in range(1, NR):
            remote(
                weights[kind](me),
                weights[kind](me),
                sem_weight.at[0, kind, step],
                sem_weight.at[1, kind, step],
                {"rays": lax.rem(me + step, NR)},
            ).start()

    def wait_weights(kind):
        for step in range(1, NR):
            origin = lax.rem(me + NR - step, NR)
            remote(
                weights[kind](origin),
                weights[kind](origin),
                sem_weight.at[0, kind, step],
                sem_weight.at[1, kind, step],
                {"rays": origin},
            ).wait()

    unit = depth_scale / (NX * NZ * BINS)
    lane = lax.broadcasted_iota(jnp.int32, (RX, RX), 1)
    slot_row = lax.broadcasted_iota(jnp.int32, (SLOTS, RX), 0)
    for load in loads[:4]:
        load.wait()
    weights[0](me)[...] = in_own[...].astype(BF16)
    weights[1](me)[...] = mid_own[...].astype(BF16)
    weights[3](me)[...] = feat_own[...].astype(BF16)
    vec_ref[me] = jnp.zeros((1, WIDE), F32)
    vec_ref[me, :, pl.ds(0, PART)] = vec_own[...].astype(BF16).astype(F32)
    for load in loads[4:]:
        load.wait()
    for total in (g_in, g_mid, g_feat, sum_one, sum_two, sum_dense, sum_feat):
        total[...] = jnp.zeros(total.shape, F32)

    def code_part(x, carry):
        lanes = pl.ds(pl.multiple_of(x * RX, RX), RX)
        bins = bins_ref[:, lanes].astype(F32)
        columns = jnp.transpose((bins + 0.5) / BINS)
        anchor = codes_ref[0, lanes, :].astype(F32)
        heading = codes_ref[1, lanes, :].astype(F32)
        for slot in range(SLOTS):
            enc[x, pl.ds(slot * RX, RX), :] = (
                anchor + columns[:, slot : slot + 1] * heading
            ).astype(BF16)
        following = jnp.concatenate([bins[1:], jnp.full((1, RX), float(BINS), F32)], 0)
        inside = (slot_row >= entry_ref[:, lanes]) & (slot_row < exit_ref[:, lanes])
        span_rows[x] = jnp.where(inside, (following - bins) * unit, 0.0)
        return carry

    lax.fori_loop(0, NX, code_part, 0)
    pl.semaphore_wait(barrier, NX + NZ + NR - 3)
    for kind in range(4):
        spread_weights(kind)

    def turn_code(x, carry):
        enc_t[x] = jnp.transpose(enc[x])
        return carry

    lax.fori_loop(0, NX, turn_code, 0)
    for kind in range(3):
        wait_weights(kind)
    row = jnp.zeros((1, 1280), F32)
    tail = jnp.zeros((1, 1280 - WIDE), F32)
    for index in range(NR):
        wide = jnp.concatenate([vec_ref[index], tail], 1)
        row = row + (pltpu.roll(wide, PART * index, 1) if index else wide)
    vec_row[...] = row
    dense_wide[...] = jnp.transpose(
        jnp.broadcast_to(row[:, 2 * HID : 3 * HID], (RX, HID))
    ).astype(BF16)

    depth_own = depth_z.at[own_z]

    def hidden_part(index, carry):
        x = along_x(index + 1)
        h1[x] = jnp.maximum(
            jnp.dot(enc[x], w_in[...], preferred_element_type=F32) + vec_row[:, :HID], 0.0
        ).astype(BF16)
        h2[x] = jnp.maximum(
            jnp.dot(h1[x], w_mid[...], preferred_element_type=F32) + vec_row[:, HID : 2 * HID],
            0.0,
        ).astype(BF16)
        dense = jnp.dot(h2[x], dense_wide[...], preferred_element_type=F32)
        grid = jnp.zeros((RX, RX), F32)
        for slot in range(SLOTS):
            grid = jnp.where(lane == slot, dense[slot * RX : (slot + 1) * RX], grid)
        raw = jnp.transpose(grid)[:SLOTS]
        soft = jnp.maximum(raw, 0.0) + jnp.log1p(jnp.exp(-jnp.abs(raw)))
        optical = soft * span_rows[x]
        before, total = sum_before(optical)
        raw_rows[x] = raw
        optical_rows[x] = optical
        before_rows[x] = before
        weight_rows[x] = jnp.exp(-before) * one_less_exp(optical)
        depth_own[x] = total
        return carry

    lax.fori_loop(0, NX, hidden_part, 0)
    spread_z(lambda z: depth_own, depth_z, sem_depth)
    wait_weights(3)

    def colour_part(index, carry):
        x = along_x(index + 1)
        colour[x] = jax.nn.sigmoid(
            jnp.dot(h2[x], w_feat[...], preferred_element_type=F32)
            + vec_row[:, 3 * HID : 3 * HID + FEAT]
        )
        columns = jnp.transpose(weight_rows[x])
        local = jnp.zeros((RX, FEAT), F32)
        for slot in range(SLOTS):
            local = local + columns[:, slot : slot + 1] * colour[x, pl.ds(slot * RX, RX), :]
        partial_send[x] = local.astype(BF16)

        @pl.when(index < NX - 1)
        def _():
            move_x(index + 1, lambda x: partial_send.at[x], partial_x, sem_partial).start()

        return carry

    lax.fori_loop(0, NX, colour_part, 0)
    partial_x[own_x] = partial_send[own_x]
    wait_z(lambda z: depth_own, depth_z, sem_depth)
    column, lower, upper = z_sums(depth_z, own_z)
    for x in range(NX):
        stats_send[x, 0] = column[x]
        stats_send[x, 1] = lower[x]
        stats_send[x, 2] = upper[x]
    stats_x[own_x] = stats_send[own_x]
    spread_x(lambda x: stats_send.at[x], stats_x, sem_stats)
    wait_x(lambda x: stats_send.at[x], stats_x, sem_stats)
    below, above = x_sums(
        [stats_x[x, 0] for x in range(NX)],
        [stats_x[x, 1] for x in range(NX)],
        [stats_x[x, 2] for x in range(NX)],
    )
    onward = onward_ref[own_x] == 0
    trans = [jnp.exp(-jnp.where(onward, below[x], above[x])) for x in range(NX)]
    for x in range(NX):
        trans_send[x] = trans[x]
    trans_all[own_x] = trans_send[own_x]
    spread_x(lambda x: trans_send.at[x], trans_all, sem_trans)
    columns = jnp.transpose(jnp.concatenate(trans + trans, 0))
    wait_x(lambda x: partial_send.at[x], partial_x, sem_partial)
    total = jnp.zeros((RX, FEAT), F32)
    for x in range(NX):
        total = total + columns[:, x : x + 1] * partial_x[x].astype(F32)
    pieces[...] = total.reshape(NZ, RZ, FEAT).astype(BF16)
    spread_z(lambda z: pieces.at[z], pieces_z, sem_piece)
    pieces_z[own_z] = pieces[own_z]

    def turn_part(x, carry):
        h1_t[x] = jnp.transpose(h1[x])
        h2_t[x] = jnp.transpose(h2[x])
        return carry

    lax.fori_loop(0, NX, turn_part, 0)
    start = pl.multiple_of(own_x * RX + (own_z // 2) * (2 * RZ), 2 * RZ)
    wanted = target_ref[pl.ds(start, 2 * RZ), :].astype(F32)
    odd = lax.rem(own_z, 2).astype(F32)
    wanted = wanted[:RZ] * (1.0 - odd) + wanted[RZ:] * odd
    wait_z(lambda z: pieces.at[z], pieces_z, sem_piece)
    rendered = jnp.sum(pieces_z[...].astype(F32), 0)
    grad_z[own_z] = (rendered - wanted).astype(BF16)
    spread_z(lambda z: grad_z.at[own_z], grad_z, sem_grad_z)
    wait_x(lambda x: trans_send.at[x], trans_all, sem_trans)

    def coef_part(x, carry):
        columns = jnp.transpose(trans_all[x] * weight_rows[x])
        for slot in range(SLOTS):
            rows = pl.ds(slot * RX, RX)
            shade = colour[x, rows, :]
            coef[x, rows, :] = columns[:, slot : slot + 1] * (shade * (1.0 - shade))
        return carry

    lax.fori_loop(0, NX, coef_part, 0)
    wait_z(lambda z: grad_z.at[own_z], grad_z, sem_grad_z)
    grad_float = grad_z[...].astype(F32).reshape(RX, FEAT)
    grad_all[own_x] = grad_float.astype(BF16)
    spread_x(lambda x: grad_all.at[own_x], grad_all, sem_grad)
    grid = jnp.zeros((RX, RX), F32)
    for x in range(NX):
        dots = jnp.sum(grad_float * partial_x[x].astype(F32), -1, keepdims=True)
        grid = jnp.where(lane == x, dots, grid)
    grid = jnp.transpose(grid)
    region_own = region_z.at[own_z]
    for x in range(NX):
        region_own[x] = grid[x : x + 1] * trans_send[x]
    spread_z(lambda z: region_own, region_z, sem_region)

    def feat_part(index, carry):
        x = along_x(index)

        @pl.when(index > 0)
        def _():
            wait_x(lambda x: grad_all.at[own_x], grad_all, sem_grad, (NX - index,))

        grads = grad_all[x].astype(F32)
        grid = jnp.zeros((RX, RX), F32)
        added = jnp.zeros((8, FEAT), F32)
        for slot in range(SLOTS):
            rows = pl.ds(slot * RX, RX)
            shade = colour[x, rows, :]
            grid = jnp.where(lane == slot, jnp.sum(shade * grads, -1, keepdims=True), grid)
            found = (coef[x, rows, :] * grads).astype(BF16)
            cgrad[rows, :] = found
            added = added + to_row_groups(found.astype(F32))
        sample_rows[x] = jnp.transpose(grid)[:SLOTS]
        sum_feat[...] += added
        g_feat[...] += jnp.dot(h2_t[x], cgrad[...], preferred_element_type=F32)
        hgrad[x] = dot_nt(cgrad[...], w_feat[...])
        return carry

    lax.fori_loop(0, NX, feat_part, 0)
    feat_send[...] = g_feat[...].astype(BF16).reshape(NR, 32, FEAT)
    spread_rays(0, feat_send, feat_got)
    wait_z(lambda z: region_own, region_z, sem_region)
    below, above = x_sums(*z_sums(region_z, own_z))
    for x in range(NX):
        after_send[x] = jnp.where(onward, above[x], below[x])
    after_out[own_x] = after_send[own_x]
    spread_x(lambda x: after_send.at[x], after_out, sem_after)
    wait_x(lambda x: after_send.at[x], after_out, sem_after)

    def mid_part(x, carry):
        samples = sample_rows[x]
        later = sum_after(weight_rows[x] * samples)
        optical_grad = (
            trans_all[x] * (jnp.exp(-(before_rows[x] + optical_rows[x])) * samples - later)
            - after_out[x]
        )
        dense_grad = (
            (optical_grad * span_rows[x] * jax.nn.sigmoid(raw_rows[x])).astype(BF16).astype(F32)
        )
        columns = jnp.transpose(dense_grad)
        dense_row = vec_row[:, 2 * HID : 3 * HID]
        added = jnp.zeros((8, HID), F32)
        dense_added = jnp.zeros((8, HID), F32)
        for slot in range(SLOTS):
            rows = pl.ds(slot * RX, RX)
            hidden = h2[x, rows, :].astype(F32)
            scale = columns[:, slot : slot + 1]
            found = jnp.where(hidden > 0.0, hgrad[x, rows, :] + scale * dense_row, 0.0)
            found = found.astype(BF16)
            second[x, rows, :] = found
            added = added + to_row_groups(found.astype(F32))
            dense_added = dense_added + to_row_groups(scale * hidden)
        sum_two[...] += added
        sum_dense[...] += dense_added
        g_mid[...] += jnp.dot(h1_t[x], second[x], preferred_element_type=F32)
        return carry

    lax.fori_loop(0, NX, mid_part, 0)
    mid_send[...] = g_mid[...].astype(BF16).reshape(NR, 32, HID)
    spread_rays(1, mid_send, mid_got)

    def in_part(x, carry):
        found = jnp.where(
            h1[x].astype(F32) > 0.0, dot_nt(second[x], w_mid[...]), 0.0
        ).astype(BF16)
        first[...] = found
        sum_one[...] += to_row_groups(found.astype(F32))
        g_in[...] += jnp.dot(enc_t[x], first[...], preferred_element_type=F32)
        return carry

    lax.fori_loop(0, NX, in_part, 0)
    in_send[...] = g_in[...].astype(BF16).reshape(NR, 16, HID)
    spread_rays(2, in_send, in_got)
    sums = [
        jnp.sum(part[...], 0, keepdims=True) for part in (sum_one, sum_two, sum_dense, sum_feat)
    ]
    row = jnp.concatenate(sums + [jnp.zeros((1, 128), F32)], 1)
    for index in range(NR):
        turned = pltpu.roll(row, 1280 - PART * index, 1) if index else row
        vec_send[index] = turned[:, :WIDE]
    spread_rays(3, vec_send, vec_got)

    def own_rows(total, count):
        return total[pl.ds(pl.multiple_of(me * count, count), count), :]

    feat_out[...] = gather_rays(0, feat_send, feat_got, own_rows(g_feat, 32))
    mid_out[...] = gather_rays(1, mid_send, mid_got, own_rows(g_mid, 32))
    in_out[...] = gather_rays(2, in_send, in_got, own_rows(g_in, 16))
    vec_out[...] = gather_rays(3, vec_send, vec_got, vec_send[me])


def run_step(*operands):
    def pair(count):
        return pltpu.SemaphoreType.DMA((2, count))

    outs = (((16, 256), F32), ((32, 256), F32), ((32, 384), F32), ((1, WIDE), F32))
    outs += (((NX, 1, RX), F32),)
    scratch = (
        ((2, NX * RX, IN), BF16),
        ((SLOTS, NX * RX), jnp.int32),
        ((1, NX * RX), jnp.int32),
        ((1, NX * RX), jnp.int32),
        ((NX, 1, RX), jnp.int32),
        ((NX * RX, FEAT), BF16),
        ((16, HID), F32),
        ((32, HID), F32),
        ((32, FEAT), F32),
        ((1, PART), F32),
        ((IN, HID), BF16),
        ((HID, HID), BF16),
        ((HID, FEAT), BF16),
        ((NR, 1, WIDE), F32),
        ((NX, ROWS, IN), BF16),
        ((NX, ROWS, HID), BF16),
        ((NX, ROWS, HID), BF16),
        ((NX, IN, ROWS), BF16),
        ((NX, HID, ROWS), BF16),
        ((NX, HID, ROWS), BF16),
        ((NX, ROWS, FEAT), F32),
        ((NX, ROWS, FEAT), F32),
        ((ROWS, FEAT), BF16),
        ((NX, ROWS, HID), F32),
        ((NX, ROWS, HID), BF16),
        ((ROWS, HID), BF16),
        ((NX, SLOTS, RX), F32),
        ((NX, SLOTS, RX), F32),
        ((NX, SLOTS, RX), F32),
        ((NX, SLOTS, RX), F32),
        ((NX, SLOTS, RX), F32),
        ((NX, SLOTS, RX), F32),
        ((HID, RX), BF16),
        ((1, 1280), F32),
        ((IN, HID), F32),
        ((HID, HID), F32),
        ((HID, FEAT), F32),
        ((8, HID), F32),
        ((8, HID), F32),
        ((8, HID), F32),
        ((8, FEAT), F32),
        ((NZ, NX, 1, RX), F32),
        ((NX, 3, 1, RX), F32),
        ((NX, 3, 1, RX), F32),
        ((NX, RX, FEAT), BF16),
        ((NX, RX, FEAT), BF16),
        ((NX, 1, RX), F32),
        ((NX, 1, RX), F32),
        ((NZ, RZ, FEAT), BF16),
        ((NZ, RZ, FEAT), BF16),
        ((NZ, RZ, FEAT), BF16),
        ((NX, RX, FEAT), BF16),
        ((NZ, NX, 1, RX), F32),
        ((NX, 1, RX), F32),
        ((NR, 16, 256), BF16),
        ((NR, 32, 256), BF16),
        ((NR, 32, 384), BF16),
        ((NR, 1, WIDE), F32),
        ((NR, 16, 256), BF16),
        ((NR, 32, 256), BF16),
        ((NR, 32, 384), BF16),
        ((NR, 1, WIDE), F32),
    )
    return pl.pallas_call(
        step_kernel,
        out_shape=tuple(jax.ShapeDtypeStruct(*out) for out in outs),
        in_specs=[pl.BlockSpec(memory_space=pl.ANY)] * len(operands),
        out_specs=tuple(vmem(len(outs))),
        scratch_shapes=[pltpu.VMEM(*part) for part in scratch]
        + [pair(NZ), pair(NX), pair(NX), pair(NX), pair(NZ), pair(NZ), pair(NX), pair(NZ), pair(NX)]
        + [pltpu.SemaphoreType.DMA((2, 4, NR)), pltpu.SemaphoreType.DMA((10,))]
        + [pltpu.SemaphoreType.DMA((2, 4, NR))],
        compiler_params=pltpu.CompilerParams(
            collective_id=0, has_side_effects=True, vmem_limit_bytes=60 * 2**20
        ),
        name="run_step",
    )(*operands)


def adam_kernel(*refs):
    states, grads, after_ref, outs, depth_out = refs[:4], refs[4:8], refs[8], refs[9:13], refs[13]
    for state, grad, out in zip(states, grads, outs):
        gradient = grad[...].reshape((1,) + grad.shape) if len(state.shape) == 4 else grad[...]
        gradient = gradient[..., : state.shape[-1]]
        first_moment = beta_one * state[1] + (1.0 - beta_one) * gradient
        second = beta_two * state[2] + (1.0 - beta_two) * gradient * gradient
        update_step = first_moment / first_fix / (jnp.sqrt(second / second_fix) + epsilon)
        out[0] = state[0] - learn_rate * update_step
        out[1] = first_moment
        out[2] = second
    depth_out[...] = -after_ref[...]


def adam_all(states, grads, after):
    shapes = [jax.ShapeDtypeStruct(state.shape, F32) for state in states]
    shapes.append(jax.ShapeDtypeStruct(after.shape, F32))
    return pl.pallas_call(
        adam_kernel,
        out_shape=tuple(shapes),
        in_specs=vmem(9),
        out_specs=tuple(vmem(5)),
        name="adam_all",
    )(*states, *grads, after)


def per_device(
    ray_codes,
    target,
    direction,
    entries,
    exits,
    depth_bins,
    in_layer,
    mid_layer,
    feat_layer,
    vectors,
):
    *grads, after = run_step(
        ray_codes,
        depth_bins,
        entries,
        exits,
        direction.reshape(NX, 1, RX),
        target,
        in_layer,
        mid_layer,
        feat_layer,
        vectors,
    )
    *states, depth_grad = adam_all((in_layer, mid_layer, feat_layer, vectors), grads, after)
    return (*states, depth_grad.reshape(1, NX * RX))


def solution(mesh):
    placed = (
        P(None, "rays", None),
        P("rays", None),
        P("rays"),
        P("region", "rays"),
        P("region", "rays"),
        P("region", None, "rays"),
        P(None, "region", "rays", None),
        P(None, "region", "rays", None),
        P(None, "region", "rays", None),
        P(None, "region", "rays"),
    )
    return jax.shard_map(
        per_device,
        mesh=mesh,
        in_specs=placed,
        out_specs=(
            P(None, "region", "rays", None),
            P(None, "region", "rays", None),
            P(None, "region", "rays", None),
            P(None, "region", "rays"),
            P("region", "rays"),
        ),
        check_vma=False,
    )
```

```python
import jax
import jax.numpy as jnp
from jax import lax
from jax.experimental import pallas as pl
from jax.experimental.pallas import tpu as pltpu
from jax.sharding import PartitionSpec as P

BINS = 64


depth_scale = 4.0
beta_one = 0.9
beta_two = 0.999
learn_rate = 0.001
epsilon = 1e-08
first_fix = 1.0 - 0.9**10
second_fix = 1.0 - 0.999**10

MESH = pl.DeviceIdType.MESH
NX = 4
NZ = 16
NR = 8
RX = 128
RZ = 8
IN = 128
HID = 256
FEAT = 384
SLOTS = 8
ROWS = SLOTS * RX
PART = 144
WIDE = 256
F32 = jnp.float32
BF16 = jnp.bfloat16


def vmem(count):
    return [pl.BlockSpec(memory_space=pltpu.VMEM)] * count


def remote(source, target, send_sem, recv_sem, peer):
    return pltpu.make_async_remote_copy(
        src_ref=source,
        dst_ref=target,
        send_sem=send_sem,
        recv_sem=recv_sem,
        device_id=peer,
        device_id_type=MESH,
    )


def far_first(count):
    half = count // 2
    order = [half]
    for gap in range(1, half):
        order += [half - gap, half + gap]
    return order


def z_sums(table, own_z):
    column = jnp.zeros((NX, 1, RX), F32)
    lower = jnp.zeros((NX, 1, RX), F32)
    upper = jnp.zeros((NX, 1, RX), F32)
    for z in range(NZ):
        rows = table[:, z]
        column = column + rows
        lower = lower + rows * (z < own_z).astype(F32)
        upper = upper + rows * (z > own_z).astype(F32)
    return column, lower, upper


def far_regions():
    hops = [
        (min(x, NX - x) + min(z, NZ - z), x, z) for x in range(NX) for z in range(NZ) if x + z
    ]
    return [(x, z) for _, x, z in sorted(hops, reverse=True)]


def x_sums(column, lower, upper):
    below, above = [], []
    for x in range(NX):
        under, over = lower[x], upper[x]
        for other in range(NX):
            if other < x:
                under = under + column[other]
            if other > x:
                over = over + column[other]
        below.append(under)
        above.append(over)
    return below, above


def one_less_exp(value):
    series = value * (
        1.0 - value / 2.0 * (1.0 - value / 3.0 * (1.0 - value / 4.0 * (1.0 - value / 5.0)))
    )
    return jnp.where(value < 0.0625, series, 1.0 - jnp.exp(-value))


def sum_before(rows):
    running = jnp.zeros((NX, 1, RX), F32)
    found = []
    for slot in range(SLOTS):
        found.append(running)
        running = running + rows[:, slot : slot + 1]
    return jnp.concatenate(found, 1), running


def sum_after(rows):
    running = jnp.zeros((NX, 1, RX), F32)
    found = []
    for slot in range(SLOTS - 1, -1, -1):
        found.append(running)
        running = running + rows[:, slot : slot + 1]
    return jnp.concatenate(found[::-1], 1)


def to_row_groups(values):
    return jnp.sum(values.reshape(values.shape[0] // 8, 8, values.shape[1]), 0)


def dot_nt(left, right):
    return lax.dot_general(left, right, (((1,), (1,)), ((), ())), preferred_element_type=F32)


def step_kernel(
    codes_hbm,
    bins_hbm,
    entry_hbm,
    exit_hbm,
    onward_hbm,
    target_hbm,
    in_layer,
    mid_layer,
    feat_layer,
    vectors,
    in_out,
    mid_out,
    feat_out,
    vec_out,
    after_out,
    codes_ref,
    bins_ref,
    entry_ref,
    exit_ref,
    onward_ref,
    target_ref,
    in_own,
    mid_own,
    feat_own,
    vec_own,
    w_in,
    w_mid,
    w_feat,
    vec_ref,
    enc,
    h1,
    h2,
    enc_t,
    h1_t,
    h2_t,
    colour,
    coef,
    cgrad,
    hgrad,
    second,
    first,
    raw_rows,
    optical_rows,
    before_rows,
    weight_rows,
    span_rows,
    sample_rows,
    dense_wide,
    vec_row,
    g_in,
    g_mid,
    g_feat,
    sum_dense,
    dense_columns,
    depth_send,
    depth_all,
    partial_send,
    partial_x,
    trans_send,
    trans_all,
    pieces,
    pieces_z,
    grad_z,
    grad_all,
    region_send,
    region_all,
    in_send,
    mid_send,
    feat_send,
    vec_send,
    in_got,
    mid_got,
    feat_got,
    vec_got,
    sem_depth,
    sem_partial,
    sem_trans,
    sem_piece,
    sem_grad_z,
    sem_grad,
    sem_region,
    sem_rays,
    sem_load,
    sem_weight,
):
    place = lax.axis_index("region")
    me = lax.axis_index("rays")
    own_x, own_z = place // NZ, lax.rem(place, NZ)

    def along_x(step):
        return lax.rem(own_x + step, NX)

    def along_z(step):
        return lax.rem(own_z + step, NZ)

    def at(x, z):
        return {"region": x * NZ + z}

    barrier = pltpu.get_barrier_semaphore()
    for far_x, far_z in far_regions():
        pl.semaphore_signal(
            barrier, inc=1, device_id=at(along_x(far_x), along_z(far_z)), device_id_type=MESH
        )
    for step in range(1, NR):
        pl.semaphore_signal(
            barrier, inc=1, device_id={"rays": lax.rem(me + step, NR)}, device_id_type=MESH
        )

    def move_x(step, source, target, sems):
        x = along_x(step)
        return remote(
            source(x), target.at[own_x], sems.at[0, step], sems.at[1, step], at(x, own_z)
        )

    def spread_x(source, target, sems):
        for step in (2, 1, 3):
            move_x(step, source, target, sems).start()

    def wait_x(source, target, sems, steps=(1, 3, 2)):
        for step in steps:
            x = along_x(NX - step)
            remote(source(x), target.at[x], sems.at[0, step], sems.at[1, step], at(x, own_z)).wait()

    def spread_z(source, target, sems):
        for step in far_first(NZ):
            z = along_z(step)
            remote(
                source(z), target.at[own_z], sems.at[0, step], sems.at[1, step], at(own_x, z)
            ).start()

    def wait_z(source, target, sems):
        for step in far_first(NZ)[::-1]:
            z = along_z(NZ - step)
            remote(source(z), target.at[z], sems.at[0, step], sems.at[1, step], at(own_x, z)).wait()

    def spread_all(source, target, sems):
        for far_x, far_z in far_regions():
            x, z = along_x(far_x), along_z(far_z)
            index = far_x * NZ + far_z
            remote(
                source(x), target.at[own_x, own_z], sems.at[0, index], sems.at[1, index], at(x, z)
            ).start()

    def wait_all(source, target, sems):
        for far_x, far_z in far_regions()[::-1]:
            x, z = along_x(NX - far_x), along_z(NZ - far_z)
            index = far_x * NZ + far_z
            remote(
                source(x), target.at[x, z], sems.at[0, index], sems.at[1, index], at(x, z)
            ).wait()

    def spread_rays(kind, source, target):
        for step in range(1, NR):
            peer = lax.rem(me + step, NR)
            remote(
                source.at[peer],
                target.at[step],
                sem_rays.at[0, kind, step],
                sem_rays.at[1, kind, step],
                {"rays": peer},
            ).start()

    def gather_rays(kind, source, target, total):
        for step in range(1, NR):
            origin = lax.rem(me + NR - step, NR)
            remote(
                source.at[origin],
                target.at[step],
                sem_rays.at[0, kind, step],
                sem_rays.at[1, kind, step],
                {"rays": origin},
            ).wait()
            total = total + target[step].astype(F32)
        return total

    loads = [
        pltpu.make_async_copy(source, target, sem_load.at[index])
        for index, (source, target) in enumerate(
            (
                (in_layer.at[0, 0], in_own),
                (mid_layer.at[0, 0], mid_own),
                (feat_layer.at[0, 0], feat_own),
                (vectors.at[0], vec_own),
                (codes_hbm, codes_ref),
                (bins_hbm.at[0], bins_ref),
                (entry_hbm, entry_ref),
                (exit_hbm, exit_ref),
                (onward_hbm, onward_ref),
                (target_hbm, target_ref),
            )
        )
    ]
    for load in loads:
        load.start()

    def mine(array, count, index):
        return array.at[pl.ds(pl.multiple_of(index * count, count), count)]

    weights = (
        lambda index: mine(w_in, 16, index),
        lambda index: mine(w_mid, 32, index),
        lambda index: vec_ref.at[index],
        lambda index: mine(w_feat, 32, index),
    )

    def spread_weights(kind):
        for step in range(1, NR):
            remote(
                weights[kind](me),
                weights[kind](me),
                sem_weight.at[0, kind, step],
                sem_weight.at[1, kind, step],
                {"rays": lax.rem(me + step, NR)},
            ).start()

    def wait_weights(kind):
        for step in range(1, NR):
            origin = lax.rem(me + NR - step, NR)
            remote(
                weights[kind](origin),
                weights[kind](origin),
                sem_weight.at[0, kind, step],
                sem_weight.at[1, kind, step],
                {"rays": origin},
            ).wait()

    unit = depth_scale / (NX * NZ * BINS)
    lane = lax.broadcasted_iota(jnp.int32, (RX, RX), 1)
    slot_row = lax.broadcasted_iota(jnp.int32, (SLOTS, RX), 0)
    for load in loads[:4]:
        load.wait()
    weights[0](me)[...] = in_own[...].astype(BF16)
    weights[1](me)[...] = mid_own[...].astype(BF16)
    weights[3](me)[...] = feat_own[...].astype(BF16)
    vec_ref[me] = jnp.zeros((1, WIDE), F32)
    vec_ref[me, :, pl.ds(0, PART)] = vec_own[...].astype(BF16).astype(F32)
    for load in loads[4:]:
        load.wait()
    for total in (g_in, g_mid, g_feat, sum_dense):
        total[...] = jnp.zeros(total.shape, F32)
    ones = jnp.ones((16, ROWS), BF16)
    for x in range(NX):
        enc_t[x, pl.ds(IN, 16), :] = ones
        h1_t[x, pl.ds(HID, 16), :] = ones
        h2_t[x, pl.ds(HID, 16), :] = ones

    def code_part(x, carry):
        lanes = pl.ds(pl.multiple_of(x * RX, RX), RX)
        bins = bins_ref[:, lanes].astype(F32)
        columns = jnp.transpose((bins + 0.5) / BINS)
        anchor = codes_ref[0, lanes, :].astype(F32)
        heading = codes_ref[1, lanes, :].astype(F32)
        for slot in range(SLOTS):
            enc[x, pl.ds(slot * RX, RX), :] = (
                anchor + columns[:, slot : slot + 1] * heading
            ).astype(BF16)
        following = jnp.concatenate([bins[1:], jnp.full((1, RX), float(BINS), F32)], 0)
        inside = (slot_row >= entry_ref[:, lanes]) & (slot_row < exit_ref[:, lanes])
        span_rows[x] = jnp.where(inside, (following - bins) * unit, 0.0)
        return carry

    lax.fori_loop(0, NX, code_part, 0)
    pl.semaphore_wait(barrier, NX * NZ + NR - 2)
    for kind in range(4):
        spread_weights(kind)

    def turn_code(x, carry):
        enc_t[x, pl.ds(0, IN), :] = jnp.transpose(enc[x])
        return carry

    lax.fori_loop(0, NX, turn_code, 0)
    for kind in range(3):
        wait_weights(kind)
    row = jnp.zeros((1, 1280), F32)
    tail = jnp.zeros((1, 1280 - WIDE), F32)
    for index in range(NR):
        wide = jnp.concatenate([vec_ref[index], tail], 1)
        row = row + (pltpu.roll(wide, PART * index, 1) if index else wide)
    vec_row[...] = row
    dense_wide[...] = jnp.transpose(
        jnp.broadcast_to(row[:, 2 * HID : 3 * HID], (RX, HID))
    ).astype(BF16)

    def hidden_part(index, carry):
        x = along_x(index + 1)
        h1[x] = jnp.maximum(
            jnp.dot(enc[x], w_in[...], preferred_element_type=F32) + vec_row[:, :HID], 0.0
        ).astype(BF16)
        h2[x] = jnp.maximum(
            jnp.dot(h1[x], w_mid[...], preferred_element_type=F32) + vec_row[:, HID : 2 * HID],
            0.0,
        ).astype(BF16)
        dense = jnp.dot(h2[x], dense_wide[...], preferred_element_type=F32)
        grid = jnp.zeros((RX, RX), F32)
        for slot in range(SLOTS):
            grid = jnp.where(lane == slot, dense[slot * RX : (slot + 1) * RX], grid)
        raw_rows[x] = jnp.transpose(grid)[:SLOTS]
        return carry

    lax.fori_loop(0, NX, hidden_part, 0)
    raw = raw_rows[...]
    soft = jnp.maximum(raw, 0.0) + jnp.log1p(jnp.exp(-jnp.abs(raw)))
    optical = soft * span_rows[...]
    before, total = sum_before(optical)
    depth_send[...] = total
    spread_all(lambda x: depth_send.at[x], depth_all, sem_depth)
    depth_all[own_x, own_z] = depth_send[own_x]
    optical_rows[...] = optical
    before_rows[...] = before
    weight_rows[...] = jnp.exp(-before) * one_less_exp(optical)
    wait_weights(3)

    def colour_part(index, carry):
        x = along_x(index + 1)
        colour[x] = jax.nn.sigmoid(
            jnp.dot(h2[x], w_feat[...], preferred_element_type=F32)
            + vec_row[:, 3 * HID : 3 * HID + FEAT]
        )
        columns = jnp.transpose(weight_rows[x])
        local = jnp.zeros((RX, FEAT), F32)
        for slot in range(SLOTS):
            local = local + columns[:, slot : slot + 1] * colour[x, pl.ds(slot * RX, RX), :]
        partial_send[x] = local.astype(BF16)

        @pl.when(index < NX - 1)
        def _():
            move_x(index + 1, lambda x: partial_send.at[x], partial_x, sem_partial).start()

        return carry

    lax.fori_loop(0, NX, colour_part, 0)
    partial_x[own_x] = partial_send[own_x]
    wait_all(lambda x: depth_send.at[x], depth_all, sem_depth)
    below, above = x_sums(*z_sums(depth_all, own_z))
    onward = onward_ref[own_x] == 0
    trans = [jnp.exp(-jnp.where(onward, below[x], above[x])) for x in range(NX)]
    for x in range(NX):
        trans_send[x] = trans[x]
    trans_all[own_x] = trans_send[own_x]
    spread_x(lambda x: trans_send.at[x], trans_all, sem_trans)
    columns = jnp.transpose(jnp.concatenate(trans + trans, 0))
    wait_x(lambda x: partial_send.at[x], partial_x, sem_partial)
    total = jnp.zeros((RX, FEAT), F32)
    for x in range(NX):
        total = total + columns[:, x : x + 1] * partial_x[x].astype(F32)
    pieces[...] = total.reshape(NZ, RZ, FEAT).astype(BF16)
    spread_z(lambda z: pieces.at[z], pieces_z, sem_piece)
    pieces_z[own_z] = pieces[own_z]

    def turn_part(x, carry):
        h1_t[x, pl.ds(0, HID), :] = jnp.transpose(h1[x])
        h2_t[x, pl.ds(0, HID), :] = jnp.transpose(h2[x])
        return carry

    lax.fori_loop(0, NX, turn_part, 0)
    start = pl.multiple_of(own_x * RX + (own_z // 2) * (2 * RZ), 2 * RZ)
    wanted = target_ref[pl.ds(start, 2 * RZ), :].astype(F32)
    odd = lax.rem(own_z, 2).astype(F32)
    wanted = wanted[:RZ] * (1.0 - odd) + wanted[RZ:] * odd
    wait_z(lambda z: pieces.at[z], pieces_z, sem_piece)
    rendered = jnp.sum(pieces_z[...].astype(F32), 0)
    grad_z[own_z] = (rendered - wanted).astype(BF16)
    spread_z(lambda z: grad_z.at[own_z], grad_z, sem_grad_z)
    wait_x(lambda x: trans_send.at[x], trans_all, sem_trans)

    def coef_part(x, carry):
        columns = jnp.transpose(trans_all[x] * weight_rows[x])
        for slot in range(SLOTS):
            rows = pl.ds(slot * RX, RX)
            shade = colour[x, rows, :]
            coef[x, rows, :] = columns[:, slot : slot + 1] * (shade * (1.0 - shade))
        return carry

    lax.fori_loop(0, NX, coef_part, 0)
    wait_z(lambda z: grad_z.at[own_z], grad_z, sem_grad_z)
    grad_float = grad_z[...].astype(F32).reshape(RX, FEAT)
    grad_all[own_x] = grad_float.astype(BF16)
    spread_x(lambda x: grad_all.at[own_x], grad_all, sem_grad)
    grid = jnp.zeros((RX, RX), F32)
    for x in range(NX):
        dots = jnp.sum(grad_float * partial_x[x].astype(F32), -1, keepdims=True)
        grid = jnp.where(lane == x, dots, grid)
    grid = jnp.transpose(grid)
    for x in range(NX):
        region_send[x] = grid[x : x + 1] * trans_send[x]
    spread_all(lambda x: region_send, region_all, sem_region)
    region_all[own_x, own_z] = region_send[...]

    def feat_part(index, carry):
        x = along_x(index)

        @pl.when(index > 0)
        def _():
            wait_x(lambda x: grad_all.at[own_x], grad_all, sem_grad, (NX - index,))

        grads = grad_all[x].astype(F32)
        grid = jnp.zeros((RX, RX), F32)
        for slot in range(SLOTS):
            rows = pl.ds(slot * RX, RX)
            shade = colour[x, rows, :]
            grid = jnp.where(lane == slot, jnp.sum(shade * grads, -1, keepdims=True), grid)
            cgrad[rows, :] = (coef[x, rows, :] * grads).astype(BF16)
        sample_rows[x] = jnp.transpose(grid)[:SLOTS]
        g_feat[...] += jnp.dot(h2_t[x], cgrad[...], preferred_element_type=F32)
        hgrad[x] = dot_nt(cgrad[...], w_feat[...])
        return carry

    lax.fori_loop(0, NX, feat_part, 0)
    feat_send[...] = g_feat[pl.ds(0, HID), :].astype(BF16).reshape(NR, 32, FEAT)
    spread_rays(0, feat_send, feat_got)
    samples = sample_rows[...]
    later = sum_after(weight_rows[...] * samples)
    local_grad = trans_all[...] * (
        jnp.exp(-(before_rows[...] + optical_rows[...])) * samples - later
    )
    dense_scale = span_rows[...] * jax.nn.sigmoid(raw_rows[...])
    wait_all(lambda x: region_send, region_all, sem_region)
    above = jnp.zeros((NX, 1, RX), F32)
    below = jnp.zeros((NX, 1, RX), F32)
    for x in range(NX):
        for z in range(NZ):
            rows = region_all[:, z, x]
            above = above + rows * (x * NZ + z > place).astype(F32)
            below = below + rows * (x * NZ + z < place).astype(F32)
    after = jnp.where(onward_ref[...] == 0, above, below)
    after_out[...] = after
    dense_grad = ((local_grad - after) * dense_scale).astype(BF16).astype(F32)
    for x in range(NX):
        dense_columns[x] = jnp.transpose(dense_grad[x])

    def mid_part(x, carry):
        columns = dense_columns[x]
        dense_row = vec_row[:, 2 * HID : 3 * HID]
        dense_added = jnp.zeros((8, HID), F32)
        for slot in range(SLOTS):
            rows = pl.ds(slot * RX, RX)
            hidden = h2[x, rows, :].astype(F32)
            scale = columns[:, slot : slot + 1]
            found = jnp.where(hidden > 0.0, hgrad[x, rows, :] + scale * dense_row, 0.0)
            second[x, rows, :] = found.astype(BF16)
            dense_added = dense_added + to_row_groups(scale * hidden)
        sum_dense[...] += dense_added
        g_mid[...] += jnp.dot(h1_t[x], second[x], preferred_element_type=F32)
        return carry

    lax.fori_loop(0, NX, mid_part, 0)
    mid_send[...] = g_mid[pl.ds(0, HID), :].astype(BF16).reshape(NR, 32, HID)
    spread_rays(1, mid_send, mid_got)

    def in_part(x, carry):
        first[...] = jnp.where(
            h1[x].astype(F32) > 0.0, dot_nt(second[x], w_mid[...]), 0.0
        ).astype(BF16)
        g_in[...] += jnp.dot(enc_t[x], first[...], preferred_element_type=F32)
        return carry

    lax.fori_loop(0, NX, in_part, 0)
    in_send[...] = g_in[pl.ds(0, IN), :].astype(BF16).reshape(NR, 16, HID)
    spread_rays(2, in_send, in_got)
    sums = [
        g_in[pl.ds(IN, 8), :][:1],
        g_mid[pl.ds(HID, 8), :][:1],
        jnp.sum(sum_dense[...], 0, keepdims=True),
        g_feat[pl.ds(HID, 8), :][:1],
    ]
    row = jnp.concatenate(sums + [jnp.zeros((1, 128), F32)], 1)
    for index in range(NR):
        turned = pltpu.roll(row, 1280 - PART * index, 1) if index else row
        vec_send[index] = turned[:, :WIDE]
    spread_rays(3, vec_send, vec_got)

    def own_rows(total, count):
        return total[pl.ds(pl.multiple_of(me * count, count), count), :]

    feat_out[...] = gather_rays(0, feat_send, feat_got, own_rows(g_feat, 32))
    mid_out[...] = gather_rays(1, mid_send, mid_got, own_rows(g_mid, 32))
    in_out[...] = gather_rays(2, in_send, in_got, own_rows(g_in, 16))
    vec_out[...] = gather_rays(3, vec_send, vec_got, vec_send[me])


def run_step(*operands):
    def pair(count):
        return pltpu.SemaphoreType.DMA((2, count))

    outs = (((16, 256), F32), ((32, 256), F32), ((32, 384), F32), ((1, WIDE), F32))
    outs += (((NX, 1, RX), F32),)
    scratch = (
        ((2, NX * RX, IN), BF16),
        ((SLOTS, NX * RX), jnp.int32),
        ((1, NX * RX), jnp.int32),
        ((1, NX * RX), jnp.int32),
        ((NX, 1, RX), jnp.int32),
        ((NX * RX, FEAT), BF16),
        ((16, HID), F32),
        ((32, HID), F32),
        ((32, FEAT), F32),
        ((1, PART), F32),
        ((IN, HID), BF16),
        ((HID, HID), BF16),
        ((HID, FEAT), BF16),
        ((NR, 1, WIDE), F32),
        ((NX, ROWS, IN), BF16),
        ((NX, ROWS, HID), BF16),
        ((NX, ROWS, HID), BF16),
        ((NX, IN + 16, ROWS), BF16),
        ((NX, HID + 16, ROWS), BF16),
        ((NX, HID + 16, ROWS), BF16),
        ((NX, ROWS, FEAT), F32),
        ((NX, ROWS, FEAT), F32),
        ((ROWS, FEAT), BF16),
        ((NX, ROWS, HID), F32),
        ((NX, ROWS, HID), BF16),
        ((ROWS, HID), BF16),
        ((NX, SLOTS, RX), F32),
        ((NX, SLOTS, RX), F32),
        ((NX, SLOTS, RX), F32),
        ((NX, SLOTS, RX), F32),
        ((NX, SLOTS, RX), F32),
        ((NX, SLOTS, RX), F32),
        ((HID, RX), BF16),
        ((1, 1280), F32),
        ((IN + 16, HID), F32),
        ((HID + 16, HID), F32),
        ((HID + 16, FEAT), F32),
        ((8, HID), F32),
        ((NX, RX, SLOTS), F32),
        ((NX, 1, RX), F32),
        ((NX, NZ, 1, RX), F32),
        ((NX, RX, FEAT), BF16),
        ((NX, RX, FEAT), BF16),
        ((NX, 1, RX), F32),
        ((NX, 1, RX), F32),
        ((NZ, RZ, FEAT), BF16),
        ((NZ, RZ, FEAT), BF16),
        ((NZ, RZ, FEAT), BF16),
        ((NX, RX, FEAT), BF16),
        ((NX, 1, RX), F32),
        ((NX, NZ, NX, 1, RX), F32),
        ((NR, 16, 256), BF16),
        ((NR, 32, 256), BF16),
        ((NR, 32, 384), BF16),
        ((NR, 1, WIDE), F32),
        ((NR, 16, 256), BF16),
        ((NR, 32, 256), BF16),
        ((NR, 32, 384), BF16),
        ((NR, 1, WIDE), F32),
    )
    return pl.pallas_call(
        step_kernel,
        out_shape=tuple(jax.ShapeDtypeStruct(*out) for out in outs),
        in_specs=[pl.BlockSpec(memory_space=pl.ANY)] * len(operands),
        out_specs=tuple(vmem(len(outs))),
        scratch_shapes=[pltpu.VMEM(*part) for part in scratch]
        + [pair(NX * NZ), pair(NX), pair(NX), pair(NZ), pair(NZ), pair(NX), pair(NX * NZ)]
        + [pltpu.SemaphoreType.DMA((2, 4, NR)), pltpu.SemaphoreType.DMA((10,))]
        + [pltpu.SemaphoreType.DMA((2, 4, NR))],
        compiler_params=pltpu.CompilerParams(
            collective_id=0, has_side_effects=True, vmem_limit_bytes=60 * 2**20
        ),
        name="run_step",
    )(*operands)


def adam_kernel(*refs):
    states, grads, after_ref, outs, depth_out = refs[:4], refs[4:8], refs[8], refs[9:13], refs[13]
    for state, grad, out in zip(states, grads, outs):
        gradient = grad[...].reshape((1,) + grad.shape) if len(state.shape) == 4 else grad[...]
        gradient = gradient[..., : state.shape[-1]]
        first_moment = beta_one * state[1] + (1.0 - beta_one) * gradient
        second = beta_two * state[2] + (1.0 - beta_two) * gradient * gradient
        update_step = first_moment / first_fix / (jnp.sqrt(second / second_fix) + epsilon)
        out[0] = state[0] - learn_rate * update_step
        out[1] = first_moment
        out[2] = second
    depth_out[...] = -after_ref[...]


def adam_all(states, grads, after):
    shapes = [jax.ShapeDtypeStruct(state.shape, F32) for state in states]
    shapes.append(jax.ShapeDtypeStruct(after.shape, F32))
    return pl.pallas_call(
        adam_kernel,
        out_shape=tuple(shapes),
        in_specs=vmem(9),
        out_specs=tuple(vmem(5)),
        name="adam_all",
    )(*states, *grads, after)


def per_device(
    ray_codes,
    target,
    direction,
    entries,
    exits,
    depth_bins,
    in_layer,
    mid_layer,
    feat_layer,
    vectors,
):
    *grads, after = run_step(
        ray_codes,
        depth_bins,
        entries,
        exits,
        direction.reshape(NX, 1, RX),
        target,
        in_layer,
        mid_layer,
        feat_layer,
        vectors,
    )
    *states, depth_grad = adam_all((in_layer, mid_layer, feat_layer, vectors), grads, after)
    return (*states, depth_grad.reshape(1, NX * RX))


def solution(mesh):
    placed = (
        P(None, "rays", None),
        P("rays", None),
        P("rays"),
        P("region", "rays"),
        P("region", "rays"),
        P("region", None, "rays"),
        P(None, "region", "rays", None),
        P(None, "region", "rays", None),
        P(None, "region", "rays", None),
        P(None, "region", "rays"),
    )
    return jax.shard_map(
        per_device,
        mesh=mesh,
        in_specs=placed,
        out_specs=(
            P(None, "region", "rays", None),
            P(None, "region", "rays", None),
            P(None, "region", "rays", None),
            P(None, "region", "rays"),
            P("region", "rays"),
        ),
        check_vma=False,
    )
```

```python
import jax
import jax.numpy as jnp
from jax import lax
from jax.experimental import pallas as pl
from jax.experimental.pallas import tpu as pltpu
from jax.sharding import PartitionSpec as P

BINS = 64


depth_scale = 4.0
beta_one = 0.9
beta_two = 0.999
learn_rate = 0.001
epsilon = 1e-08
first_fix = 1.0 - 0.9**10
second_fix = 1.0 - 0.999**10

MESH = pl.DeviceIdType.MESH
NX = 4
NZ = 16
NR = 8
RX = 128
RZ = 8
IN = 128
HID = 256
FEAT = 384
SLOTS = 8
ROWS = SLOTS * RX
PART = 144
WIDE = 256
F32 = jnp.float32
BF16 = jnp.bfloat16


def vmem(count):
    return [pl.BlockSpec(memory_space=pltpu.VMEM)] * count


def remote(source, target, send_sem, recv_sem, peer):
    return pltpu.make_async_remote_copy(
        src_ref=source,
        dst_ref=target,
        send_sem=send_sem,
        recv_sem=recv_sem,
        device_id=peer,
        device_id_type=MESH,
    )


def far_first(count):
    half = count // 2
    order = [half]
    for gap in range(1, half):
        order += [half - gap, half + gap]
    return order


def z_sums(table, own_z):
    column = [jnp.zeros((1, RX), F32) for _ in range(NX)]
    lower, upper = list(column), list(column)
    for z in range(NZ):
        under, over = (z < own_z).astype(F32), (z > own_z).astype(F32)
        for x in range(NX):
            rows = table[x * NZ + z]
            column[x] = column[x] + rows
            lower[x] = lower[x] + rows * under
            upper[x] = upper[x] + rows * over
    return column, lower, upper


def far_regions():
    hops = [
        (min(x, NX - x) + min(z, NZ - z), x, z) for x in range(NX) for z in range(NZ) if x + z
    ]
    return [(x, z) for _, x, z in sorted(hops, reverse=True)]


def x_sums(column, lower, upper):
    below, above = [], []
    for x in range(NX):
        under, over = lower[x], upper[x]
        for other in range(NX):
            if other < x:
                under = under + column[other]
            if other > x:
                over = over + column[other]
        below.append(under)
        above.append(over)
    return below, above


def one_less_exp(value):
    series = value * (
        1.0 - value / 2.0 * (1.0 - value / 3.0 * (1.0 - value / 4.0 * (1.0 - value / 5.0)))
    )
    return jnp.where(value < 0.0625, series, 1.0 - jnp.exp(-value))


def sum_before(rows):
    running = jnp.zeros((NX, 1, RX), F32)
    found = []
    for slot in range(SLOTS):
        found.append(running)
        running = running + rows[:, slot : slot + 1]
    return jnp.concatenate(found, 1), running


def sum_after(rows):
    running = jnp.zeros((NX, 1, RX), F32)
    found = []
    for slot in range(SLOTS - 1, -1, -1):
        found.append(running)
        running = running + rows[:, slot : slot + 1]
    return jnp.concatenate(found[::-1], 1)


def to_row_groups(values):
    return jnp.sum(values.reshape(values.shape[0] // 8, 8, values.shape[1]), 0)


def dot_nt(left, right):
    return lax.dot_general(left, right, (((1,), (1,)), ((), ())), preferred_element_type=F32)


def step_kernel(
    codes_hbm,
    bins_hbm,
    entry_hbm,
    exit_hbm,
    onward_hbm,
    target_hbm,
    in_layer,
    mid_layer,
    feat_layer,
    vectors,
    in_out,
    mid_out,
    feat_out,
    vec_out,
    after_out,
    codes_ref,
    bins_ref,
    entry_ref,
    exit_ref,
    onward_ref,
    target_ref,
    in_own,
    mid_own,
    feat_own,
    vec_own,
    w_in,
    w_mid,
    w_feat,
    vec_ref,
    enc,
    h1,
    h2,
    enc_t,
    h1_t,
    h2_t,
    colour,
    coef,
    cgrad,
    hgrad,
    second,
    first,
    raw_rows,
    optical_rows,
    before_rows,
    weight_rows,
    span_rows,
    sample_rows,
    dense_wide,
    vec_row,
    g_in,
    g_mid,
    g_feat,
    sum_dense,
    dense_columns,
    depth_send,
    depth_all,
    partial_send,
    partial_x,
    trans_send,
    trans_all,
    pieces,
    pieces_z,
    grad_z,
    grad_all,
    region_send,
    region_all,
    in_send,
    mid_send,
    feat_send,
    vec_send,
    in_got,
    mid_got,
    feat_got,
    vec_got,
    sem_depth,
    sem_partial,
    sem_trans,
    sem_piece,
    sem_grad_z,
    sem_grad,
    sem_region,
    sem_rays,
    sem_load,
    sem_weight,
):
    place = lax.axis_index("region")
    me = lax.axis_index("rays")
    own_x, own_z = place // NZ, lax.rem(place, NZ)

    def along_x(step):
        return lax.rem(own_x + step, NX)

    def along_z(step):
        return lax.rem(own_z + step, NZ)

    def at(x, z):
        return {"region": x * NZ + z}

    barrier = pltpu.get_barrier_semaphore()
    for far_x, far_z in far_regions():
        pl.semaphore_signal(
            barrier, inc=1, device_id=at(along_x(far_x), along_z(far_z)), device_id_type=MESH
        )
    for step in range(1, NR):
        pl.semaphore_signal(
            barrier, inc=1, device_id={"rays": lax.rem(me + step, NR)}, device_id_type=MESH
        )

    def arrived(sent, got, count, sems, peer):
        first = pl.ds(0, count)
        remote(sent.at[first], got.at[first], sems.at[0], sems.at[1], peer).wait()

    def spread_x(source, target, sems):
        for step in (2, 1, 3):
            x = along_x(step)
            remote(source(x), target.at[own_x], sems.at[0], sems.at[1], at(x, own_z)).start()

    def wait_x(sent, got, sems):
        arrived(sent, got, NX - 1, sems, at(along_x(1), own_z))

    def spread_z(source, target, sems):
        for step in far_first(NZ):
            z = along_z(step)
            remote(source(z), target.at[own_z], sems.at[0], sems.at[1], at(own_x, z)).start()

    def wait_z(sent, got, sems):
        arrived(sent, got, NZ - 1, sems, at(own_x, along_z(1)))

    def spread_all(source, target, sems):
        for far_x, far_z in far_regions():
            x, z = along_x(far_x), along_z(far_z)
            remote(source(x), target.at[place], sems.at[0], sems.at[1], at(x, z)).start()

    def wait_all(table, sems):
        arrived(table, table, NX * NZ - 1, sems, at(along_x(1), own_z))

    def spread_rays(kind, source, target):
        for step in range(1, NR):
            peer = lax.rem(me + step, NR)
            remote(
                source.at[peer],
                target.at[me],
                sem_rays.at[0, kind],
                sem_rays.at[1, kind],
                {"rays": peer},
            ).start()
        target[me] = jnp.zeros(target.shape[1:], target.dtype)

    def gather_rays(kind, source, target, total):
        first = pl.ds(0, NR - 1)
        remote(
            source.at[first],
            target.at[first],
            sem_rays.at[0, kind],
            sem_rays.at[1, kind],
            {"rays": lax.rem(me + 1, NR)},
        ).wait()
        return total + jnp.sum(target[...].astype(F32), 0)

    loads = [
        pltpu.make_async_copy(source, target, sem_load.at[index])
        for index, (source, target) in enumerate(
            (
                (in_layer.at[0, 0], in_own),
                (mid_layer.at[0, 0], mid_own),
                (feat_layer.at[0, 0], feat_own),
                (vectors.at[0], vec_own),
                (codes_hbm, codes_ref),
                (bins_hbm.at[0], bins_ref),
                (entry_hbm, entry_ref),
                (exit_hbm, exit_ref),
                (onward_hbm, onward_ref),
                (target_hbm, target_ref),
            )
        )
    ]
    for load in loads:
        load.start()

    def mine(array, count, index):
        return array.at[pl.ds(pl.multiple_of(index * count, count), count)]

    weights = (
        lambda index: mine(w_in, 16, index),
        lambda index: mine(w_mid, 32, index),
        lambda index: vec_ref.at[index],
        lambda index: mine(w_feat, 32, index),
    )

    def spread_weights(kind):
        for step in range(1, NR):
            remote(
                weights[kind](me),
                weights[kind](me),
                sem_weight.at[0, kind],
                sem_weight.at[1, kind],
                {"rays": lax.rem(me + step, NR)},
            ).start()

    def wait_weights(kind):
        array, count = ((w_in, 16), (w_mid, 32), (vec_ref, 1), (w_feat, 32))[kind]
        first = array.at[pl.ds(0, count * (NR - 1))]
        remote(
            first,
            first,
            sem_weight.at[0, kind],
            sem_weight.at[1, kind],
            {"rays": lax.rem(me + 1, NR)},
        ).wait()

    unit = depth_scale / (NX * NZ * BINS)
    lane = lax.broadcasted_iota(jnp.int32, (RX, RX), 1)
    slot_row = lax.broadcasted_iota(jnp.int32, (SLOTS, RX), 0)
    for load in loads[:4]:
        load.wait()
    weights[0](me)[...] = in_own[...].astype(BF16)
    weights[1](me)[...] = mid_own[...].astype(BF16)
    weights[3](me)[...] = feat_own[...].astype(BF16)
    vec_ref[me] = jnp.zeros((1, WIDE), F32)
    vec_ref[me, :, pl.ds(0, PART)] = vec_own[...].astype(BF16).astype(F32)
    for load in loads[4:]:
        load.wait()
    for total in (g_in, g_mid, g_feat, sum_dense):
        total[...] = jnp.zeros(total.shape, F32)
    ones = jnp.ones((16, ROWS), BF16)
    for x in range(NX):
        enc_t[x, pl.ds(IN, 16), :] = ones
        h1_t[x, pl.ds(HID, 16), :] = ones
        h2_t[x, pl.ds(HID, 16), :] = ones

    def code_part(x, carry):
        lanes = pl.ds(pl.multiple_of(x * RX, RX), RX)
        bins = bins_ref[:, lanes].astype(F32)
        columns = jnp.transpose((bins + 0.5) / BINS)
        anchor = codes_ref[0, lanes, :].astype(F32)
        heading = codes_ref[1, lanes, :].astype(F32)
        for slot in range(SLOTS):
            enc[x, pl.ds(slot * RX, RX), :] = (
                anchor + columns[:, slot : slot + 1] * heading
            ).astype(BF16)
        following = jnp.concatenate([bins[1:], jnp.full((1, RX), float(BINS), F32)], 0)
        inside = (slot_row >= entry_ref[:, lanes]) & (slot_row < exit_ref[:, lanes])
        span_rows[x] = jnp.where(inside, (following - bins) * unit, 0.0)
        return carry

    lax.fori_loop(0, NX, code_part, 0)
    pl.semaphore_wait(barrier, NX * NZ + NR - 2)
    for kind in range(4):
        spread_weights(kind)

    def turn_code(x, carry):
        enc_t[x, pl.ds(0, IN), :] = jnp.transpose(enc[x])
        return carry

    lax.fori_loop(0, NX, turn_code, 0)
    for kind in range(3):
        wait_weights(kind)
    row = jnp.zeros((1, 1280), F32)
    tail = jnp.zeros((1, 1280 - WIDE), F32)
    for index in range(NR):
        wide = jnp.concatenate([vec_ref[index], tail], 1)
        row = row + (pltpu.roll(wide, PART * index, 1) if index else wide)
    vec_row[...] = row
    dense_wide[...] = jnp.transpose(
        jnp.broadcast_to(row[:, 2 * HID : 3 * HID], (RX, HID))
    ).astype(BF16)

    def hidden_part(index, carry):
        x = along_x(index + 1)
        h1[x] = jnp.maximum(
            jnp.dot(enc[x], w_in[...], preferred_element_type=F32) + vec_row[:, :HID], 0.0
        ).astype(BF16)
        h2[x] = jnp.maximum(
            jnp.dot(h1[x], w_mid[...], preferred_element_type=F32) + vec_row[:, HID : 2 * HID],
            0.0,
        ).astype(BF16)
        dense = jnp.dot(h2[x], dense_wide[...], preferred_element_type=F32)
        grid = jnp.zeros((RX, RX), F32)
        for slot in range(SLOTS):
            grid = jnp.where(lane == slot, dense[slot * RX : (slot + 1) * RX], grid)
        raw_rows[x] = jnp.transpose(grid)[:SLOTS]
        return carry

    lax.fori_loop(0, NX, hidden_part, 0)
    raw = raw_rows[...]
    soft = jnp.maximum(raw, 0.0) + jnp.log1p(jnp.exp(-jnp.abs(raw)))
    optical = soft * span_rows[...]
    before, total = sum_before(optical)
    depth_send[...] = total
    spread_all(lambda x: depth_send.at[x], depth_all, sem_depth)
    depth_all[place] = depth_send[own_x]
    optical_rows[...] = optical
    before_rows[...] = before
    weight_rows[...] = jnp.exp(-before) * one_less_exp(optical)
    wait_weights(3)

    def colour_part(index, carry):
        x = along_x(index + 1)
        colour[x] = jax.nn.sigmoid(
            jnp.dot(h2[x], w_feat[...], preferred_element_type=F32)
            + vec_row[:, 3 * HID : 3 * HID + FEAT]
        )
        columns = jnp.transpose(weight_rows[x])
        local = jnp.zeros((RX, FEAT), F32)
        for slot in range(SLOTS):
            local = local + columns[:, slot : slot + 1] * colour[x, pl.ds(slot * RX, RX), :]
        partial_send[x] = local.astype(BF16)

        @pl.when(index < NX - 1)
        def _():
            remote(
                partial_send.at[x],
                partial_x.at[own_x],
                sem_partial.at[0],
                sem_partial.at[1],
                at(x, own_z),
            ).start()

        return carry

    lax.fori_loop(0, NX, colour_part, 0)
    partial_x[own_x] = partial_send[own_x]
    wait_all(depth_all, sem_depth)
    below, above = x_sums(*z_sums(depth_all, own_z))
    onward = onward_ref[own_x] == 0
    trans = [jnp.exp(-jnp.where(onward, below[x], above[x])) for x in range(NX)]
    for x in range(NX):
        trans_send[x] = trans[x]
    trans_all[own_x] = trans_send[own_x]
    spread_x(lambda x: trans_send.at[x], trans_all, sem_trans)
    columns = jnp.transpose(jnp.concatenate(trans + trans, 0))
    wait_x(partial_send, partial_x, sem_partial)
    total = jnp.zeros((RX, FEAT), F32)
    for x in range(NX):
        total = total + columns[:, x : x + 1] * partial_x[x].astype(F32)
    pieces[...] = total.reshape(NZ, RZ, FEAT).astype(BF16)
    spread_z(lambda z: pieces.at[z], pieces_z, sem_piece)
    pieces_z[own_z] = pieces[own_z]

    def turn_part(x, carry):
        h1_t[x, pl.ds(0, HID), :] = jnp.transpose(h1[x])
        h2_t[x, pl.ds(0, HID), :] = jnp.transpose(h2[x])
        return carry

    lax.fori_loop(0, NX, turn_part, 0)
    start = pl.multiple_of(own_x * RX + (own_z // 2) * (2 * RZ), 2 * RZ)
    wanted = target_ref[pl.ds(start, 2 * RZ), :].astype(F32)
    odd = lax.rem(own_z, 2).astype(F32)
    wanted = wanted[:RZ] * (1.0 - odd) + wanted[RZ:] * odd
    wait_z(pieces, pieces_z, sem_piece)
    rendered = jnp.sum(pieces_z[...].astype(F32), 0)
    grad_z[own_z] = (rendered - wanted).astype(BF16)
    spread_z(lambda z: grad_z.at[own_z], grad_z, sem_grad_z)
    wait_x(trans_send, trans_all, sem_trans)

    def coef_part(x, carry):
        columns = jnp.transpose(trans_all[x] * weight_rows[x])
        for slot in range(SLOTS):
            rows = pl.ds(slot * RX, RX)
            shade = colour[x, rows, :]
            coef[x, rows, :] = columns[:, slot : slot + 1] * (shade * (1.0 - shade))
        return carry

    lax.fori_loop(0, NX, coef_part, 0)
    wait_z(grad_z, grad_z, sem_grad_z)
    grad_float = grad_z[...].astype(F32).reshape(RX, FEAT)
    grad_all[own_x] = grad_float.astype(BF16)
    for step in (2, 1, 3):
        remote(
            grad_all.at[own_x],
            grad_all.at[own_x],
            sem_grad.at[0, step],
            sem_grad.at[1, step],
            at(along_x(step), own_z),
        ).start()
    grid = jnp.zeros((RX, RX), F32)
    for x in range(NX):
        dots = jnp.sum(grad_float * partial_x[x].astype(F32), -1, keepdims=True)
        grid = jnp.where(lane == x, dots, grid)
    grid = jnp.transpose(grid)
    for x in range(NX):
        region_send[x] = grid[x : x + 1] * trans_send[x]
    spread_all(lambda x: region_send, region_all, sem_region)
    region_all[place] = region_send[...]

    def feat_part(index, carry):
        x = along_x(index)

        @pl.when(index > 0)
        def _():
            step = NX - index
            remote(
                grad_all.at[own_x],
                grad_all.at[x],
                sem_grad.at[0, step],
                sem_grad.at[1, step],
                at(x, own_z),
            ).wait()

        grads = grad_all[x].astype(F32)
        grid = jnp.zeros((RX, RX), F32)
        for slot in range(SLOTS):
            rows = pl.ds(slot * RX, RX)
            shade = colour[x, rows, :]
            grid = jnp.where(lane == slot, jnp.sum(shade * grads, -1, keepdims=True), grid)
            cgrad[rows, :] = (coef[x, rows, :] * grads).astype(BF16)
        sample_rows[x] = jnp.transpose(grid)[:SLOTS]
        g_feat[...] += jnp.dot(h2_t[x], cgrad[...], preferred_element_type=F32)
        hgrad[x] = dot_nt(cgrad[...], w_feat[...])
        return carry

    lax.fori_loop(0, NX, feat_part, 0)
    feat_send[...] = g_feat[pl.ds(0, HID), :].astype(BF16).reshape(NR, 32, FEAT)
    spread_rays(0, feat_send, feat_got)
    samples = sample_rows[...]
    later = sum_after(weight_rows[...] * samples)
    local_grad = trans_all[...] * (
        jnp.exp(-(before_rows[...] + optical_rows[...])) * samples - later
    )
    dense_scale = span_rows[...] * jax.nn.sigmoid(raw_rows[...])
    wait_all(region_all, sem_region)
    above = [jnp.zeros((1, RX), F32) for _ in range(NX)]
    below = list(above)
    for x in range(NX):
        for z in range(NZ):
            over = (x * NZ + z > place).astype(F32)
            under = (x * NZ + z < place).astype(F32)
            for quarter in range(NX):
                rows = region_all[quarter * NZ + z, x]
                above[quarter] = above[quarter] + rows * over
                below[quarter] = below[quarter] + rows * under
    above = jnp.stack(above)
    below = jnp.stack(below)
    after = jnp.where(onward_ref[...] == 0, above, below)
    after_out[...] = after
    dense_grad = ((local_grad - after) * dense_scale).astype(BF16).astype(F32)
    for x in range(NX):
        dense_columns[x] = jnp.transpose(dense_grad[x])

    def mid_part(x, carry):
        columns = dense_columns[x]
        dense_row = vec_row[:, 2 * HID : 3 * HID]
        dense_added = jnp.zeros((8, HID), F32)
        for slot in range(SLOTS):
            rows = pl.ds(slot * RX, RX)
            hidden = h2[x, rows, :].astype(F32)
            scale = columns[:, slot : slot + 1]
            found = jnp.where(hidden > 0.0, hgrad[x, rows, :] + scale * dense_row, 0.0)
            second[x, rows, :] = found.astype(BF16)
            dense_added = dense_added + to_row_groups(scale * hidden)
        sum_dense[...] += dense_added
        g_mid[...] += jnp.dot(h1_t[x], second[x], preferred_element_type=F32)
        return carry

    lax.fori_loop(0, NX, mid_part, 0)
    mid_send[...] = g_mid[pl.ds(0, HID), :].astype(BF16).reshape(NR, 32, HID)
    spread_rays(1, mid_send, mid_got)

    def in_part(x, carry):
        first[...] = jnp.where(
            h1[x].astype(F32) > 0.0, dot_nt(second[x], w_mid[...]), 0.0
        ).astype(BF16)
        g_in[...] += jnp.dot(enc_t[x], first[...], preferred_element_type=F32)
        return carry

    lax.fori_loop(0, NX, in_part, 0)
    in_send[...] = g_in[pl.ds(0, IN), :].astype(BF16).reshape(NR, 16, HID)
    spread_rays(2, in_send, in_got)
    sums = [
        g_in[pl.ds(IN, 8), :][:1],
        g_mid[pl.ds(HID, 8), :][:1],
        jnp.sum(sum_dense[...], 0, keepdims=True),
        g_feat[pl.ds(HID, 8), :][:1],
    ]
    row = jnp.concatenate(sums + [jnp.zeros((1, 128), F32)], 1)
    for index in range(NR):
        turned = pltpu.roll(row, 1280 - PART * index, 1) if index else row
        vec_send[index] = turned[:, :WIDE]
    spread_rays(3, vec_send, vec_got)

    def own_rows(total, count):
        return total[pl.ds(pl.multiple_of(me * count, count), count), :]

    feat_out[...] = gather_rays(0, feat_send, feat_got, own_rows(g_feat, 32))
    mid_out[...] = gather_rays(1, mid_send, mid_got, own_rows(g_mid, 32))
    in_out[...] = gather_rays(2, in_send, in_got, own_rows(g_in, 16))
    vec_out[...] = gather_rays(3, vec_send, vec_got, vec_send[me])


def run_step(*operands):
    def pair(*count):
        return pltpu.SemaphoreType.DMA((2, *count))

    outs = (((16, 256), F32), ((32, 256), F32), ((32, 384), F32), ((1, WIDE), F32))
    outs += (((NX, 1, RX), F32),)
    scratch = (
        ((2, NX * RX, IN), BF16),
        ((SLOTS, NX * RX), jnp.int32),
        ((1, NX * RX), jnp.int32),
        ((1, NX * RX), jnp.int32),
        ((NX, 1, RX), jnp.int32),
        ((NX * RX, FEAT), BF16),
        ((16, HID), F32),
        ((32, HID), F32),
        ((32, FEAT), F32),
        ((1, PART), F32),
        ((IN, HID), BF16),
        ((HID, HID), BF16),
        ((HID, FEAT), BF16),
        ((NR, 1, WIDE), F32),
        ((NX, ROWS, IN), BF16),
        ((NX, ROWS, HID), BF16),
        ((NX, ROWS, HID), BF16),
        ((NX, IN + 16, ROWS), BF16),
        ((NX, HID + 16, ROWS), BF16),
        ((NX, HID + 16, ROWS), BF16),
        ((NX, ROWS, FEAT), F32),
        ((NX, ROWS, FEAT), F32),
        ((ROWS, FEAT), BF16),
        ((NX, ROWS, HID), F32),
        ((NX, ROWS, HID), BF16),
        ((ROWS, HID), BF16),
        ((NX, SLOTS, RX), F32),
        ((NX, SLOTS, RX), F32),
        ((NX, SLOTS, RX), F32),
        ((NX, SLOTS, RX), F32),
        ((NX, SLOTS, RX), F32),
        ((NX, SLOTS, RX), F32),
        ((HID, RX), BF16),
        ((1, 1280), F32),
        ((IN + 16, HID), F32),
        ((HID + 16, HID), F32),
        ((HID + 16, FEAT), F32),
        ((8, HID), F32),
        ((NX, RX, SLOTS), F32),
        ((NX, 1, RX), F32),
        ((NX * NZ, 1, RX), F32),
        ((NX, RX, FEAT), BF16),
        ((NX, RX, FEAT), BF16),
        ((NX, 1, RX), F32),
        ((NX, 1, RX), F32),
        ((NZ, RZ, FEAT), BF16),
        ((NZ, RZ, FEAT), BF16),
        ((NZ, RZ, FEAT), BF16),
        ((NX, RX, FEAT), BF16),
        ((NX, 1, RX), F32),
        ((NX * NZ, NX, 1, RX), F32),
        ((NR, 16, 256), BF16),
        ((NR, 32, 256), BF16),
        ((NR, 32, 384), BF16),
        ((NR, 1, WIDE), F32),
        ((NR, 16, 256), BF16),
        ((NR, 32, 256), BF16),
        ((NR, 32, 384), BF16),
        ((NR, 1, WIDE), F32),
    )
    return pl.pallas_call(
        step_kernel,
        out_shape=tuple(jax.ShapeDtypeStruct(*out) for out in outs),
        in_specs=[pl.BlockSpec(memory_space=pl.ANY)] * len(operands),
        out_specs=tuple(vmem(len(outs))),
        scratch_shapes=[pltpu.VMEM(*part) for part in scratch]
        + [pair(), pair(), pair(), pair(), pair(), pair(NX), pair()]
        + [pair(4), pltpu.SemaphoreType.DMA((10,)), pair(4)],
        compiler_params=pltpu.CompilerParams(
            collective_id=0, has_side_effects=True, vmem_limit_bytes=60 * 2**20
        ),
        name="run_step",
    )(*operands)


def adam_kernel(*refs):
    states, grads, after_ref, outs, depth_out = refs[:4], refs[4:8], refs[8], refs[9:13], refs[13]
    for state, grad, out in zip(states, grads, outs):
        gradient = grad[...].reshape((1,) + grad.shape) if len(state.shape) == 4 else grad[...]
        gradient = gradient[..., : state.shape[-1]]
        first_moment = beta_one * state[1] + (1.0 - beta_one) * gradient
        second = beta_two * state[2] + (1.0 - beta_two) * gradient * gradient
        update_step = first_moment / first_fix / (jnp.sqrt(second / second_fix) + epsilon)
        out[0] = state[0] - learn_rate * update_step
        out[1] = first_moment
        out[2] = second
    depth_out[...] = -after_ref[...]


def adam_all(states, grads, after):
    shapes = [jax.ShapeDtypeStruct(state.shape, F32) for state in states]
    shapes.append(jax.ShapeDtypeStruct(after.shape, F32))
    return pl.pallas_call(
        adam_kernel,
        out_shape=tuple(shapes),
        in_specs=vmem(9),
        out_specs=tuple(vmem(5)),
        name="adam_all",
    )(*states, *grads, after)


def per_device(
    ray_codes,
    target,
    direction,
    entries,
    exits,
    depth_bins,
    in_layer,
    mid_layer,
    feat_layer,
    vectors,
):
    *grads, after = run_step(
        ray_codes,
        depth_bins,
        entries,
        exits,
        direction.reshape(NX, 1, RX),
        target,
        in_layer,
        mid_layer,
        feat_layer,
        vectors,
    )
    *states, depth_grad = adam_all((in_layer, mid_layer, feat_layer, vectors), grads, after)
    return (*states, depth_grad.reshape(1, NX * RX))


def solution(mesh):
    placed = (
        P(None, "rays", None),
        P("rays", None),
        P("rays"),
        P("region", "rays"),
        P("region", "rays"),
        P("region", None, "rays"),
        P(None, "region", "rays", None),
        P(None, "region", "rays", None),
        P(None, "region", "rays", None),
        P(None, "region", "rays"),
    )
    return jax.shard_map(
        per_device,
        mesh=mesh,
        in_specs=placed,
        out_specs=(
            P(None, "region", "rays", None),
            P(None, "region", "rays", None),
            P(None, "region", "rays", None),
            P(None, "region", "rays"),
            P("region", "rays"),
        ),
        check_vma=False,
    )
```

```python
import jax
import jax.numpy as jnp
from jax import lax
from jax.experimental import pallas as pl
from jax.experimental.pallas import tpu as pltpu
from jax.sharding import PartitionSpec as P

BINS = 64


depth_scale = 4.0
beta_one = 0.9
beta_two = 0.999
learn_rate = 0.001
epsilon = 1e-08
first_fix = 1.0 - 0.9**10
second_fix = 1.0 - 0.999**10

MESH = pl.DeviceIdType.MESH
NX = 4
NZ = 16
NR = 8
RX = 128
RZ = 8
IN = 128
HID = 256
FEAT = 384
SLOTS = 8
ROWS = SLOTS * RX
PART = 144
WIDE = 256
F32 = jnp.float32
BF16 = jnp.bfloat16


def vmem(count):
    return [pl.BlockSpec(memory_space=pltpu.VMEM)] * count


def remote(source, target, send_sem, recv_sem, peer):
    return pltpu.make_async_remote_copy(
        src_ref=source,
        dst_ref=target,
        send_sem=send_sem,
        recv_sem=recv_sem,
        device_id=peer,
        device_id_type=MESH,
    )


def far_first(count):
    half = count // 2
    order = [half]
    for gap in range(1, half):
        order += [half - gap, half + gap]
    return order


def z_sums(table, own_z):
    column = [jnp.zeros((1, RX), F32) for _ in range(NX)]
    lower, upper = list(column), list(column)
    for z in range(NZ):
        under, over = (z < own_z).astype(F32), (z > own_z).astype(F32)
        for x in range(NX):
            rows = table[x * NZ + z]
            column[x] = column[x] + rows
            lower[x] = lower[x] + rows * under
            upper[x] = upper[x] + rows * over
    return column, lower, upper


def far_regions():
    hops = [
        (min(x, NX - x) + min(z, NZ - z), x, z) for x in range(NX) for z in range(NZ) if x + z
    ]
    return [(x, z) for _, x, z in sorted(hops, reverse=True)]


def x_sums(column, lower, upper):
    below, above = [], []
    for x in range(NX):
        under, over = lower[x], upper[x]
        for other in range(NX):
            if other < x:
                under = under + column[other]
            if other > x:
                over = over + column[other]
        below.append(under)
        above.append(over)
    return below, above


def one_less_exp(value):
    series = value * (
        1.0 - value / 2.0 * (1.0 - value / 3.0 * (1.0 - value / 4.0 * (1.0 - value / 5.0)))
    )
    return jnp.where(value < 0.0625, series, 1.0 - jnp.exp(-value))


def sum_before(rows):
    running = jnp.zeros((NX, 1, RX), F32)
    found = []
    for slot in range(SLOTS):
        found.append(running)
        running = running + rows[:, slot : slot + 1]
    return jnp.concatenate(found, 1), running


def sum_after(rows):
    running = jnp.zeros((NX, 1, RX), F32)
    found = []
    for slot in range(SLOTS - 1, -1, -1):
        found.append(running)
        running = running + rows[:, slot : slot + 1]
    return jnp.concatenate(found[::-1], 1)


def to_row_groups(values):
    return jnp.sum(values.reshape(values.shape[0] // 8, 8, values.shape[1]), 0)


def dot_nt(left, right):
    return lax.dot_general(left, right, (((1,), (1,)), ((), ())), preferred_element_type=F32)


def step_kernel(
    codes_hbm,
    bins_hbm,
    entry_hbm,
    exit_hbm,
    onward_hbm,
    target_hbm,
    in_layer,
    mid_layer,
    feat_layer,
    vectors,
    in_out,
    mid_out,
    feat_out,
    vec_out,
    after_out,
    codes_ref,
    bins_ref,
    entry_ref,
    exit_ref,
    onward_ref,
    target_ref,
    in_own,
    mid_own,
    feat_own,
    vec_own,
    w_in,
    w_mid,
    w_feat,
    vec_ref,
    enc,
    h1,
    h2,
    enc_t,
    h1_t,
    h2_t,
    colour,
    coef,
    cgrad,
    hgrad,
    second,
    first,
    raw_rows,
    optical_rows,
    before_rows,
    weight_rows,
    span_rows,
    sample_rows,
    dense_wide,
    vec_row,
    g_in,
    g_mid,
    g_feat,
    sum_dense,
    dense_columns,
    depth_send,
    depth_all,
    partial_send,
    partial_x,
    trans_send,
    trans_all,
    pieces,
    pieces_z,
    grad_z,
    grad_all,
    region_send,
    region_all,
    in_send,
    mid_send,
    feat_send,
    vec_send,
    in_got,
    mid_got,
    feat_got,
    vec_got,
    sem_depth,
    sem_partial,
    sem_trans,
    sem_piece,
    sem_grad_z,
    sem_grad,
    sem_region,
    sem_rays,
    sem_load,
    sem_weight,
    column_sem,
    line_sem,
):
    place = lax.axis_index("region")
    me = lax.axis_index("rays")
    own_x, own_z = place // NZ, lax.rem(place, NZ)

    def along_x(step):
        return lax.rem(own_x + step, NX)

    def along_z(step):
        return lax.rem(own_z + step, NZ)

    def at(x, z):
        return {"region": x * NZ + z}

    barrier = pltpu.get_barrier_semaphore()
    for step in (1, NZ - 1):
        pl.semaphore_signal(
            barrier, inc=1, device_id=at(own_x, along_z(step)), device_id_type=MESH
        )
    for step in (2, 1, 3):
        pl.semaphore_signal(
            barrier, inc=1, device_id=at(along_x(step), own_z), device_id_type=MESH
        )
    for step in range(1, NR):
        pl.semaphore_signal(
            barrier, inc=1, device_id={"rays": lax.rem(me + step, NR)}, device_id_type=MESH
        )

    def arrived(sent, got, count, sems, peer):
        first = pl.ds(0, count)
        remote(sent.at[first], got.at[first], sems.at[0], sems.at[1], peer).wait()

    def spread_x(source, target, sems):
        for step in (2, 1, 3):
            x = along_x(step)
            remote(source(x), target.at[own_x], sems.at[0], sems.at[1], at(x, own_z)).start()

    def wait_x(sent, got, sems):
        arrived(sent, got, NX - 1, sems, at(along_x(1), own_z))

    def spread_z(source, target, sems):
        for step in far_first(NZ):
            z = along_z(step)
            remote(source(z), target.at[own_z], sems.at[0], sems.at[1], at(own_x, z)).start()

    def wait_z(sent, got, sems):
        arrived(sent, got, NZ - 1, sems, at(own_x, along_z(1)))

    def spread_all(source, target, sems):
        for far_x, far_z in far_regions():
            x, z = along_x(far_x), along_z(far_z)
            remote(source(x, z), target.at[place], sems.at[0], sems.at[1], at(x, z)).start()

    def wait_all(table, sems):
        arrived(table, table, NX * NZ - 1, sems, at(along_x(1), own_z))

    def spread_rays(kind, source, target):
        for step in range(1, NR):
            peer = lax.rem(me + step, NR)
            remote(
                source.at[peer],
                target.at[me],
                sem_rays.at[0, kind],
                sem_rays.at[1, kind],
                {"rays": peer},
            ).start()
        target[me] = jnp.zeros(target.shape[1:], target.dtype)

    def gather_rays(kind, source, target, total):
        first = pl.ds(0, NR - 1)
        remote(
            source.at[first],
            target.at[first],
            sem_rays.at[0, kind],
            sem_rays.at[1, kind],
            {"rays": lax.rem(me + 1, NR)},
        ).wait()
        return total + jnp.sum(target[...].astype(F32), 0)

    loads = [
        pltpu.make_async_copy(source, target, sem_load.at[index])
        for index, (source, target) in enumerate(
            (
                (in_layer.at[0, 0], in_own),
                (mid_layer.at[0, 0], mid_own),
                (feat_layer.at[0, 0], feat_own),
                (vectors.at[0], vec_own),
                (codes_hbm, codes_ref),
                (bins_hbm.at[0], bins_ref),
                (entry_hbm, entry_ref),
                (exit_hbm, exit_ref),
                (onward_hbm, onward_ref),
                (target_hbm, target_ref),
            )
        )
    ]
    for load in loads:
        load.start()

    def mine(array, count, index):
        return array.at[pl.ds(pl.multiple_of(index * count, count), count)]

    weights = (
        lambda index: mine(w_in, 16, index),
        lambda index: mine(w_mid, 32, index),
        lambda index: vec_ref.at[index],
        lambda index: mine(w_feat, 32, index),
    )

    def spread_weights(kind):
        for step in range(1, NR):
            remote(
                weights[kind](me),
                weights[kind](me),
                sem_weight.at[0, kind],
                sem_weight.at[1, kind],
                {"rays": lax.rem(me + step, NR)},
            ).start()

    def wait_weights(kind):
        array, count = ((w_in, 16), (w_mid, 32), (vec_ref, 1), (w_feat, 32))[kind]
        first = array.at[pl.ds(0, count * (NR - 1))]
        remote(
            first,
            first,
            sem_weight.at[0, kind],
            sem_weight.at[1, kind],
            {"rays": lax.rem(me + 1, NR)},
        ).wait()

    unit = depth_scale / (NX * NZ * BINS)
    lane = lax.broadcasted_iota(jnp.int32, (RX, RX), 1)
    slot_row = lax.broadcasted_iota(jnp.int32, (SLOTS, RX), 0)
    for load in loads[:4]:
        load.wait()
    weights[0](me)[...] = in_own[...].astype(BF16)
    weights[1](me)[...] = mid_own[...].astype(BF16)
    weights[3](me)[...] = feat_own[...].astype(BF16)
    vec_ref[me] = jnp.zeros((1, WIDE), F32)
    vec_ref[me, :, pl.ds(0, PART)] = vec_own[...].astype(BF16).astype(F32)
    pl.semaphore_wait(barrier, NX + NR)
    for kind in range(4):
        spread_weights(kind)

    def tell_line(reach):
        for step in (reach, NZ - reach):
            pl.semaphore_signal(
                line_sem.at[reach.bit_length() - 1],
                inc=1,
                device_id=at(own_x, along_z(step)),
                device_id_type=MESH,
            )

    def hear_line(reach):
        pl.semaphore_wait(line_sem.at[reach.bit_length() - 1], 2)

    tell_line(1)
    for load in loads[4:]:
        load.wait()
    for total in (g_in, g_mid, g_feat, sum_dense):
        total[...] = jnp.zeros(total.shape, F32)
    ones = jnp.ones((16, ROWS), BF16)
    for x in range(NX):
        enc_t[x, pl.ds(IN, 16), :] = ones
        h1_t[x, pl.ds(HID, 16), :] = ones
        h2_t[x, pl.ds(HID, 16), :] = ones

    hear_line(1)
    tell_line(2)

    def code_part(x, carry):
        lanes = pl.ds(pl.multiple_of(x * RX, RX), RX)
        bins = bins_ref[:, lanes].astype(F32)
        columns = jnp.transpose((bins + 0.5) / BINS)
        anchor = codes_ref[0, lanes, :].astype(F32)
        heading = codes_ref[1, lanes, :].astype(F32)
        for slot in range(SLOTS):
            enc[x, pl.ds(slot * RX, RX), :] = (
                anchor + columns[:, slot : slot + 1] * heading
            ).astype(BF16)
        following = jnp.concatenate([bins[1:], jnp.full((1, RX), float(BINS), F32)], 0)
        inside = (slot_row >= entry_ref[:, lanes]) & (slot_row < exit_ref[:, lanes])
        span_rows[x] = jnp.where(inside, (following - bins) * unit, 0.0)
        return carry

    lax.fori_loop(0, NX, code_part, 0)
    hear_line(2)
    tell_line(4)

    def turn_code(x, carry):
        enc_t[x, pl.ds(0, IN), :] = jnp.transpose(enc[x])
        return carry

    lax.fori_loop(0, NX, turn_code, 0)
    hear_line(4)
    for step in (2, 1, 3):
        pl.semaphore_signal(
            column_sem, inc=1, device_id=at(along_x(step), own_z), device_id_type=MESH
        )
    for kind in range(3):
        wait_weights(kind)
    row = jnp.zeros((1, 1280), F32)
    tail = jnp.zeros((1, 1280 - WIDE), F32)
    for index in range(NR):
        wide = jnp.concatenate([vec_ref[index], tail], 1)
        row = row + (pltpu.roll(wide, PART * index, 1) if index else wide)
    vec_row[...] = row
    dense_wide[...] = jnp.transpose(
        jnp.broadcast_to(row[:, 2 * HID : 3 * HID], (RX, HID))
    ).astype(BF16)

    def hidden_part(index, carry):
        x = along_x(index + 1)
        h1[x] = jnp.maximum(
            jnp.dot(enc[x], w_in[...], preferred_element_type=F32) + vec_row[:, :HID], 0.0
        ).astype(BF16)
        h2[x] = jnp.maximum(
            jnp.dot(h1[x], w_mid[...], preferred_element_type=F32) + vec_row[:, HID : 2 * HID],
            0.0,
        ).astype(BF16)
        dense = jnp.dot(h2[x], dense_wide[...], preferred_element_type=F32)
        grid = jnp.zeros((RX, RX), F32)
        for slot in range(SLOTS):
            grid = jnp.where(lane == slot, dense[slot * RX : (slot + 1) * RX], grid)
        raw_rows[x] = jnp.transpose(grid)[:SLOTS]
        return carry

    lax.fori_loop(0, NX, hidden_part, 0)
    raw = raw_rows[...]
    soft = jnp.maximum(raw, 0.0) + jnp.log1p(jnp.exp(-jnp.abs(raw)))
    optical = soft * span_rows[...]
    before, total = sum_before(optical)
    depth_send[...] = total
    pl.semaphore_wait(column_sem, NX - 1)
    spread_all(lambda x, z: depth_send.at[x], depth_all, sem_depth)
    depth_all[place] = depth_send[own_x]
    optical_rows[...] = optical
    before_rows[...] = before
    weight_rows[...] = jnp.exp(-before) * one_less_exp(optical)
    wait_weights(3)

    def colour_part(index, carry):
        x = along_x(index + 1)
        colour[x] = jax.nn.sigmoid(
            jnp.dot(h2[x], w_feat[...], preferred_element_type=F32)
            + vec_row[:, 3 * HID : 3 * HID + FEAT]
        )
        columns = jnp.transpose(weight_rows[x])
        local = jnp.zeros((RX, FEAT), F32)
        for slot in range(SLOTS):
            local = local + columns[:, slot : slot + 1] * colour[x, pl.ds(slot * RX, RX), :]
        partial_send[x] = local.astype(BF16)

        @pl.when(index < NX - 1)
        def _():
            remote(
                partial_send.at[x],
                partial_x.at[own_x],
                sem_partial.at[0],
                sem_partial.at[1],
                at(x, own_z),
            ).start()

        return carry

    lax.fori_loop(0, NX, colour_part, 0)
    partial_x[own_x] = partial_send[own_x]
    wait_all(depth_all, sem_depth)
    below, above = x_sums(*z_sums(depth_all, own_z))
    onward = onward_ref[own_x] == 0
    trans = [jnp.exp(-jnp.where(onward, below[x], above[x])) for x in range(NX)]
    for x in range(NX):
        trans_send[x] = trans[x]
    trans_all[own_x] = trans_send[own_x]
    spread_x(lambda x: trans_send.at[x], trans_all, sem_trans)
    columns = jnp.transpose(jnp.concatenate(trans + trans, 0))
    wait_x(partial_send, partial_x, sem_partial)
    total = jnp.zeros((RX, FEAT), F32)
    for x in range(NX):
        total = total + columns[:, x : x + 1] * partial_x[x].astype(F32)
    pieces[...] = total.reshape(NZ, RZ, FEAT).astype(BF16)
    spread_z(lambda z: pieces.at[z], pieces_z, sem_piece)
    pieces_z[own_z] = pieces[own_z]

    def turn_part(x, carry):
        h1_t[x, pl.ds(0, HID), :] = jnp.transpose(h1[x])
        h2_t[x, pl.ds(0, HID), :] = jnp.transpose(h2[x])
        return carry

    lax.fori_loop(0, NX, turn_part, 0)
    start = pl.multiple_of(own_x * RX + (own_z // 2) * (2 * RZ), 2 * RZ)
    wanted = target_ref[pl.ds(start, 2 * RZ), :].astype(F32)
    odd = lax.rem(own_z, 2).astype(F32)
    wanted = wanted[:RZ] * (1.0 - odd) + wanted[RZ:] * odd
    wait_z(pieces, pieces_z, sem_piece)
    rendered = jnp.sum(pieces_z[...].astype(F32), 0)
    grad_z[own_z] = (rendered - wanted).astype(BF16)
    spread_z(lambda z: grad_z.at[own_z], grad_z, sem_grad_z)
    wait_x(trans_send, trans_all, sem_trans)

    def coef_part(x, carry):
        columns = jnp.transpose(trans_all[x] * weight_rows[x])
        for slot in range(SLOTS):
            rows = pl.ds(slot * RX, RX)
            shade = colour[x, rows, :]
            coef[x, rows, :] = columns[:, slot : slot + 1] * (shade * (1.0 - shade))
        return carry

    lax.fori_loop(0, NX, coef_part, 0)
    wait_z(grad_z, grad_z, sem_grad_z)
    grad_float = grad_z[...].astype(F32).reshape(RX, FEAT)
    grad_all[own_x] = grad_float.astype(BF16)
    for step in (2, 1, 3):
        remote(
            grad_all.at[own_x],
            grad_all.at[own_x],
            sem_grad.at[0, step],
            sem_grad.at[1, step],
            at(along_x(step), own_z),
        ).start()
    grid = jnp.zeros((RX, RX), F32)
    for x in range(NX):
        dots = jnp.sum(grad_float * partial_x[x].astype(F32), -1, keepdims=True)
        grid = jnp.where(lane == x, dots, grid)
    grid = jnp.transpose(grid)
    grads = [grid[x : x + 1] * trans_send[x] for x in range(NX)]
    for x in range(NX):
        over, under = jnp.zeros((1, RX), F32), jnp.zeros((1, RX), F32)
        for other in range(NX):
            if other > x:
                over = over + grads[other]
            if other < x:
                under = under + grads[other]
        level = jnp.where(onward, over, under)
        region_send[3 * x] = level
        region_send[3 * x + 1] = level + jnp.where(onward, grads[x], 0.0)
        region_send[3 * x + 2] = level + jnp.where(onward, 0.0, grads[x])

    def after_row(x, z):
        side = (own_z > z).astype(jnp.int32) + 2 * (own_z < z).astype(jnp.int32)
        return region_send.at[3 * x + side]

    spread_all(after_row, region_all, sem_region)
    region_all[place] = region_send[3 * own_x]

    def feat_part(index, carry):
        x = along_x(index)

        @pl.when(index > 0)
        def _():
            step = NX - index
            remote(
                grad_all.at[own_x],
                grad_all.at[x],
                sem_grad.at[0, step],
                sem_grad.at[1, step],
                at(x, own_z),
            ).wait()

        grads = grad_all[x].astype(F32)
        grid = jnp.zeros((RX, RX), F32)
        for slot in range(SLOTS):
            rows = pl.ds(slot * RX, RX)
            shade = colour[x, rows, :]
            grid = jnp.where(lane == slot, jnp.sum(shade * grads, -1, keepdims=True), grid)
            cgrad[rows, :] = (coef[x, rows, :] * grads).astype(BF16)
        sample_rows[x] = jnp.transpose(grid)[:SLOTS]
        g_feat[...] += jnp.dot(h2_t[x], cgrad[...], preferred_element_type=F32)
        hgrad[x] = dot_nt(cgrad[...], w_feat[...])
        return carry

    lax.fori_loop(0, NX, feat_part, 0)
    feat_send[...] = g_feat[pl.ds(0, HID), :].astype(BF16).reshape(NR, 32, FEAT)
    spread_rays(0, feat_send, feat_got)
    samples = sample_rows[...]
    later = sum_after(weight_rows[...] * samples)
    local_grad = trans_all[...] * (
        jnp.exp(-(before_rows[...] + optical_rows[...])) * samples - later
    )
    dense_scale = span_rows[...] * jax.nn.sigmoid(raw_rows[...])
    wait_all(region_all, sem_region)
    after = jnp.sum(region_all[...].reshape(NX, NZ, 1, RX), 1)
    after_out[...] = after
    dense_grad = ((local_grad - after) * dense_scale).astype(BF16).astype(F32)
    for x in range(NX):
        dense_columns[x] = jnp.transpose(dense_grad[x])

    def mid_part(x, carry):
        columns = dense_columns[x]
        dense_row = vec_row[:, 2 * HID : 3 * HID]
        dense_added = jnp.zeros((8, HID), F32)
        for slot in range(SLOTS):
            rows = pl.ds(slot * RX, RX)
            hidden = h2[x, rows, :].astype(F32)
            scale = columns[:, slot : slot + 1]
            found = jnp.where(hidden > 0.0, hgrad[x, rows, :] + scale * dense_row, 0.0)
            second[x, rows, :] = found.astype(BF16)
            dense_added = dense_added + to_row_groups(scale * hidden)
        sum_dense[...] += dense_added
        g_mid[...] += jnp.dot(h1_t[x], second[x], preferred_element_type=F32)
        return carry

    lax.fori_loop(0, NX, mid_part, 0)
    mid_send[...] = g_mid[pl.ds(0, HID), :].astype(BF16).reshape(NR, 32, HID)
    spread_rays(1, mid_send, mid_got)

    def in_part(x, carry):
        first[...] = jnp.where(
            h1[x].astype(F32) > 0.0, dot_nt(second[x], w_mid[...]), 0.0
        ).astype(BF16)
        g_in[...] += jnp.dot(enc_t[x], first[...], preferred_element_type=F32)
        return carry

    lax.fori_loop(0, NX, in_part, 0)
    in_send[...] = g_in[pl.ds(0, IN), :].astype(BF16).reshape(NR, 16, HID)
    spread_rays(2, in_send, in_got)
    sums = [
        g_in[pl.ds(IN, 8), :][:1],
        g_mid[pl.ds(HID, 8), :][:1],
        jnp.sum(sum_dense[...], 0, keepdims=True),
        g_feat[pl.ds(HID, 8), :][:1],
    ]
    row = jnp.concatenate(sums + [jnp.zeros((1, 128), F32)], 1)
    for index in range(NR):
        turned = pltpu.roll(row, 1280 - PART * index, 1) if index else row
        vec_send[index] = turned[:, :WIDE]
    spread_rays(3, vec_send, vec_got)

    def own_rows(total, count):
        return total[pl.ds(pl.multiple_of(me * count, count), count), :]

    feat_out[...] = gather_rays(0, feat_send, feat_got, own_rows(g_feat, 32))
    mid_out[...] = gather_rays(1, mid_send, mid_got, own_rows(g_mid, 32))
    in_out[...] = gather_rays(2, in_send, in_got, own_rows(g_in, 16))
    vec_out[...] = gather_rays(3, vec_send, vec_got, vec_send[me])


def run_step(*operands):
    def pair(*count):
        return pltpu.SemaphoreType.DMA((2, *count))

    outs = (((16, 256), F32), ((32, 256), F32), ((32, 384), F32), ((1, WIDE), F32))
    outs += (((NX, 1, RX), F32),)
    scratch = (
        ((2, NX * RX, IN), BF16),
        ((SLOTS, NX * RX), jnp.int32),
        ((1, NX * RX), jnp.int32),
        ((1, NX * RX), jnp.int32),
        ((NX, 1, RX), jnp.int32),
        ((NX * RX, FEAT), BF16),
        ((16, HID), F32),
        ((32, HID), F32),
        ((32, FEAT), F32),
        ((1, PART), F32),
        ((IN, HID), BF16),
        ((HID, HID), BF16),
        ((HID, FEAT), BF16),
        ((NR, 1, WIDE), F32),
        ((NX, ROWS, IN), BF16),
        ((NX, ROWS, HID), BF16),
        ((NX, ROWS, HID), BF16),
        ((NX, IN + 16, ROWS), BF16),
        ((NX, HID + 16, ROWS), BF16),
        ((NX, HID + 16, ROWS), BF16),
        ((NX, ROWS, FEAT), F32),
        ((NX, ROWS, FEAT), F32),
        ((ROWS, FEAT), BF16),
        ((NX, ROWS, HID), F32),
        ((NX, ROWS, HID), BF16),
        ((ROWS, HID), BF16),
        ((NX, SLOTS, RX), F32),
        ((NX, SLOTS, RX), F32),
        ((NX, SLOTS, RX), F32),
        ((NX, SLOTS, RX), F32),
        ((NX, SLOTS, RX), F32),
        ((NX, SLOTS, RX), F32),
        ((HID, RX), BF16),
        ((1, 1280), F32),
        ((IN + 16, HID), F32),
        ((HID + 16, HID), F32),
        ((HID + 16, FEAT), F32),
        ((8, HID), F32),
        ((NX, RX, SLOTS), F32),
        ((NX, 1, RX), F32),
        ((NX * NZ, 1, RX), F32),
        ((NX, RX, FEAT), BF16),
        ((NX, RX, FEAT), BF16),
        ((NX, 1, RX), F32),
        ((NX, 1, RX), F32),
        ((NZ, RZ, FEAT), BF16),
        ((NZ, RZ, FEAT), BF16),
        ((NZ, RZ, FEAT), BF16),
        ((NX, RX, FEAT), BF16),
        ((3 * NX, 1, RX), F32),
        ((NX * NZ, 1, RX), F32),
        ((NR, 16, 256), BF16),
        ((NR, 32, 256), BF16),
        ((NR, 32, 384), BF16),
        ((NR, 1, WIDE), F32),
        ((NR, 16, 256), BF16),
        ((NR, 32, 256), BF16),
        ((NR, 32, 384), BF16),
        ((NR, 1, WIDE), F32),
    )
    return pl.pallas_call(
        step_kernel,
        out_shape=tuple(jax.ShapeDtypeStruct(*out) for out in outs),
        in_specs=[pl.BlockSpec(memory_space=pl.ANY)] * len(operands),
        out_specs=tuple(vmem(len(outs))),
        scratch_shapes=[pltpu.VMEM(*part) for part in scratch]
        + [pair(), pair(), pair(), pair(), pair(), pair(NX), pair()]
        + [pair(4), pltpu.SemaphoreType.DMA((10,)), pair(4), pltpu.SemaphoreType.REGULAR]
        + [pltpu.SemaphoreType.REGULAR((3,))],
        compiler_params=pltpu.CompilerParams(
            collective_id=0, has_side_effects=True, vmem_limit_bytes=60 * 2**20
        ),
        name="run_step",
    )(*operands)


def adam_kernel(*refs):
    states, grads, after_ref, outs, depth_out = refs[:4], refs[4:8], refs[8], refs[9:13], refs[13]
    for state, grad, out in zip(states, grads, outs):
        gradient = grad[...].reshape((1,) + grad.shape) if len(state.shape) == 4 else grad[...]
        gradient = gradient[..., : state.shape[-1]]
        first_moment = beta_one * state[1] + (1.0 - beta_one) * gradient
        second = beta_two * state[2] + (1.0 - beta_two) * gradient * gradient
        update_step = first_moment / first_fix / (jnp.sqrt(second / second_fix) + epsilon)
        out[0] = state[0] - learn_rate * update_step
        out[1] = first_moment
        out[2] = second
    depth_out[...] = -after_ref[...]


def adam_all(states, grads, after):
    shapes = [jax.ShapeDtypeStruct(state.shape, F32) for state in states]
    shapes.append(jax.ShapeDtypeStruct(after.shape, F32))
    return pl.pallas_call(
        adam_kernel,
        out_shape=tuple(shapes),
        in_specs=vmem(9),
        out_specs=tuple(vmem(5)),
        name="adam_all",
    )(*states, *grads, after)


def per_device(
    ray_codes,
    target,
    direction,
    entries,
    exits,
    depth_bins,
    in_layer,
    mid_layer,
    feat_layer,
    vectors,
):
    *grads, after = run_step(
        ray_codes,
        depth_bins,
        entries,
        exits,
        direction.reshape(NX, 1, RX),
        target,
        in_layer,
        mid_layer,
        feat_layer,
        vectors,
    )
    *states, depth_grad = adam_all((in_layer, mid_layer, feat_layer, vectors), grads, after)
    return (*states, depth_grad.reshape(1, NX * RX))


def solution(mesh):
    placed = (
        P(None, "rays", None),
        P("rays", None),
        P("rays"),
        P("region", "rays"),
        P("region", "rays"),
        P("region", None, "rays"),
        P(None, "region", "rays", None),
        P(None, "region", "rays", None),
        P(None, "region", "rays", None),
        P(None, "region", "rays"),
    )
    return jax.shard_map(
        per_device,
        mesh=mesh,
        in_specs=placed,
        out_specs=(
            P(None, "region", "rays", None),
            P(None, "region", "rays", None),
            P(None, "region", "rays", None),
            P(None, "region", "rays"),
            P("region", "rays"),
        ),
        check_vma=False,
    )
```

```python
import jax
import jax.numpy as jnp
from jax import lax
from jax.experimental import pallas as pl
from jax.experimental.pallas import tpu as pltpu
from jax.sharding import PartitionSpec as P

BINS = 64


depth_scale = 4.0
beta_one = 0.9
beta_two = 0.999
learn_rate = 0.001
epsilon = 1e-08
first_fix = 1.0 - 0.9**10
second_fix = 1.0 - 0.999**10

MESH = pl.DeviceIdType.MESH
NX = 4
NZ = 16
NR = 8
RX = 128
RZ = 8
IN = 128
HID = 256
FEAT = 384
SLOTS = 8
ROWS = SLOTS * RX
PART = 144
WIDE = 256
F32 = jnp.float32
BF16 = jnp.bfloat16


def vmem(count):
    return [pl.BlockSpec(memory_space=pltpu.VMEM)] * count


def remote(source, target, send_sem, recv_sem, peer):
    return pltpu.make_async_remote_copy(
        src_ref=source,
        dst_ref=target,
        send_sem=send_sem,
        recv_sem=recv_sem,
        device_id=peer,
        device_id_type=MESH,
    )


def far_first(count):
    half = count // 2
    order = [half]
    for gap in range(1, half):
        order += [half - gap, half + gap]
    return order


def z_sums(table, own_z):
    column = [jnp.zeros((1, RX), F32) for _ in range(NX)]
    lower, upper = list(column), list(column)
    for z in range(NZ):
        under, over = (z < own_z).astype(F32), (z > own_z).astype(F32)
        for x in range(NX):
            rows = table[x * NZ + z]
            column[x] = column[x] + rows
            lower[x] = lower[x] + rows * under
            upper[x] = upper[x] + rows * over
    return column, lower, upper


def far_regions():
    hops = [
        (min(x, NX - x) + min(z, NZ - z), x, z) for x in range(NX) for z in range(NZ) if x + z
    ]
    return [(x, z) for _, x, z in sorted(hops, reverse=True)]


def x_sums(column, lower, upper):
    below, above = [], []
    for x in range(NX):
        under, over = lower[x], upper[x]
        for other in range(NX):
            if other < x:
                under = under + column[other]
            if other > x:
                over = over + column[other]
        below.append(under)
        above.append(over)
    return below, above


def one_less_exp(value):
    series = value * (
        1.0 - value / 2.0 * (1.0 - value / 3.0 * (1.0 - value / 4.0 * (1.0 - value / 5.0)))
    )
    return jnp.where(value < 0.0625, series, 1.0 - jnp.exp(-value))


def sum_before(rows):
    running = jnp.zeros((NX, 1, RX), F32)
    found = []
    for slot in range(SLOTS):
        found.append(running)
        running = running + rows[:, slot : slot + 1]
    return jnp.concatenate(found, 1), running


def sum_after(rows):
    running = jnp.zeros((NX, 1, RX), F32)
    found = []
    for slot in range(SLOTS - 1, -1, -1):
        found.append(running)
        running = running + rows[:, slot : slot + 1]
    return jnp.concatenate(found[::-1], 1)


def to_row_groups(values):
    return jnp.sum(values.reshape(values.shape[0] // 8, 8, values.shape[1]), 0)


def step_kernel(
    codes_hbm,
    bins_hbm,
    entry_hbm,
    exit_hbm,
    onward_hbm,
    target_hbm,
    in_layer,
    mid_layer,
    feat_layer,
    vectors,
    in_out,
    mid_out,
    feat_out,
    vec_out,
    after_out,
    codes_ref,
    bins_ref,
    entry_ref,
    exit_ref,
    onward_ref,
    target_ref,
    in_own,
    mid_own,
    feat_own,
    vec_own,
    w_in,
    w_mid,
    w_feat,
    vec_ref,
    w_mid_t,
    w_feat_t,
    enc,
    h1,
    h2,
    enc_t,
    h1_t,
    h2_t,
    colour,
    coef,
    cgrad,
    hgrad,
    second,
    first,
    raw_rows,
    optical_rows,
    before_rows,
    weight_rows,
    span_rows,
    sample_rows,
    dense_wide,
    vec_row,
    g_in,
    g_mid,
    g_feat,
    sum_dense,
    dense_columns,
    depth_send,
    depth_all,
    partial_send,
    partial_x,
    trans_send,
    trans_all,
    pieces,
    pieces_z,
    grad_z,
    grad_all,
    region_send,
    region_all,
    in_send,
    mid_send,
    feat_send,
    vec_send,
    in_got,
    mid_got,
    feat_got,
    vec_got,
    sem_depth,
    sem_partial,
    sem_trans,
    sem_piece,
    sem_grad_z,
    sem_grad,
    sem_region,
    sem_rays,
    sem_load,
    sem_weight,
    column_sem,
    line_sem,
):
    place = lax.axis_index("region")
    me = lax.axis_index("rays")
    own_x, own_z = place // NZ, lax.rem(place, NZ)

    def along_x(step):
        return lax.rem(own_x + step, NX)

    def along_z(step):
        return lax.rem(own_z + step, NZ)

    def at(x, z):
        return {"region": x * NZ + z}

    barrier = pltpu.get_barrier_semaphore()
    for step in (1, NZ - 1):
        pl.semaphore_signal(
            barrier, inc=1, device_id=at(own_x, along_z(step)), device_id_type=MESH
        )
    for step in (2, 1, 3):
        pl.semaphore_signal(
            barrier, inc=1, device_id=at(along_x(step), own_z), device_id_type=MESH
        )
    for step in range(1, NR):
        pl.semaphore_signal(
            barrier, inc=1, device_id={"rays": lax.rem(me + step, NR)}, device_id_type=MESH
        )

    def arrived(sent, got, count, sems, peer):
        first = pl.ds(0, count)
        remote(sent.at[first], got.at[first], sems.at[0], sems.at[1], peer).wait()

    def spread_x(source, target, sems):
        for step in (2, 1, 3):
            x = along_x(step)
            remote(source(x), target.at[own_x], sems.at[0], sems.at[1], at(x, own_z)).start()

    def wait_x(sent, got, sems):
        arrived(sent, got, NX - 1, sems, at(along_x(1), own_z))

    def spread_z(source, target, sems):
        for step in far_first(NZ):
            z = along_z(step)
            remote(source(z), target.at[own_z], sems.at[0], sems.at[1], at(own_x, z)).start()

    def wait_z(sent, got, sems):
        arrived(sent, got, NZ - 1, sems, at(own_x, along_z(1)))

    def spread_all(source, target, sems):
        for far_x, far_z in far_regions():
            x, z = along_x(far_x), along_z(far_z)
            remote(source(x, z), target.at[place], sems.at[0], sems.at[1], at(x, z)).start()

    def wait_all(table, sems):
        arrived(table, table, NX * NZ - 1, sems, at(along_x(1), own_z))

    def spread_rays(kind, source, target):
        for step in range(1, NR):
            peer = lax.rem(me + step, NR)
            remote(
                source.at[peer],
                target.at[me],
                sem_rays.at[0, kind],
                sem_rays.at[1, kind],
                {"rays": peer},
            ).start()
        target[me] = jnp.zeros(target.shape[1:], target.dtype)

    def gather_rays(kind, source, target, total):
        first = pl.ds(0, NR - 1)
        remote(
            source.at[first],
            target.at[first],
            sem_rays.at[0, kind],
            sem_rays.at[1, kind],
            {"rays": lax.rem(me + 1, NR)},
        ).wait()
        return total + jnp.sum(target[...].astype(F32), 0)

    loads = [
        pltpu.make_async_copy(source, target, sem_load.at[index])
        for index, (source, target) in enumerate(
            (
                (in_layer.at[0, 0], in_own),
                (mid_layer.at[0, 0], mid_own),
                (feat_layer.at[0, 0], feat_own),
                (vectors.at[0], vec_own),
                (codes_hbm, codes_ref),
                (bins_hbm.at[0], bins_ref),
                (entry_hbm, entry_ref),
                (exit_hbm, exit_ref),
                (onward_hbm, onward_ref),
                (target_hbm, target_ref),
            )
        )
    ]
    for load in loads:
        load.start()

    def mine(array, count, index):
        return array.at[pl.ds(pl.multiple_of(index * count, count), count)]

    weights = (
        lambda index: mine(w_in, 16, index),
        lambda index: mine(w_mid, 32, index),
        lambda index: vec_ref.at[index],
        lambda index: mine(w_feat, 32, index),
    )

    def spread_weights(kind):
        for step in range(1, NR):
            remote(
                weights[kind](me),
                weights[kind](me),
                sem_weight.at[0, kind],
                sem_weight.at[1, kind],
                {"rays": lax.rem(me + step, NR)},
            ).start()

    def wait_weights(kind):
        array, count = ((w_in, 16), (w_mid, 32), (vec_ref, 1), (w_feat, 32))[kind]
        first = array.at[pl.ds(0, count * (NR - 1))]
        remote(
            first,
            first,
            sem_weight.at[0, kind],
            sem_weight.at[1, kind],
            {"rays": lax.rem(me + 1, NR)},
        ).wait()

    unit = depth_scale / (NX * NZ * BINS)
    lane = lax.broadcasted_iota(jnp.int32, (RX, RX), 1)
    slot_row = lax.broadcasted_iota(jnp.int32, (SLOTS, RX), 0)
    for load in loads[:4]:
        load.wait()
    weights[0](me)[...] = in_own[...].astype(BF16)
    weights[1](me)[...] = mid_own[...].astype(BF16)
    weights[3](me)[...] = feat_own[...].astype(BF16)
    vec_ref[me] = jnp.zeros((1, WIDE), F32)
    vec_ref[me, :, pl.ds(0, PART)] = vec_own[...].astype(BF16).astype(F32)
    pl.semaphore_wait(barrier, NX + NR)
    for kind in range(4):
        spread_weights(kind)

    def tell_line(reach):
        for step in (reach, NZ - reach):
            pl.semaphore_signal(
                line_sem.at[reach.bit_length() - 1],
                inc=1,
                device_id=at(own_x, along_z(step)),
                device_id_type=MESH,
            )

    def hear_line(reach):
        pl.semaphore_wait(line_sem.at[reach.bit_length() - 1], 2)

    tell_line(1)
    for load in loads[4:]:
        load.wait()
    for total in (g_in, g_mid, g_feat, sum_dense):
        total[...] = jnp.zeros(total.shape, F32)
    ones = jnp.ones((16, ROWS), BF16)
    for x in range(NX):
        enc_t[x, pl.ds(IN, 16), :] = ones
        h1_t[x, pl.ds(HID, 16), :] = ones
        h2_t[x, pl.ds(HID, 16), :] = ones

    hear_line(1)
    tell_line(2)

    def code_part(x, carry):
        lanes = pl.ds(pl.multiple_of(x * RX, RX), RX)
        bins = bins_ref[:, lanes].astype(F32)
        columns = jnp.transpose((bins + 0.5) / BINS)
        anchor = codes_ref[0, lanes, :].astype(F32)
        heading = codes_ref[1, lanes, :].astype(F32)
        for slot in range(SLOTS):
            enc[x, pl.ds(slot * RX, RX), :] = (
                anchor + columns[:, slot : slot + 1] * heading
            ).astype(BF16)
        following = jnp.concatenate([bins[1:], jnp.full((1, RX), float(BINS), F32)], 0)
        inside = (slot_row >= entry_ref[:, lanes]) & (slot_row < exit_ref[:, lanes])
        span_rows[x] = jnp.where(inside, (following - bins) * unit, 0.0)
        return carry

    lax.fori_loop(0, NX, code_part, 0)
    hear_line(2)
    tell_line(4)

    def turn_code(x, carry):
        enc_t[x, pl.ds(0, IN), :] = jnp.transpose(enc[x])
        return carry

    lax.fori_loop(0, NX, turn_code, 0)
    for kind in range(3):
        wait_weights(kind)
    row = jnp.zeros((1, 1280), F32)
    tail = jnp.zeros((1, 1280 - WIDE), F32)
    for index in range(NR):
        wide = jnp.concatenate([vec_ref[index], tail], 1)
        row = row + (pltpu.roll(wide, PART * index, 1) if index else wide)
    vec_row[...] = row
    dense_wide[...] = jnp.transpose(
        jnp.broadcast_to(row[:, 2 * HID : 3 * HID], (RX, HID))
    ).astype(BF16)

    def hidden_part(index, carry):
        x = along_x(index + 1)
        h1[x] = jnp.maximum(
            jnp.dot(enc[x], w_in[...], preferred_element_type=F32) + vec_row[:, :HID], 0.0
        ).astype(BF16)
        h2[x] = jnp.maximum(
            jnp.dot(h1[x], w_mid[...], preferred_element_type=F32) + vec_row[:, HID : 2 * HID],
            0.0,
        ).astype(BF16)
        dense = jnp.dot(h2[x], dense_wide[...], preferred_element_type=F32)
        grid = jnp.zeros((RX, RX), F32)
        for slot in range(SLOTS):
            grid = jnp.where(lane == slot, dense[slot * RX : (slot + 1) * RX], grid)
        raw_rows[x] = jnp.transpose(grid)[:SLOTS]
        return carry

    lax.fori_loop(0, 2, hidden_part, 0)
    hear_line(4)
    for step in (2, 1, 3):
        pl.semaphore_signal(
            column_sem, inc=1, device_id=at(along_x(step), own_z), device_id_type=MESH
        )
    lax.fori_loop(2, NX, hidden_part, 0)
    raw = raw_rows[...]
    soft = jnp.maximum(raw, 0.0) + jnp.log1p(jnp.exp(-jnp.abs(raw)))
    optical = soft * span_rows[...]
    before, total = sum_before(optical)
    depth_send[...] = total
    pl.semaphore_wait(column_sem, NX - 1)
    spread_all(lambda x, z: depth_send.at[x], depth_all, sem_depth)
    depth_all[place] = depth_send[own_x]
    optical_rows[...] = optical
    before_rows[...] = before
    weight_rows[...] = jnp.exp(-before) * one_less_exp(optical)
    wait_weights(3)

    def colour_part(index, carry):
        x = along_x(index + 1)
        colour[x] = jax.nn.sigmoid(
            jnp.dot(h2[x], w_feat[...], preferred_element_type=F32)
            + vec_row[:, 3 * HID : 3 * HID + FEAT]
        )
        columns = jnp.transpose(weight_rows[x])
        local = jnp.zeros((RX, FEAT), F32)
        for slot in range(SLOTS):
            local = local + columns[:, slot : slot + 1] * colour[x, pl.ds(slot * RX, RX), :]
        partial_send[x] = local.astype(BF16)

        @pl.when(index < NX - 1)
        def _():
            remote(
                partial_send.at[x],
                partial_x.at[own_x],
                sem_partial.at[0],
                sem_partial.at[1],
                at(x, own_z),
            ).start()

        return carry

    lax.fori_loop(0, NX, colour_part, 0)
    partial_x[own_x] = partial_send[own_x]
    wait_all(depth_all, sem_depth)
    below, above = x_sums(*z_sums(depth_all, own_z))
    onward = onward_ref[own_x] == 0
    trans = [jnp.exp(-jnp.where(onward, below[x], above[x])) for x in range(NX)]
    for x in range(NX):
        trans_send[x] = trans[x]
    trans_all[own_x] = trans_send[own_x]
    spread_x(lambda x: trans_send.at[x], trans_all, sem_trans)
    columns = jnp.transpose(jnp.concatenate(trans + trans, 0))
    wait_x(partial_send, partial_x, sem_partial)
    total = jnp.zeros((RX, FEAT), F32)
    for x in range(NX):
        total = total + columns[:, x : x + 1] * partial_x[x].astype(F32)
    pieces[...] = total.reshape(NZ, RZ, FEAT).astype(BF16)
    spread_z(lambda z: pieces.at[z], pieces_z, sem_piece)
    pieces_z[own_z] = pieces[own_z]

    def turn_part(x, carry):
        h1_t[x, pl.ds(0, HID), :] = jnp.transpose(h1[x])
        h2_t[x, pl.ds(0, HID), :] = jnp.transpose(h2[x])
        return carry

    lax.fori_loop(0, NX, turn_part, 0)
    w_mid_t[...] = jnp.transpose(w_mid[...])
    w_feat_t[...] = jnp.transpose(w_feat[...])
    start = pl.multiple_of(own_x * RX + (own_z // 2) * (2 * RZ), 2 * RZ)
    wanted = target_ref[pl.ds(start, 2 * RZ), :].astype(F32)
    odd = lax.rem(own_z, 2).astype(F32)
    wanted = wanted[:RZ] * (1.0 - odd) + wanted[RZ:] * odd
    wait_z(pieces, pieces_z, sem_piece)
    rendered = jnp.sum(pieces_z[...].astype(F32), 0)
    grad_z[own_z] = (rendered - wanted).astype(BF16)
    spread_z(lambda z: grad_z.at[own_z], grad_z, sem_grad_z)
    wait_x(trans_send, trans_all, sem_trans)

    def coef_part(x, carry):
        columns = jnp.transpose(trans_all[x] * weight_rows[x])
        for slot in range(SLOTS):
            rows = pl.ds(slot * RX, RX)
            shade = colour[x, rows, :]
            coef[x, rows, :] = columns[:, slot : slot + 1] * (shade * (1.0 - shade))
        return carry

    lax.fori_loop(0, NX, coef_part, 0)
    wait_z(grad_z, grad_z, sem_grad_z)
    grad_float = grad_z[...].astype(F32).reshape(RX, FEAT)
    grad_all[own_x] = grad_float.astype(BF16)
    for step in (1, 3, 2):
        remote(
            grad_all.at[own_x],
            grad_all.at[own_x],
            sem_grad.at[0, step],
            sem_grad.at[1, step],
            at(along_x(step), own_z),
        ).start()
    grid = jnp.zeros((RX, RX), F32)
    for x in range(NX):
        dots = jnp.sum(grad_float * partial_x[x].astype(F32), -1, keepdims=True)
        grid = jnp.where(lane == x, dots, grid)
    grid = jnp.transpose(grid)
    grads = [grid[x : x + 1] * trans_send[x] for x in range(NX)]
    for x in range(NX):
        over, under = jnp.zeros((1, RX), F32), jnp.zeros((1, RX), F32)
        for other in range(NX):
            if other > x:
                over = over + grads[other]
            if other < x:
                under = under + grads[other]
        level = jnp.where(onward, over, under)
        region_send[3 * x] = level
        region_send[3 * x + 1] = level + jnp.where(onward, grads[x], 0.0)
        region_send[3 * x + 2] = level + jnp.where(onward, 0.0, grads[x])

    def after_row(x, z):
        side = (own_z > z).astype(jnp.int32) + 2 * (own_z < z).astype(jnp.int32)
        return region_send.at[3 * x + side]

    spread_all(after_row, region_all, sem_region)
    region_all[place] = region_send[3 * own_x]

    def feat_part(index, carry):
        late = (index == 2).astype(jnp.int32) - (index == 3).astype(jnp.int32)
        offset = index + late
        x = along_x(offset)

        @pl.when(index > 0)
        def _():
            step = NX - offset
            remote(
                grad_all.at[own_x],
                grad_all.at[x],
                sem_grad.at[0, step],
                sem_grad.at[1, step],
                at(x, own_z),
            ).wait()

        grads = grad_all[x].astype(F32)
        grid = jnp.zeros((RX, RX), F32)
        for slot in range(SLOTS):
            rows = pl.ds(slot * RX, RX)
            shade = colour[x, rows, :]
            grid = jnp.where(lane == slot, jnp.sum(shade * grads, -1, keepdims=True), grid)
            cgrad[rows, :] = (coef[x, rows, :] * grads).astype(BF16)
        sample_rows[x] = jnp.transpose(grid)[:SLOTS]
        g_feat[...] += jnp.dot(h2_t[x], cgrad[...], preferred_element_type=F32)
        hgrad[x] = jnp.dot(cgrad[...], w_feat_t[...], preferred_element_type=F32)
        return carry

    lax.fori_loop(0, NX, feat_part, 0)
    feat_send[...] = g_feat[pl.ds(0, HID), :].astype(BF16).reshape(NR, 32, FEAT)
    spread_rays(0, feat_send, feat_got)
    samples = sample_rows[...]
    later = sum_after(weight_rows[...] * samples)
    local_grad = trans_all[...] * (
        jnp.exp(-(before_rows[...] + optical_rows[...])) * samples - later
    )
    dense_scale = span_rows[...] * jax.nn.sigmoid(raw_rows[...])
    wait_all(region_all, sem_region)
    after = jnp.sum(region_all[...].reshape(NX, NZ, 1, RX), 1)
    after_out[...] = after
    dense_grad = ((local_grad - after) * dense_scale).astype(BF16).astype(F32)
    for x in range(NX):
        dense_columns[x] = jnp.transpose(dense_grad[x])

    def mid_part(x, carry):
        columns = dense_columns[x]
        dense_row = vec_row[:, 2 * HID : 3 * HID]
        dense_added = jnp.zeros((8, HID), F32)
        for slot in range(SLOTS):
            rows = pl.ds(slot * RX, RX)
            hidden = h2[x, rows, :].astype(F32)
            scale = columns[:, slot : slot + 1]
            found = jnp.where(hidden > 0.0, hgrad[x, rows, :] + scale * dense_row, 0.0)
            second[x, rows, :] = found.astype(BF16)
            dense_added = dense_added + to_row_groups(scale * hidden)
        sum_dense[...] += dense_added
        g_mid[...] += jnp.dot(h1_t[x], second[x], preferred_element_type=F32)
        return carry

    lax.fori_loop(0, NX, mid_part, 0)
    mid_send[...] = g_mid[pl.ds(0, HID), :].astype(BF16).reshape(NR, 32, HID)
    spread_rays(1, mid_send, mid_got)

    def in_part(x, carry):
        first[...] = jnp.where(
            h1[x].astype(F32) > 0.0,
            jnp.dot(second[x], w_mid_t[...], preferred_element_type=F32),
            0.0,
        ).astype(BF16)
        g_in[...] += jnp.dot(enc_t[x], first[...], preferred_element_type=F32)
        return carry

    lax.fori_loop(0, NX, in_part, 0)
    in_send[...] = g_in[pl.ds(0, IN), :].astype(BF16).reshape(NR, 16, HID)
    spread_rays(2, in_send, in_got)
    sums = [
        g_in[pl.ds(IN, 8), :][:1],
        g_mid[pl.ds(HID, 8), :][:1],
        jnp.sum(sum_dense[...], 0, keepdims=True),
        g_feat[pl.ds(HID, 8), :][:1],
    ]
    row = jnp.concatenate(sums + [jnp.zeros((1, 128), F32)], 1)
    for index in range(NR):
        turned = pltpu.roll(row, 1280 - PART * index, 1) if index else row
        vec_send[index] = turned[:, :WIDE]
    spread_rays(3, vec_send, vec_got)

    def own_rows(total, count):
        return total[pl.ds(pl.multiple_of(me * count, count), count), :]

    feat_out[...] = gather_rays(0, feat_send, feat_got, own_rows(g_feat, 32))
    mid_out[...] = gather_rays(1, mid_send, mid_got, own_rows(g_mid, 32))
    in_out[...] = gather_rays(2, in_send, in_got, own_rows(g_in, 16))
    vec_out[...] = gather_rays(3, vec_send, vec_got, vec_send[me])


def run_step(*operands):
    def pair(*count):
        return pltpu.SemaphoreType.DMA((2, *count))

    outs = (((16, 256), F32), ((32, 256), F32), ((32, 384), F32), ((1, WIDE), F32))
    outs += (((NX, 1, RX), F32),)
    scratch = (
        ((2, NX * RX, IN), BF16),
        ((SLOTS, NX * RX), jnp.int32),
        ((1, NX * RX), jnp.int32),
        ((1, NX * RX), jnp.int32),
        ((NX, 1, RX), jnp.int32),
        ((NX * RX, FEAT), BF16),
        ((16, HID), F32),
        ((32, HID), F32),
        ((32, FEAT), F32),
        ((1, PART), F32),
        ((IN, HID), BF16),
        ((HID, HID), BF16),
        ((HID, FEAT), BF16),
        ((NR, 1, WIDE), F32),
        ((HID, HID), BF16),
        ((FEAT, HID), BF16),
        ((NX, ROWS, IN), BF16),
        ((NX, ROWS, HID), BF16),
        ((NX, ROWS, HID), BF16),
        ((NX, IN + 16, ROWS), BF16),
        ((NX, HID + 16, ROWS), BF16),
        ((NX, HID + 16, ROWS), BF16),
        ((NX, ROWS, FEAT), F32),
        ((NX, ROWS, FEAT), F32),
        ((ROWS, FEAT), BF16),
        ((NX, ROWS, HID), F32),
        ((NX, ROWS, HID), BF16),
        ((ROWS, HID), BF16),
        ((NX, SLOTS, RX), F32),
        ((NX, SLOTS, RX), F32),
        ((NX, SLOTS, RX), F32),
        ((NX, SLOTS, RX), F32),
        ((NX, SLOTS, RX), F32),
        ((NX, SLOTS, RX), F32),
        ((HID, RX), BF16),
        ((1, 1280), F32),
        ((IN + 16, HID), F32),
        ((HID + 16, HID), F32),
        ((HID + 16, FEAT), F32),
        ((8, HID), F32),
        ((NX, RX, SLOTS), F32),
        ((NX, 1, RX), F32),
        ((NX * NZ, 1, RX), F32),
        ((NX, RX, FEAT), BF16),
        ((NX, RX, FEAT), BF16),
        ((NX, 1, RX), F32),
        ((NX, 1, RX), F32),
        ((NZ, RZ, FEAT), BF16),
        ((NZ, RZ, FEAT), BF16),
        ((NZ, RZ, FEAT), BF16),
        ((NX, RX, FEAT), BF16),
        ((3 * NX, 1, RX), F32),
        ((NX * NZ, 1, RX), F32),
        ((NR, 16, 256), BF16),
        ((NR, 32, 256), BF16),
        ((NR, 32, 384), BF16),
        ((NR, 1, WIDE), F32),
        ((NR, 16, 256), BF16),
        ((NR, 32, 256), BF16),
        ((NR, 32, 384), BF16),
        ((NR, 1, WIDE), F32),
    )
    return pl.pallas_call(
        step_kernel,
        out_shape=tuple(jax.ShapeDtypeStruct(*out) for out in outs),
        in_specs=[pl.BlockSpec(memory_space=pl.ANY)] * len(operands),
        out_specs=tuple(vmem(len(outs))),
        scratch_shapes=[pltpu.VMEM(*part) for part in scratch]
        + [pair(), pair(), pair(), pair(), pair(), pair(NX), pair()]
        + [pair(4), pltpu.SemaphoreType.DMA((10,)), pair(4), pltpu.SemaphoreType.REGULAR]
        + [pltpu.SemaphoreType.REGULAR((3,))],
        compiler_params=pltpu.CompilerParams(
            collective_id=0, has_side_effects=True, vmem_limit_bytes=60 * 2**20
        ),
        name="run_step",
    )(*operands)


def adam_kernel(*refs):
    states, grads, after_ref, outs, depth_out = refs[:4], refs[4:8], refs[8], refs[9:13], refs[13]
    for state, grad, out in zip(states, grads, outs):
        gradient = grad[...].reshape((1,) + grad.shape) if len(state.shape) == 4 else grad[...]
        gradient = gradient[..., : state.shape[-1]]
        first_moment = beta_one * state[1] + (1.0 - beta_one) * gradient
        second = beta_two * state[2] + (1.0 - beta_two) * gradient * gradient
        update_step = first_moment / first_fix / (jnp.sqrt(second / second_fix) + epsilon)
        out[0] = state[0] - learn_rate * update_step
        out[1] = first_moment
        out[2] = second
    depth_out[...] = -after_ref[...]


def adam_all(states, grads, after):
    shapes = [jax.ShapeDtypeStruct(state.shape, F32) for state in states]
    shapes.append(jax.ShapeDtypeStruct(after.shape, F32))
    return pl.pallas_call(
        adam_kernel,
        out_shape=tuple(shapes),
        in_specs=vmem(9),
        out_specs=tuple(vmem(5)),
        name="adam_all",
    )(*states, *grads, after)


def per_device(
    ray_codes,
    target,
    direction,
    entries,
    exits,
    depth_bins,
    in_layer,
    mid_layer,
    feat_layer,
    vectors,
):
    *grads, after = run_step(
        ray_codes,
        depth_bins,
        entries,
        exits,
        direction.reshape(NX, 1, RX),
        target,
        in_layer,
        mid_layer,
        feat_layer,
        vectors,
    )
    *states, depth_grad = adam_all((in_layer, mid_layer, feat_layer, vectors), grads, after)
    return (*states, depth_grad.reshape(1, NX * RX))


def solution(mesh):
    placed = (
        P(None, "rays", None),
        P("rays", None),
        P("rays"),
        P("region", "rays"),
        P("region", "rays"),
        P("region", None, "rays"),
        P(None, "region", "rays", None),
        P(None, "region", "rays", None),
        P(None, "region", "rays", None),
        P(None, "region", "rays"),
    )
    return jax.shard_map(
        per_device,
        mesh=mesh,
        in_specs=placed,
        out_specs=(
            P(None, "region", "rays", None),
            P(None, "region", "rays", None),
            P(None, "region", "rays", None),
            P(None, "region", "rays"),
            P("region", "rays"),
        ),
        check_vma=False,
    )
```

```python
import jax
import jax.numpy as jnp
from jax import lax
from jax.experimental import pallas as pl
from jax.experimental.pallas import tpu as pltpu
from jax.sharding import PartitionSpec as P

BINS = 64


depth_scale = 4.0
beta_one = 0.9
beta_two = 0.999
learn_rate = 0.001
epsilon = 1e-08
first_fix = 1.0 - 0.9**10
second_fix = 1.0 - 0.999**10

MESH = pl.DeviceIdType.MESH
NX = 4
NZ = 16
NR = 8
RX = 128
RZ = 8
IN = 128
HID = 256
FEAT = 384
SLOTS = 8
ROWS = SLOTS * RX
PART = 144
WIDE = 256
F32 = jnp.float32
BF16 = jnp.bfloat16


def vmem(count):
    return [pl.BlockSpec(memory_space=pltpu.VMEM)] * count


def remote(source, target, send_sem, recv_sem, peer):
    return pltpu.make_async_remote_copy(
        src_ref=source,
        dst_ref=target,
        send_sem=send_sem,
        recv_sem=recv_sem,
        device_id=peer,
        device_id_type=MESH,
    )


def far_first(count):
    half = count // 2
    order = [half]
    for gap in range(1, half):
        order += [half - gap, half + gap]
    return order


def z_sums(table, own_z):
    column = [jnp.zeros((1, RX), F32) for _ in range(NX)]
    lower, upper = list(column), list(column)
    for z in range(NZ):
        under, over = (z < own_z).astype(F32), (z > own_z).astype(F32)
        for x in range(NX):
            rows = table[x * NZ + z]
            column[x] = column[x] + rows
            lower[x] = lower[x] + rows * under
            upper[x] = upper[x] + rows * over
    return column, lower, upper


def far_regions():
    hops = [
        (min(x, NX - x) + min(z, NZ - z), x, z) for x in range(NX) for z in range(NZ) if x + z
    ]
    return [(x, z) for _, x, z in sorted(hops, reverse=True)]


def x_sums(column, lower, upper):
    below, above = [], []
    for x in range(NX):
        under, over = lower[x], upper[x]
        for other in range(NX):
            if other < x:
                under = under + column[other]
            if other > x:
                over = over + column[other]
        below.append(under)
        above.append(over)
    return below, above


def one_less_exp(value):
    series = value * (
        1.0 - value / 2.0 * (1.0 - value / 3.0 * (1.0 - value / 4.0 * (1.0 - value / 5.0)))
    )
    return jnp.where(value < 0.0625, series, 1.0 - jnp.exp(-value))


def sum_before(rows):
    running = jnp.zeros((NX, 1, RX), F32)
    found = []
    for slot in range(SLOTS):
        found.append(running)
        running = running + rows[:, slot : slot + 1]
    return jnp.concatenate(found, 1), running


def sum_after(rows):
    running = jnp.zeros((NX, 1, RX), F32)
    found = []
    for slot in range(SLOTS - 1, -1, -1):
        found.append(running)
        running = running + rows[:, slot : slot + 1]
    return jnp.concatenate(found[::-1], 1)


def to_row_groups(values):
    return jnp.sum(values.reshape(values.shape[0] // 8, 8, values.shape[1]), 0)


def step_kernel(
    codes_hbm,
    bins_hbm,
    entry_hbm,
    exit_hbm,
    onward_hbm,
    target_hbm,
    in_layer,
    mid_layer,
    feat_layer,
    vectors,
    in_out,
    mid_out,
    feat_out,
    vec_out,
    after_out,
    codes_ref,
    bins_ref,
    entry_ref,
    exit_ref,
    onward_ref,
    target_ref,
    in_own,
    mid_own,
    feat_own,
    vec_own,
    w_in,
    w_mid,
    w_feat,
    vec_ref,
    w_mid_t,
    w_feat_t,
    enc,
    h1,
    h2,
    enc_t,
    h1_t,
    h2_t,
    colour,
    coef,
    cgrad,
    hgrad,
    second,
    first,
    raw_rows,
    optical_rows,
    before_rows,
    weight_rows,
    span_rows,
    sample_rows,
    dense_wide,
    vec_row,
    g_in,
    g_mid,
    g_feat,
    sum_dense,
    dense_columns,
    depth_send,
    depth_all,
    partial_send,
    partial_x,
    trans_send,
    trans_all,
    pieces,
    pieces_z,
    grad_z,
    grad_all,
    region_send,
    region_all,
    in_send,
    mid_send,
    feat_send,
    vec_send,
    in_got,
    mid_got,
    feat_got,
    vec_got,
    sem_depth,
    sem_partial,
    sem_trans,
    sem_piece,
    sem_grad_z,
    sem_grad,
    sem_region,
    sem_rays,
    sem_load,
    sem_weight,
    column_sem,
    line_sem,
):
    place = lax.axis_index("region")
    me = lax.axis_index("rays")
    own_x, own_z = place // NZ, lax.rem(place, NZ)

    def along_x(step):
        return lax.rem(own_x + step, NX)

    def along_z(step):
        return lax.rem(own_z + step, NZ)

    def at(x, z):
        return {"region": x * NZ + z}

    barrier = pltpu.get_barrier_semaphore()
    for step in (1, NZ - 1):
        pl.semaphore_signal(
            barrier, inc=1, device_id=at(own_x, along_z(step)), device_id_type=MESH
        )
    for step in (2, 1, 3):
        pl.semaphore_signal(
            barrier, inc=1, device_id=at(along_x(step), own_z), device_id_type=MESH
        )
    for step in range(1, NR):
        pl.semaphore_signal(
            barrier, inc=1, device_id={"rays": lax.rem(me + step, NR)}, device_id_type=MESH
        )

    def arrived(sent, got, count, sems, peer):
        first = pl.ds(0, count)
        remote(sent.at[first], got.at[first], sems.at[0], sems.at[1], peer).wait()

    def spread_x(source, target, sems):
        for step in (2, 1, 3):
            x = along_x(step)
            remote(source(x), target.at[own_x], sems.at[0], sems.at[1], at(x, own_z)).start()

    def wait_x(sent, got, sems):
        arrived(sent, got, NX - 1, sems, at(along_x(1), own_z))

    def spread_z(source, target, sems):
        for step in far_first(NZ):
            z = along_z(step)
            remote(source(z), target.at[own_z], sems.at[0], sems.at[1], at(own_x, z)).start()

    def wait_z(sent, got, sems):
        arrived(sent, got, NZ - 1, sems, at(own_x, along_z(1)))

    def spread_all(source, target, sems):
        for far_x, far_z in far_regions():
            x, z = along_x(far_x), along_z(far_z)
            remote(source(x, z), target.at[place], sems.at[0], sems.at[1], at(x, z)).start()

    def wait_all(table, sems):
        arrived(table, table, NX * NZ - 1, sems, at(along_x(1), own_z))

    def spread_rays(kind, source, target):
        for step in range(1, NR):
            peer = lax.rem(me + step, NR)
            remote(
                source.at[peer],
                target.at[me],
                sem_rays.at[0, kind],
                sem_rays.at[1, kind],
                {"rays": peer},
            ).start()
        target[me] = jnp.zeros(target.shape[1:], target.dtype)

    def gather_rays(kind, source, target, total):
        first = pl.ds(0, NR - 1)
        remote(
            source.at[first],
            target.at[first],
            sem_rays.at[0, kind],
            sem_rays.at[1, kind],
            {"rays": lax.rem(me + 1, NR)},
        ).wait()
        return total + jnp.sum(target[...].astype(F32), 0)

    loads = [
        pltpu.make_async_copy(source, target, sem_load.at[index])
        for index, (source, target) in enumerate(
            (
                (in_layer.at[0, 0], in_own),
                (mid_layer.at[0, 0], mid_own),
                (feat_layer.at[0, 0], feat_own),
                (vectors.at[0], vec_own),
                (codes_hbm, codes_ref),
                (bins_hbm.at[0], bins_ref),
                (entry_hbm, entry_ref),
                (exit_hbm, exit_ref),
                (onward_hbm, onward_ref),
                (target_hbm, target_ref),
            )
        )
    ]
    for load in loads:
        load.start()

    def mine(array, count, index):
        return array.at[pl.ds(pl.multiple_of(index * count, count), count)]

    weights = (
        lambda index: mine(w_in, 16, index),
        lambda index: mine(w_mid, 32, index),
        lambda index: vec_ref.at[index],
        lambda index: mine(w_feat, 32, index),
    )

    def spread_weights(kind):
        for step in range(1, NR):
            remote(
                weights[kind](me),
                weights[kind](me),
                sem_weight.at[0, kind],
                sem_weight.at[1, kind],
                {"rays": lax.rem(me + step, NR)},
            ).start()

    def wait_weights(kind):
        array, count = ((w_in, 16), (w_mid, 32), (vec_ref, 1), (w_feat, 32))[kind]
        first = array.at[pl.ds(0, count * (NR - 1))]
        remote(
            first,
            first,
            sem_weight.at[0, kind],
            sem_weight.at[1, kind],
            {"rays": lax.rem(me + 1, NR)},
        ).wait()

    unit = depth_scale / (NX * NZ * BINS)
    lane = lax.broadcasted_iota(jnp.int32, (RX, RX), 1)
    slot_row = lax.broadcasted_iota(jnp.int32, (SLOTS, RX), 0)
    for load in loads[:4]:
        load.wait()
    weights[0](me)[...] = in_own[...].astype(BF16)
    weights[1](me)[...] = mid_own[...].astype(BF16)
    weights[3](me)[...] = feat_own[...].astype(BF16)
    vec_ref[me] = jnp.zeros((1, WIDE), F32)
    vec_ref[me, :, pl.ds(0, PART)] = vec_own[...].astype(BF16).astype(F32)
    pl.semaphore_wait(barrier, NX + NR)
    for kind in range(4):
        spread_weights(kind)

    def tell_line(reach):
        for step in (reach, NZ - reach):
            pl.semaphore_signal(
                line_sem.at[reach.bit_length() - 1],
                inc=1,
                device_id=at(own_x, along_z(step)),
                device_id_type=MESH,
            )

    def hear_line(reach):
        pl.semaphore_wait(line_sem.at[reach.bit_length() - 1], 2)

    tell_line(1)
    for load in loads[4:]:
        load.wait()
    for total in (g_in, g_mid, g_feat, sum_dense):
        total[...] = jnp.zeros(total.shape, F32)
    ones = jnp.ones((16, ROWS), BF16)
    for x in range(NX):
        enc_t[x, pl.ds(IN, 16), :] = ones
        h1_t[x, pl.ds(HID, 16), :] = ones
        h2_t[x, pl.ds(HID, 16), :] = ones

    hear_line(1)
    tell_line(2)

    def code_part(x, carry):
        lanes = pl.ds(pl.multiple_of(x * RX, RX), RX)
        bins = bins_ref[:, lanes].astype(F32)
        columns = jnp.transpose((bins + 0.5) / BINS)
        anchor = codes_ref[0, lanes, :].astype(F32)
        heading = codes_ref[1, lanes, :].astype(F32)
        for slot in range(SLOTS):
            enc[x, pl.ds(slot * RX, RX), :] = (
                anchor + columns[:, slot : slot + 1] * heading
            ).astype(BF16)
        following = jnp.concatenate([bins[1:], jnp.full((1, RX), float(BINS), F32)], 0)
        inside = (slot_row >= entry_ref[:, lanes]) & (slot_row < exit_ref[:, lanes])
        span_rows[x] = jnp.where(inside, (following - bins) * unit, 0.0)
        return carry

    lax.fori_loop(0, NX, code_part, 0)
    hear_line(2)
    tell_line(4)

    def turn_code(x, carry):
        enc_t[x, pl.ds(0, IN), :] = jnp.transpose(enc[x])
        return carry

    lax.fori_loop(0, NX, turn_code, 0)
    for kind in range(3):
        wait_weights(kind)
    row = jnp.zeros((1, 1280), F32)
    tail = jnp.zeros((1, 1280 - WIDE), F32)
    for index in range(NR):
        wide = jnp.concatenate([vec_ref[index], tail], 1)
        row = row + (pltpu.roll(wide, PART * index, 1) if index else wide)
    vec_row[...] = row
    dense_wide[...] = jnp.transpose(
        jnp.broadcast_to(row[:, 2 * HID : 3 * HID], (RX, HID))
    ).astype(BF16)

    def hidden_part(index, carry):
        x = along_x(index + 1)
        h1[x] = jnp.maximum(
            jnp.dot(enc[x], w_in[...], preferred_element_type=F32) + vec_row[:, :HID], 0.0
        ).astype(BF16)
        h2[x] = jnp.maximum(
            jnp.dot(h1[x], w_mid[...], preferred_element_type=F32) + vec_row[:, HID : 2 * HID],
            0.0,
        ).astype(BF16)
        dense = jnp.dot(h2[x], dense_wide[...], preferred_element_type=F32)
        grid = jnp.zeros((RX, RX), F32)
        for slot in range(SLOTS):
            grid = jnp.where(lane == slot, dense[slot * RX : (slot + 1) * RX], grid)
        raw_rows[x] = jnp.transpose(grid)[:SLOTS]
        return carry

    lax.fori_loop(0, 2, hidden_part, 0)
    hear_line(4)
    for step in (2, 1, 3):
        pl.semaphore_signal(
            column_sem, inc=1, device_id=at(along_x(step), own_z), device_id_type=MESH
        )
    lax.fori_loop(2, NX, hidden_part, 0)
    raw = raw_rows[...]
    soft = jnp.maximum(raw, 0.0) + jnp.log1p(jnp.exp(-jnp.abs(raw)))
    optical = soft * span_rows[...]
    before, total = sum_before(optical)
    depth_send[...] = total
    pl.semaphore_wait(column_sem, NX - 1)
    spread_all(lambda x, z: depth_send.at[x], depth_all, sem_depth)
    depth_all[place] = depth_send[own_x]
    optical_rows[...] = optical
    before_rows[...] = before
    weight_rows[...] = jnp.exp(-before) * one_less_exp(optical)
    wait_weights(3)

    def colour_part(index, carry):
        x = along_x(index + 1)
        colour[x] = jax.nn.sigmoid(
            jnp.dot(h2[x], w_feat[...], preferred_element_type=F32)
            + vec_row[:, 3 * HID : 3 * HID + FEAT]
        )
        columns = jnp.transpose(weight_rows[x])
        local = jnp.zeros((RX, FEAT), F32)
        for slot in range(SLOTS):
            local = local + columns[:, slot : slot + 1] * colour[x, pl.ds(slot * RX, RX), :]
        partial_send[x] = local.astype(BF16)

        @pl.when(index < NX - 1)
        def _():
            remote(
                partial_send.at[x],
                partial_x.at[own_x],
                sem_partial.at[0],
                sem_partial.at[1],
                at(x, own_z),
            ).start()

        return carry

    lax.fori_loop(0, NX, colour_part, 0)
    partial_x[own_x] = partial_send[own_x]
    wait_all(depth_all, sem_depth)
    below, above = x_sums(*z_sums(depth_all, own_z))
    onward = onward_ref[own_x] == 0
    trans = [jnp.exp(-jnp.where(onward, below[x], above[x])) for x in range(NX)]
    for x in range(NX):
        trans_send[x] = trans[x]
    trans_all[own_x] = trans_send[own_x]
    spread_x(lambda x: trans_send.at[x], trans_all, sem_trans)
    columns = jnp.transpose(jnp.concatenate(trans + trans, 0))
    wait_x(partial_send, partial_x, sem_partial)
    total = jnp.zeros((RX, FEAT), F32)
    for x in range(NX):
        total = total + columns[:, x : x + 1] * partial_x[x].astype(F32)
    pieces[...] = total.reshape(NZ, RZ, FEAT).astype(BF16)
    spread_z(lambda z: pieces.at[z], pieces_z, sem_piece)
    pieces_z[own_z] = pieces[own_z]

    def turn_part(x, carry):
        h1_t[x, pl.ds(0, HID), :] = jnp.transpose(h1[x])
        h2_t[x, pl.ds(0, HID), :] = jnp.transpose(h2[x])
        return carry

    lax.fori_loop(0, NX, turn_part, 0)
    w_mid_t[...] = jnp.transpose(w_mid[...])
    w_feat_t[...] = jnp.transpose(w_feat[...])
    start = pl.multiple_of(own_x * RX + (own_z // 2) * (2 * RZ), 2 * RZ)
    wanted = target_ref[pl.ds(start, 2 * RZ), :].astype(F32)
    odd = lax.rem(own_z, 2).astype(F32)
    wanted = wanted[:RZ] * (1.0 - odd) + wanted[RZ:] * odd
    wait_z(pieces, pieces_z, sem_piece)
    rendered = jnp.sum(pieces_z[...].astype(F32), 0)
    grad_z[own_z] = (rendered - wanted).astype(BF16)
    spread_z(lambda z: grad_z.at[own_z], grad_z, sem_grad_z)
    wait_x(trans_send, trans_all, sem_trans)

    def coef_part(x, carry):
        columns = jnp.transpose(trans_all[x] * weight_rows[x])
        for slot in range(SLOTS):
            rows = pl.ds(slot * RX, RX)
            shade = colour[x, rows, :]
            coef[x, rows, :] = columns[:, slot : slot + 1] * (shade * (1.0 - shade))
        return carry

    lax.fori_loop(0, NX, coef_part, 0)
    wait_z(grad_z, grad_z, sem_grad_z)
    grad_float = grad_z[...].astype(F32).reshape(RX, FEAT)
    grad_all[own_x] = grad_float.astype(BF16)
    for step in (2, 1, 3):
        remote(
            grad_all.at[own_x],
            grad_all.at[own_x],
            sem_grad.at[0, step],
            sem_grad.at[1, step],
            at(along_x(step), own_z),
        ).start()
    grid = jnp.zeros((RX, RX), F32)
    for x in range(NX):
        dots = jnp.sum(grad_float * partial_x[x].astype(F32), -1, keepdims=True)
        grid = jnp.where(lane == x, dots, grid)
    grid = jnp.transpose(grid)
    grads = [grid[x : x + 1] * trans_send[x] for x in range(NX)]
    for x in range(NX):
        over, under = jnp.zeros((1, RX), F32), jnp.zeros((1, RX), F32)
        for other in range(NX):
            if other > x:
                over = over + grads[other]
            if other < x:
                under = under + grads[other]
        level = jnp.where(onward, over, under)
        region_send[3 * x] = level
        region_send[3 * x + 1] = level + jnp.where(onward, grads[x], 0.0)
        region_send[3 * x + 2] = level + jnp.where(onward, 0.0, grads[x])

    def after_row(x, z):
        side = (own_z > z).astype(jnp.int32) + 2 * (own_z < z).astype(jnp.int32)
        return region_send.at[3 * x + side]

    spread_all(after_row, region_all, sem_region)
    region_all[place] = region_send[3 * own_x]

    def feat_part(index, carry):
        late = (index == 2).astype(jnp.int32) - (index == 3).astype(jnp.int32)
        offset = index + late
        x = along_x(offset)

        @pl.when(index > 0)
        def _():
            step = NX - offset
            remote(
                grad_all.at[own_x],
                grad_all.at[x],
                sem_grad.at[0, step],
                sem_grad.at[1, step],
                at(x, own_z),
            ).wait()

        grads = grad_all[x].astype(F32)
        grid = jnp.zeros((RX, RX), F32)
        for slot in range(SLOTS):
            rows = pl.ds(slot * RX, RX)
            shade = colour[x, rows, :]
            grid = jnp.where(lane == slot, jnp.sum(shade * grads, -1, keepdims=True), grid)
            cgrad[rows, :] = (coef[x, rows, :] * grads).astype(BF16)
        sample_rows[x] = jnp.transpose(grid)[:SLOTS]
        g_feat[...] += jnp.dot(h2_t[x], cgrad[...], preferred_element_type=F32)
        hgrad[x] = jnp.dot(cgrad[...], w_feat_t[...], preferred_element_type=F32)
        return carry

    lax.fori_loop(0, NX, feat_part, 0)
    feat_send[...] = g_feat[pl.ds(0, HID), :].astype(BF16).reshape(NR, 32, FEAT)
    spread_rays(0, feat_send, feat_got)
    samples = sample_rows[...]
    later = sum_after(weight_rows[...] * samples)
    local_grad = trans_all[...] * (
        jnp.exp(-(before_rows[...] + optical_rows[...])) * samples - later
    )
    dense_scale = span_rows[...] * jax.nn.sigmoid(raw_rows[...])
    wait_all(region_all, sem_region)
    after = jnp.sum(region_all[...].reshape(NX, NZ, 1, RX), 1)
    after_out[...] = after
    dense_grad = ((local_grad - after) * dense_scale).astype(BF16).astype(F32)
    for x in range(NX):
        dense_columns[x] = jnp.transpose(dense_grad[x])

    def mid_part(x, carry):
        columns = dense_columns[x]
        dense_row = vec_row[:, 2 * HID : 3 * HID]
        dense_added = jnp.zeros((8, HID), F32)
        for slot in range(SLOTS):
            rows = pl.ds(slot * RX, RX)
            hidden = h2[x, rows, :].astype(F32)
            scale = columns[:, slot : slot + 1]
            found = jnp.where(hidden > 0.0, hgrad[x, rows, :] + scale * dense_row, 0.0)
            second[x, rows, :] = found.astype(BF16)
            dense_added = dense_added + to_row_groups(scale * hidden)
        sum_dense[...] += dense_added
        g_mid[...] += jnp.dot(h1_t[x], second[x], preferred_element_type=F32)
        return carry

    lax.fori_loop(0, NX, mid_part, 0)
    mid_send[...] = g_mid[pl.ds(0, HID), :].astype(BF16).reshape(NR, 32, HID)
    spread_rays(1, mid_send, mid_got)

    def in_part(x, carry):
        first[...] = jnp.where(
            h1[x].astype(F32) > 0.0,
            jnp.dot(second[x], w_mid_t[...], preferred_element_type=F32),
            0.0,
        ).astype(BF16)
        g_in[...] += jnp.dot(enc_t[x], first[...], preferred_element_type=F32)
        return carry

    lax.fori_loop(0, NX, in_part, 0)
    in_send[...] = g_in[pl.ds(0, IN), :].astype(BF16).reshape(NR, 16, HID)
    spread_rays(2, in_send, in_got)
    sums = [
        g_in[pl.ds(IN, 8), :][:1],
        g_mid[pl.ds(HID, 8), :][:1],
        jnp.sum(sum_dense[...], 0, keepdims=True),
        g_feat[pl.ds(HID, 8), :][:1],
    ]
    row = jnp.concatenate(sums + [jnp.zeros((1, 128), F32)], 1)
    for index in range(NR):
        turned = pltpu.roll(row, 1280 - PART * index, 1) if index else row
        vec_send[index] = turned[:, :WIDE]
    spread_rays(3, vec_send, vec_got)

    def own_rows(total, count):
        return total[pl.ds(pl.multiple_of(me * count, count), count), :]

    feat_out[...] = gather_rays(0, feat_send, feat_got, own_rows(g_feat, 32))
    mid_out[...] = gather_rays(1, mid_send, mid_got, own_rows(g_mid, 32))
    in_out[...] = gather_rays(2, in_send, in_got, own_rows(g_in, 16))
    vec_out[...] = gather_rays(3, vec_send, vec_got, vec_send[me])


def run_step(*operands):
    def pair(*count):
        return pltpu.SemaphoreType.DMA((2, *count))

    outs = (((16, 256), F32), ((32, 256), F32), ((32, 384), F32), ((1, WIDE), F32))
    outs += (((NX, 1, RX), F32),)
    scratch = (
        ((2, NX * RX, IN), BF16),
        ((SLOTS, NX * RX), jnp.int32),
        ((1, NX * RX), jnp.int32),
        ((1, NX * RX), jnp.int32),
        ((NX, 1, RX), jnp.int32),
        ((NX * RX, FEAT), BF16),
        ((16, HID), F32),
        ((32, HID), F32),
        ((32, FEAT), F32),
        ((1, PART), F32),
        ((IN, HID), BF16),
        ((HID, HID), BF16),
        ((HID, FEAT), BF16),
        ((NR, 1, WIDE), F32),
        ((HID, HID), BF16),
        ((FEAT, HID), BF16),
        ((NX, ROWS, IN), BF16),
        ((NX, ROWS, HID), BF16),
        ((NX, ROWS, HID), BF16),
        ((NX, IN + 16, ROWS), BF16),
        ((NX, HID + 16, ROWS), BF16),
        ((NX, HID + 16, ROWS), BF16),
        ((NX, ROWS, FEAT), F32),
        ((NX, ROWS, FEAT), F32),
        ((ROWS, FEAT), BF16),
        ((NX, ROWS, HID), F32),
        ((NX, ROWS, HID), BF16),
        ((ROWS, HID), BF16),
        ((NX, SLOTS, RX), F32),
        ((NX, SLOTS, RX), F32),
        ((NX, SLOTS, RX), F32),
        ((NX, SLOTS, RX), F32),
        ((NX, SLOTS, RX), F32),
        ((NX, SLOTS, RX), F32),
        ((HID, RX), BF16),
        ((1, 1280), F32),
        ((IN + 16, HID), F32),
        ((HID + 16, HID), F32),
        ((HID + 16, FEAT), F32),
        ((8, HID), F32),
        ((NX, RX, SLOTS), F32),
        ((NX, 1, RX), F32),
        ((NX * NZ, 1, RX), F32),
        ((NX, RX, FEAT), BF16),
        ((NX, RX, FEAT), BF16),
        ((NX, 1, RX), F32),
        ((NX, 1, RX), F32),
        ((NZ, RZ, FEAT), BF16),
        ((NZ, RZ, FEAT), BF16),
        ((NZ, RZ, FEAT), BF16),
        ((NX, RX, FEAT), BF16),
        ((3 * NX, 1, RX), F32),
        ((NX * NZ, 1, RX), F32),
        ((NR, 16, 256), BF16),
        ((NR, 32, 256), BF16),
        ((NR, 32, 384), BF16),
        ((NR, 1, WIDE), F32),
        ((NR, 16, 256), BF16),
        ((NR, 32, 256), BF16),
        ((NR, 32, 384), BF16),
        ((NR, 1, WIDE), F32),
    )
    return pl.pallas_call(
        step_kernel,
        out_shape=tuple(jax.ShapeDtypeStruct(*out) for out in outs),
        in_specs=[pl.BlockSpec(memory_space=pl.ANY)] * len(operands),
        out_specs=tuple(vmem(len(outs))),
        scratch_shapes=[pltpu.VMEM(*part) for part in scratch]
        + [pair(), pair(), pair(), pair(), pair(), pair(NX), pair()]
        + [pair(4), pltpu.SemaphoreType.DMA((10,)), pair(4), pltpu.SemaphoreType.REGULAR]
        + [pltpu.SemaphoreType.REGULAR((3,))],
        compiler_params=pltpu.CompilerParams(
            collective_id=0, has_side_effects=True, vmem_limit_bytes=60 * 2**20
        ),
        name="run_step",
    )(*operands)


def adam_kernel(*refs):
    states, grads, after_ref, outs, depth_out = refs[:4], refs[4:8], refs[8], refs[9:13], refs[13]
    for state, grad, out in zip(states, grads, outs):
        gradient = grad[...].reshape((1,) + grad.shape) if len(state.shape) == 4 else grad[...]
        gradient = gradient[..., : state.shape[-1]]
        first_moment = beta_one * state[1] + (1.0 - beta_one) * gradient
        second = beta_two * state[2] + (1.0 - beta_two) * gradient * gradient
        update_step = first_moment / first_fix / (jnp.sqrt(second / second_fix) + epsilon)
        out[0] = state[0] - learn_rate * update_step
        out[1] = first_moment
        out[2] = second
    depth_out[...] = -after_ref[...]


def adam_all(states, grads, after):
    shapes = [jax.ShapeDtypeStruct(state.shape, F32) for state in states]
    shapes.append(jax.ShapeDtypeStruct(after.shape, F32))
    return pl.pallas_call(
        adam_kernel,
        out_shape=tuple(shapes),
        in_specs=vmem(9),
        out_specs=tuple(vmem(5)),
        name="adam_all",
    )(*states, *grads, after)


def per_device(
    ray_codes,
    target,
    direction,
    entries,
    exits,
    depth_bins,
    in_layer,
    mid_layer,
    feat_layer,
    vectors,
):
    *grads, after = run_step(
        ray_codes,
        depth_bins,
        entries,
        exits,
        direction.reshape(NX, 1, RX),
        target,
        in_layer,
        mid_layer,
        feat_layer,
        vectors,
    )
    *states, depth_grad = adam_all((in_layer, mid_layer, feat_layer, vectors), grads, after)
    return (*states, depth_grad.reshape(1, NX * RX))


def solution(mesh):
    placed = (
        P(None, "rays", None),
        P("rays", None),
        P("rays"),
        P("region", "rays"),
        P("region", "rays"),
        P("region", None, "rays"),
        P(None, "region", "rays", None),
        P(None, "region", "rays", None),
        P(None, "region", "rays", None),
        P(None, "region", "rays"),
    )
    return jax.shard_map(
        per_device,
        mesh=mesh,
        in_specs=placed,
        out_specs=(
            P(None, "region", "rays", None),
            P(None, "region", "rays", None),
            P(None, "region", "rays", None),
            P(None, "region", "rays"),
            P("region", "rays"),
        ),
        check_vma=False,
    )
```
